32 devices in a mesh: dp: 8 (over z, y), mp: 4 (over x, core).
Axes of the slice: x: 2, y: 2, z: 4, core: 2. Of those that a mesh axis runs over, the one named last changes fastest.
Arguments:
- tokens: bfloat16 [8192, 256], P('dp'), may hold values from -6 to 6
- cotangent: bfloat16 [8192, 256], P('dp'), may hold values from -6 to 6
- lengths: int32 [8], P('dp'), may hold values from 257 to 1024, as said below
- projector: float32 [3, 256, 256], P(None, 'dp', 'mp'), may hold values from -0.375 to 0.375
- projector_mean: float32 [3, 256, 256], P(None, 'dp', 'mp')
- projector_square: float32 [3, 256, 256], P(None, 'dp', 'mp')
- combiner: float32 [256, 256], P('mp', 'dp'), may hold values from -4 to 4
- combiner_mean: float32 [256, 256], P('mp', 'dp')
- combiner_square: float32 [256, 256], P('mp', 'dp')
- expander: float32 [256, 2048], P('dp', 'mp'), may hold values from -0.375 to 0.375
- expander_mean: float32 [256, 2048], P('dp', 'mp')
- expander_square: float32 [256, 2048], P('dp', 'mp')
- reducer: float32 [2048, 256], P('mp', 'dp'), may hold values from -0.125 to 0.125
- reducer_mean: float32 [2048, 256], P('mp', 'dp')
- reducer_square: float32 [2048, 256], P('mp', 'dp')
- affines: float32 [4, 256], P(None, 'dp')
- affines_mean: float32 [4, 256], P(None, 'dp')
- affines_square: float32 [4, 256], P(None, 'dp')
Outputs:
- layer_out: bfloat16 [8192, 256], P('dp')
- input_grad: float32 [8192, 256], P('dp')
- projector_next: float32 [3, 256, 256], P(None, 'dp', 'mp')
- mean_projector: float32 [3, 256, 256], P(None, 'dp', 'mp')
- square_projector: float32 [3, 256, 256], P(None, 'dp', 'mp')
- combiner_next: float32 [256, 256], P('mp', 'dp')
- mean_combiner: float32 [256, 256], P('mp', 'dp')
- square_combiner: float32 [256, 256], P('mp', 'dp')
- expander_next: float32 [256, 2048], P('dp', 'mp')
- mean_expander: float32 [256, 2048], P('dp', 'mp')
- square_expander: float32 [256, 2048], P('dp', 'mp')
- reducer_next: float32 [2048, 256], P('mp', 'dp')
- mean_reducer: float32 [2048, 256], P('mp', 'dp')
- square_reducer: float32 [2048, 256], P('mp', 'dp')
- affines_next: float32 [4, 256], P(None, 'dp')
- mean_affines: float32 [4, 256], P(None, 'dp')
- square_affines: float32 [4, 256], P(None, 'dp')
- projector_copy: bfloat16 [3, 256, 256], P(None, None, 'mp')
- combiner_copy: bfloat16 [256, 256], P('mp')
- expander_copy: bfloat16 [256, 2048], P(None, 'mp')
- reducer_copy: bfloat16 [2048, 256], P('mp')
The draws below stay inside these ranges and needn't reach their ends.
Inputs may be any that keep to these rules, and one draw needn't show every extreme that they name: `lengths`: each image has at least 257 tokens; in every draw some image has exactly 1024.
All inputs are finite; a program needn't handle non-finite values.
Results may differ from the reference program's by a relative error of at most 0.018.
Values may be sent and summed in bfloat16 or wider, within the bound.
No kernel may reach another device: no remote copies, remote signals or barrier semaphores. Data moves between devices by JAX's collectives and lax.ppermute only.
A program may use at most 64 MiB of HBM per device.

```python
import math
import jax
import jax.numpy as jnp
from jax import lax

D = 256
HEADS = 8
FF = 2048
HD = 32
SEQ = 1024
WROW = 32
STEP = 5
CFAN = 2
IMAGES = 8
TOKENS = 8192


def spread_of(factor):
    return factor * (0.6 * TOKENS) ** 0.5


def mean_state(key, shape, factor, salt):
    return spread_of(factor) * jax.random.normal(jax.random.fold_in(key, salt), shape, jnp.float32)


def square_state(key, shape, factor, salt):
    spread = spread_of(factor)
    factors = jnp.exp(jax.random.uniform(jax.random.fold_in(key, salt), shape, jnp.float32, 0.0, math.log(4.0)))
    return spread * spread * factors


def draw_lengths(key, part):
    base = jax.random.randint(jax.random.fold_in(key, 3), (IMAGES,), SEQ // 4 + 1, SEQ + 1)
    chosen = jax.random.randint(jax.random.fold_in(key, 7), (), 0, IMAGES)
    return jnp.where(jnp.arange(IMAGES) == chosen, SEQ, base).astype(jnp.int32)


def draw_projector_mean(key, part):
    return mean_state(key, (3, D, D), 1.0, 11)


def draw_projector_square(key, part):
    return square_state(key, (3, D, D), 1.0, 12)


def draw_combiner_mean(key, part):
    return mean_state(key, (D, D), 0.07, 21)


def draw_combiner_square(key, part):
    return square_state(key, (D, D), 0.07, 22)


def draw_expander_mean(key, part):
    return mean_state(key, (D, FF), 0.35, 31)


def draw_expander_square(key, part):
    return square_state(key, (D, FF), 0.35, 32)


def draw_reducer_mean(key, part):
    return mean_state(key, (FF, D), 0.4, 41)


def draw_reducer_square(key, part):
    return square_state(key, (FF, D), 0.4, 42)


def draw_affines(key, part):
    gains = 1.0 + jax.random.uniform(jax.random.fold_in(key, 51), (2, D), jnp.float32, -0.3, 0.3)
    offsets = 0.2 * jax.random.normal(jax.random.fold_in(key, 52), (2, D), jnp.float32)
    return jnp.stack([gains[0], offsets[0], gains[1], offsets[1]])


def draw_affines_mean(key, part):
    return mean_state(key, (4, D), 1.0, 61)


def draw_affines_square(key, part):
    return square_state(key, (4, D), 1.0, 62)


def levels(key, shape, split, least, top_value):
    def one(dim, shards_of):
        steps = jax.random.uniform(jax.random.fold_in(jax.random.fold_in(key, 6), dim), (shards_of,), jnp.float32, least / len(split), top_value / len(split))
        return jnp.repeat(jnp.exp(steps), shape[dim] // shards_of).reshape((-1,) + (1,) * (len(shape) - dim - 1))

    gain = one(*split[0])
    for cut in split[1:]:
        gain = gain * one(*cut)
    return gain


def gaussian(stream_key, extent, scale, limit, cuts=(), kind=jnp.bfloat16):
    result = jax.random.normal(stream_key, extent, jnp.float32) * scale
    if len(cuts) > 0:
        result = levels(stream_key, extent, cuts, -0.22, 0.18) * result
    return jnp.clip(result, min=-limit, max=limit).astype(kind)


def setup_inputs(seed: int = 0) -> dict:
    keys = jax.random.split(jax.random.key(seed), 19)
    tokens = gaussian(keys[0], (TOKENS, D), 1.0, 6.0, ((0, 8),))
    cotangent = gaussian(keys[1], (TOKENS, D), 1.0, 6.0, ((0, 8),))
    lengths = draw_lengths(jax.random.fold_in(keys[18], 71), 0)
    projector = gaussian(keys[3], (3, D, D), D ** -0.5, 0.375, ((1, 8), (2, 4)), jnp.float32)
    projector_mean = draw_projector_mean(jax.random.fold_in(keys[18], 71), 0)
    projector_square = draw_projector_square(jax.random.fold_in(keys[18], 71), 0)
    combiner = gaussian(keys[6], (D, D), CFAN ** -0.5, 4.0, ((0, 4), (1, 8)), jnp.float32)
    combiner_mean = draw_combiner_mean(jax.random.fold_in(keys[18], 71), 0)
    combiner_square = draw_combiner_square(jax.random.fold_in(keys[18], 71), 0)
    expander = gaussian(keys[9], (D, FF), D ** -0.5, 0.375, ((0, 8), (1, 4)), jnp.float32)
    expander_mean = draw_expander_mean(jax.random.fold_in(keys[18], 71), 0)
    expander_square = draw_expander_square(jax.random.fold_in(keys[18], 71), 0)
    reducer = gaussian(keys[12], (FF, D), FF ** -0.5, 0.125, ((0, 4), (1, 8)), jnp.float32)
    reducer_mean = draw_reducer_mean(jax.random.fold_in(keys[18], 71), 0)
    reducer_square = draw_reducer_square(jax.random.fold_in(keys[18], 71), 0)
    affines = draw_affines(jax.random.fold_in(keys[18], 71), 0)
    affines_mean = draw_affines_mean(jax.random.fold_in(keys[18], 71), 0)
    affines_square = draw_affines_square(jax.random.fold_in(keys[18], 71), 0)
    return {"tokens": tokens, "cotangent": cotangent, "lengths": lengths, "projector": projector, "projector_mean": projector_mean, "projector_square": projector_square, "combiner": combiner, "combiner_mean": combiner_mean, "combiner_square": combiner_square, "expander": expander, "expander_mean": expander_mean, "expander_square": expander_square, "reducer": reducer, "reducer_mean": reducer_mean, "reducer_square": reducer_square, "affines": affines, "affines_mean": affines_mean, "affines_square": affines_square}


highest = lax.Precision.HIGHEST

@jax.custom_vjp
def low(v):
    return lax.optimization_barrier(v.astype(jnp.bfloat16)).astype(jnp.float32)

@jax.custom_vjp
def low_back(v):
    return v

def low_keep(v):
    return (low(v), None)

def low_pass(kept, grad):
    return (grad,)

def back_keep(v):
    return (v, None)

def back_low(kept, grad):
    return (low(grad),)
low.defvjp(low_keep, low_pass)
low_back.defvjp(back_keep, back_low)

def round_both(value):
    return low_back(low(value))

def matmul_high(left, right):
    return jnp.dot(left, right, precision=highest, preferred_element_type=jnp.float32)

def sine_table(length, width):
    place = jnp.arange(length)
    row_place = (place // WROW + 1).astype(jnp.float32)
    col_place = (place % WROW + 1).astype(jnp.float32)
    half_width = width // 2
    channel = jnp.arange(half_width)
    exponent = (2 * (channel // 2)).astype(jnp.float32) / half_width
    frequency = jnp.exp(-math.log(10000.0) * exponent)

    def encode(coordinate):
        angles = coordinate[:, None] * frequency[None, :]
        return jnp.where(channel[None, :] % 2 == 0, jnp.sin(angles), jnp.cos(angles))
    return jnp.concatenate([encode(row_place), encode(col_place)], axis=1)

def layer_norm(features, gains, offsets):
    average = lax.optimization_barrier(jnp.mean(features, axis=-1, keepdims=True))
    centred = features - average
    variance = lax.optimization_barrier(jnp.mean(centred * centred, axis=-1, keepdims=True))
    return centred * lax.rsqrt(variance + 1e-05) * gains + offsets

def attend_image(operands):
    queries, key_rows, values, length = operands
    key_live = jnp.arange(queries.shape[0]) < length
    scores = jnp.einsum('qhd,khd->hqk', queries, key_rows, precision=highest) * HD ** (-0.5)
    scores = low_back(scores)
    scores = jnp.where(key_live[None, None, :], scores, -1e+30)
    weights = low(jax.nn.softmax(scores, axis=-1))
    context = jnp.einsum('hqk,khd->qhd', weights, values, precision=highest)
    return round_both(context)

def forward(tokens, projector, combiner, expander, reducer, affines, lengths):
    images = lengths.shape[0]
    positions = jnp.tile(sine_table(SEQ, D), (images, 1))
    query_in = low(tokens + positions)
    proj_low = low(projector)
    queries = round_both(matmul_high(query_in, proj_low[0]))
    key_rows = round_both(matmul_high(query_in, proj_low[1]))
    values = round_both(matmul_high(tokens, proj_low[2]))

    def per_image(matrix):
        return matrix.reshape(images, SEQ, HEADS, HD)
    context = lax.map(jax.checkpoint(attend_image), (per_image(queries), per_image(key_rows), per_image(values), lengths))
    context = context.reshape(tokens.shape[0], D)
    attention = low_back(matmul_high(context, low(combiner)))
    first = layer_norm(tokens + attention, affines[0], affines[1])
    pre_act = low_back(matmul_high(low(first), low(expander)))
    hidden = low(jax.nn.gelu(pre_act, approximate=True))
    feed = low_back(matmul_high(hidden, low(reducer)))
    return layer_norm(first + feed, affines[2], affines[3])

def adamw(weight, moment_one, moment_two, grad, step_rate, decay_rate):
    mean_next = 0.5 * moment_one + 0.5 * grad
    square_next = 0.5 * moment_two + 0.5 * grad * grad
    correct = 1.0 - 0.5 ** STEP
    direction = mean_next / correct / (jnp.sqrt(square_next / correct) + 1e-08)
    weight_next = weight - step_rate * (direction + decay_rate * weight)
    return (weight_next, mean_next, square_next)

def reference(tokens, cotangent, lengths, projector, projector_mean, projector_square, combiner, combiner_mean, combiner_square, expander, expander_mean, expander_square, reducer, reducer_mean, reducer_square, affines, affines_mean, affines_square):
    images = lengths.shape[0]
    tokens_full = tokens.astype(jnp.float32)
    live = (jnp.arange(SEQ)[None, :] < lengths[:, None]).reshape(images * SEQ)
    seed_grad = cotangent.astype(jnp.float32) * live[:, None].astype(jnp.float32)

    def run(tokens_arg, proj_arg, comb_arg, expand_arg, reduce_arg, affine_arg):
        return forward(tokens_arg, proj_arg, comb_arg, expand_arg, reduce_arg, affine_arg, lengths)
    output, pullback = jax.vjp(run, tokens_full, projector, combiner, expander, reducer, affines)
    grads = pullback(seed_grad)
    proj_new = adamw(projector, projector_mean, projector_square, grads[1], D ** (-0.5), 0.0001)
    comb_new = adamw(combiner, combiner_mean, combiner_square, grads[2], CFAN ** (-0.5), 0.0001)
    expand_new = adamw(expander, expander_mean, expander_square, grads[3], D ** (-0.5), 0.0001)
    reduce_new = adamw(reducer, reducer_mean, reducer_square, grads[4], FF ** (-0.5), 0.0001)
    affine_new = adamw(affines, affines_mean, affines_square, grads[5], 0.4, 0.0)
    return (output.astype(jnp.bfloat16), grads[0], proj_new[0], proj_new[1], proj_new[2], comb_new[0], comb_new[1], comb_new[2], expand_new[0], expand_new[1], expand_new[2], reduce_new[0], reduce_new[1], reduce_new[2], affine_new[0], affine_new[1], affine_new[2], proj_new[0].astype(jnp.bfloat16), comb_new[0].astype(jnp.bfloat16), expand_new[0].astype(jnp.bfloat16), reduce_new[0].astype(jnp.bfloat16))
```

```python
import math

import jax
import jax.numpy as jnp
from jax import lax
from jax.experimental import pallas as pl
from jax.experimental.pallas import tpu as pltpu
from jax.sharding import PartitionSpec as P

D = 256
FF = 2048
HD = 32
SEQ = 1024
WROW = 32
STEP = 5
LANES = 128
LOG2E = 1.4426950408889634
INTERPRET = False
BF = jnp.bfloat16
F32 = jnp.float32


def dot(a, b):
    return jnp.dot(a, b, preferred_element_type=F32)


def dot_nt(a, b):
    return lax.dot_general(a, b, (((1,), (1,)), ((), ())), preferred_element_type=F32)


def flip(x):
    if x.dtype == BF:
        return x.astype(F32).T.astype(BF)
    return x.T


def lane_of(shape):
    return lax.broadcasted_iota(jnp.int32, shape, 1)


def row_of(shape):
    return lax.broadcasted_iota(jnp.int32, shape, 0)


def place_rows(x, start, total):
    parts = []
    if start:
        parts.append(jnp.zeros((start, x.shape[1]), x.dtype))
    parts.append(x)
    if total - start - x.shape[0]:
        parts.append(jnp.zeros((total - start - x.shape[0], x.shape[1]), x.dtype))
    return jnp.concatenate(parts, axis=0) if len(parts) > 1 else x


def call(kernel, outs, *args, scratch=(), smem=0):
    vm = pl.BlockSpec(memory_space=pltpu.VMEM)
    sm = pl.BlockSpec(memory_space=pltpu.SMEM)
    return pl.pallas_call(
        kernel,
        out_shape=[jax.ShapeDtypeStruct(s, d) for s, d in outs],
        in_specs=[sm] * smem + [vm] * (len(args) - smem),
        out_specs=[vm] * len(outs),
        scratch_shapes=[pltpu.VMEM(s, d) for s, d in scratch],
        compiler_params=pltpu.CompilerParams(vmem_limit_bytes=48 * 2**20),
        interpret=INTERPRET,
    )(*args)


def prepare_kernel(tokens, projector, combiner_t, expander, reducer_t, affines, pack, query_in):
    seq, width = tokens.shape
    cl = projector.shape[2]
    fl = expander.shape[1]
    copies = pack.shape[0]
    dl = expander.shape[0]
    low = [projector[i].astype(BF) for i in range(3)] + [combiner_t[...].astype(BF)]
    gains = jnp.concatenate([affines[...], jnp.zeros((LANES - 4, dl), F32)], axis=0).T
    high = gains.astype(BF).astype(F32)
    rest = pltpu.roll(gains - high, 4, 1)
    tail = jnp.where(lane_of(high.shape) < 4, high, rest).astype(BF)
    whole = jnp.concatenate(
        low + [expander[...].astype(BF), reducer_t[...].astype(BF), tail], axis=1
    )
    for i in range(copies):
        pack[i] = whole
    half = width // 2
    rows = seq // WROW
    shape = (max(rows, WROW), half)
    channel = lane_of(shape)
    exponent = (2 * (channel // 2)).astype(F32) / half
    angles = (row_of(shape) + 1).astype(F32) * jnp.exp(-math.log(10000.0) * exponent)
    table = jnp.where(channel % 2 == 0, jnp.sin(angles), jnp.cos(angles))
    for i in range(rows):
        lower = i * WROW
        spot = jnp.concatenate(
            [jnp.broadcast_to(table[i : i + 1], (WROW, half)), table[:WROW]], axis=1
        )
        part = tokens[lower : lower + WROW, :].astype(F32) + spot
        query_in[lower : lower + WROW, :] = part.astype(BF)


def key_bias(length, start, count, lanes):
    place = row_of((count, lanes)) + start
    return jnp.where(place < length, 0.0, -1e30).astype(F32)


def attend_kernel(blocks, chunk, info, tokens, query_in, *refs):
    ins, outs, (scores, raised) = refs[:blocks], refs[blocks:-2], refs[-2:]
    seq = tokens.shape[0]
    length, offset = info[0], info[1]
    fold = HD**-0.5 * LOG2E
    for b in range(blocks):
        block = ins[b][...]
        z, q_t, context_t, logsum = outs[4 * b : 4 * b + 4]
        bw = block.shape[1]
        cl = bw // 4
        rows = q_t.shape[1]
        from_query = dot(query_in[...], block)
        from_token = dot(tokens[...], block)
        z[...] = jnp.where(lane_of((1, bw)) < 2 * cl, from_query, from_token).astype(BF)
        own = query_in[pl.ds(pl.multiple_of(offset, 8), rows), :]
        q_all = flip(dot(own, block).astype(BF))
        q_t[...] = q_all[:cl]
        z_t = flip(z[...])
        for h in range(cl // HD):
            lower = h * HD
            side = place_rows(q_all[lower : lower + HD], cl + lower, bw)
            peak = jnp.full((1, rows), -jnp.inf, F32)
            for c in range(0, seq, chunk):
                part = dot(z[c : c + chunk, :], side) * fold + key_bias(length, c, chunk, rows)
                scores[c : c + chunk, :] = part
                peak = jnp.maximum(peak, jnp.max(part, axis=0, keepdims=True))
            total = jnp.zeros((1, rows), F32)
            for c in range(0, seq, chunk):
                part = jnp.exp2(scores[c : c + chunk, :] - peak)
                total = total + jnp.sum(part, axis=0, keepdims=True)
                raised[c : c + chunk, :] = part.astype(BF)
            mixed = dot(z_t[2 * cl + lower : 2 * cl + lower + HD], raised[...])
            context_t[lower : lower + HD, :] = mixed / total
            logsum[h : h + 1, :] = peak + jnp.log(total) * LOG2E


def norm(x):
    average = jnp.mean(x, axis=-1, keepdims=True)
    centred = x - average
    scale = lax.rsqrt(jnp.mean(centred * centred, axis=-1, keepdims=True) + 1e-05)
    return centred * scale, scale


def norm_back(grad, unit, scale, gains):
    inner = grad * gains
    mean_one = jnp.mean(inner, axis=-1, keepdims=True)
    mean_two = jnp.mean(inner * unit, axis=-1, keepdims=True)
    back = scale * (inner - mean_one - unit * mean_two)
    gain_grad = jnp.sum(grad * unit, axis=0, keepdims=True)
    bias_grad = jnp.sum(grad, axis=0, keepdims=True)
    return back, gain_grad, bias_grad


def feed_kernel(blocks, info, tokens, cotangent, *refs):
    contexts, attention_blocks, feed_blocks = (
        refs[:blocks],
        refs[blocks : 2 * blocks],
        refs[2 * blocks : 3 * blocks],
    )
    layer_out, grad_one, *grads = refs[3 * blocks : 4 * blocks + 2]
    pre_all, hidden_all = refs[4 * blocks + 2 :]
    rows, width = layer_out.shape
    length, offset = info[0], pl.multiple_of(info[1], 8)
    bw = attention_blocks[0].shape[1]
    cl = bw // 4
    fl = (feed_blocks[0].shape[1] - LANES) // 2
    own = tokens[pl.ds(offset, rows), :].astype(F32)
    attention = jnp.zeros((rows, width), F32)
    for b in range(blocks):
        context = flip(place_rows(contexts[b][...].astype(BF), 3 * cl, bw))
        attention = attention + dot_nt(context, attention_blocks[b][...])
    pieces = feed_blocks[0][:, 2 * fl :].astype(F32).T
    gain_one, bias_one, gain_two, bias_two = (
        pieces[i : i + 1] + pieces[i + 4 : i + 5] for i in range(4)
    )
    unit_one, scale_one = norm(own + attention)
    first = unit_one * gain_one + bias_one
    first_low = first.astype(BF)
    feed = jnp.zeros((rows, width), F32)
    for b in range(blocks):
        pre = dot(first_low, feed_blocks[b][:, :fl])
        inner = 0.7978845608 * (pre + 0.044715 * (pre * pre * pre))
        hidden = (0.5 * pre * (1.0 + jnp.tanh(inner))).astype(BF)
        pre_all[b] = pre
        hidden_all[b] = hidden
        feed = feed + dot_nt(hidden, feed_blocks[b][:, fl : 2 * fl])
    unit_two, scale_two = norm(first + feed)
    layer_out[...] = (unit_two * gain_two + bias_two).astype(BF)
    live = (row_of((rows, width)) + offset) < length
    seed = jnp.where(live, cotangent[pl.ds(offset, rows), :].astype(F32), 0.0)
    grad_two, d_gain_two, d_bias_two = norm_back(seed, unit_two, scale_two, gain_two)
    grad_two_low = grad_two.astype(BF)
    grad_two_t = flip(grad_two_low)
    first_t = flip(first_low)
    grad_first = grad_two
    for b in range(blocks):
        grad_hidden = dot(grad_two_low, feed_blocks[b][:, fl : 2 * fl])
        pre = pre_all[b]
        square = pre * pre
        bend = jnp.tanh(0.7978845608 * (pre + 0.044715 * (square * pre)))
        slope = 0.5 * (1.0 + bend) + (0.5 * pre) * (1.0 - bend * bend) * (
            0.7978845608 * (1.0 + 0.134145 * square)
        )
        grad_pre = (grad_hidden * slope).astype(BF)
        grads[b][:, :fl] = dot(first_t, grad_pre).astype(BF)
        grads[b][:, fl : 2 * fl] = dot(grad_two_t, hidden_all[b]).astype(BF)
        grad_first = grad_first + dot_nt(grad_pre, feed_blocks[b][:, :fl])
    back, d_gain_one, d_bias_one = norm_back(grad_first, unit_one, scale_one, gain_one)
    grad_one[...] = back
    stacked = jnp.concatenate(
        [d_gain_one, d_bias_one, d_gain_two, d_bias_two, jnp.zeros((LANES - 4, width), F32)], axis=0
    )
    columns = stacked.T.astype(BF)
    for b in range(blocks):
        grads[b][:, 2 * fl :] = columns


def attend_back_kernel(blocks, chunk, info, tokens, query_in, grad_one, *refs):
    ins = refs[: 5 * blocks]
    outs = refs[5 * blocks : 6 * blocks]
    input_part, score_grads, sums, total = refs[6 * blocks :]
    seq, width = tokens.shape
    rows = grad_one.shape[0]
    length, offset = info[0], pl.multiple_of(info[1], 8)
    scaling = HD**-0.5
    fold = scaling * LOG2E
    grad_low = grad_one[...].astype(BF)
    grad_t = flip(grad_low)
    own_t = flip(query_in[pl.ds(offset, rows), :])
    query_in_t = flip(query_in[...])
    tokens_t = flip(tokens[...])
    total[...] = jnp.zeros((seq, width), F32)
    own_total = grad_one[...]
    for b in range(blocks):
        block_ref, z, q_t, context_ref, logsum = ins[5 * b : 5 * b + 5]
        block = block_ref[...]
        bw = block.shape[1]
        cl = bw // 4
        lane = lane_of((1, bw))
        context_t = context_ref[...]
        grad_context_t = flip(dot(grad_low, block).astype(BF))[3 * cl :]
        z_t = flip(z[...])
        q_side = flip(place_rows(q_t[...], cl, bw))
        grad_side = flip(place_rows(grad_context_t, 2 * cl, bw))
        query_grads = []
        for h in range(cl // HD):
            lower = h * HD
            grad_head = grad_context_t[lower : lower + HD]
            delta = jnp.sum(
                grad_head.astype(F32) * context_t[lower : lower + HD], axis=0, keepdims=True
            )
            side_q = place_rows(q_t[lower : lower + HD, :], cl + lower, bw)
            side_g = place_rows(grad_head, 2 * cl + lower, bw)
            mask_q = (lane >= cl + lower) & (lane < cl + lower + HD)
            mask_g = (lane >= 2 * cl + lower) & (lane < 2 * cl + lower + HD)
            q_head = jnp.where(mask_q, q_side.astype(F32), 0.0).astype(BF)
            g_head = jnp.where(mask_g, grad_side.astype(F32), 0.0).astype(BF)
            shift = logsum[h : h + 1, :]
            for c in range(0, seq, chunk):
                keys = z[c : c + chunk, :]
                part = dot(keys, side_q) * fold + key_bias(length, c, chunk, rows)
                weights = jnp.exp2(part - shift)
                slopes = (weights * (dot(keys, side_g) - delta)).astype(BF)
                score_grads[c : c + chunk, :] = slopes
                piece = dot(slopes, q_head) + dot(weights.astype(BF), g_head)
                if h:
                    piece = piece + sums[c : c + chunk, :]
                sums[c : c + chunk, :] = piece
            query_grads.append(
                (dot(z_t[cl + lower : cl + lower + HD], score_grads[...]) * scaling).astype(BF)
            )
        both = (sums[...] * jnp.where(lane < 2 * cl, scaling, 1.0)).astype(BF)
        query_grad = flip(place_rows(jnp.concatenate(query_grads, axis=0), 0, bw))
        context = flip(place_rows(context_t.astype(BF), 3 * cl, bw))
        of_query = dot(query_in_t, both)
        of_token = dot(tokens_t, both)
        weight_grad = dot(own_t, query_grad) + dot(grad_t, context)
        outs[b][...] = (weight_grad + jnp.where(lane < 2 * cl, of_query, of_token)).astype(BF)
        total[...] += dot_nt(both, block)
        own_total = own_total + dot_nt(query_grad, block)
    total[pl.ds(offset, rows), :] += own_total
    input_part[...] = total[...].astype(BF)


def adamw(weight, moment_one, moment_two, grad, step_rate, decay_rate):
    mean_next = 0.5 * moment_one + 0.5 * grad
    square_next = 0.5 * moment_two + 0.5 * grad * grad
    correct = 1.0 - 0.5**STEP
    direction = mean_next / correct / (jnp.sqrt(square_next / correct) + 1e-08)
    weight_next = weight - step_rate * (direction + decay_rate * weight)
    return (weight_next, mean_next, square_next)


def update_kernel(rates, sent, *refs):
    ins, outs, pack = refs[:15], refs[15:30], refs[30]
    dl = pack.shape[1]
    sources = sent.shape[0] // dl
    grad = sent[:dl, :].astype(F32)
    for i in range(1, sources):
        grad = grad + sent[i * dl : (i + 1) * dl, :].astype(F32)
    cl = ins[0].shape[2]
    fl = ins[6].shape[1]
    fresh = []
    for i in range(3):
        fresh.append(
            adamw(*(ins[k][i] for k in range(3)), grad[:, i * cl : (i + 1) * cl], *rates[0])
        )
        for k in range(3):
            outs[k][i] = fresh[-1][k]
    start = 3 * cl
    for j, size in ((1, cl), (2, fl), (3, fl)):
        fresh.append(
            adamw(*(ins[3 * j + k][...] for k in range(3)), grad[:, start : start + size], *rates[j])
        )
        for k in range(3):
            outs[3 * j + k][...] = fresh[-1][k]
        start += size
    small = grad[:, start:].T[:4]
    for k, value in enumerate(adamw(*(ins[12 + k][...] for k in range(3)), small, *rates[4])):
        outs[12 + k][...] = value
    whole = jnp.concatenate([new[0].astype(BF) for new in fresh], axis=1)
    for i in range(pack.shape[0]):
        pack[i] = whole


def finish_kernel(copies, projector_t, combiner, expander, reducer):
    cl = combiner.shape[0]
    fl = reducer.shape[0]
    for i in range(3):
        projector_t[i] = flip(copies[:, i * cl : (i + 1) * cl])
    combiner[...] = flip(copies[:, 3 * cl : 4 * cl])
    expander[...] = copies[:, 4 * cl : 4 * cl + fl]
    reducer[...] = flip(copies[:, 4 * cl + fl : 4 * cl + 2 * fl])


def body(
    tokens,
    cotangent,
    lengths,
    projector,
    projector_mean,
    projector_square,
    combiner,
    combiner_mean,
    combiner_square,
    expander,
    expander_mean,
    expander_square,
    reducer,
    reducer_mean,
    reducer_square,
    affines,
    affines_mean,
    affines_square,
):
    mp = lax.axis_size("mp")
    dp = lax.axis_size("dp")
    me = lax.axis_index("mp")
    seq = tokens.shape[0]
    if lengths.shape[0] != 1 or mp & (mp - 1):
        raise ValueError("unsupported mesh")
    rows = seq // mp
    dl = expander.shape[0]
    cl = projector.shape[2]
    fl = expander.shape[1]
    bw = 4 * cl
    heads = cl // HD
    chunk = 256
    info = jnp.stack([lengths[0], me.astype(jnp.int32) * rows])

    def swap(x, bit):
        return lax.ppermute(x, "mp", [(i, i ^ bit) for i in range(mp)])

    pack_width = bw + 2 * fl + LANES
    pack, query_in = call(
        prepare_kernel,
        [((dp, dl, pack_width), BF), ((seq, D), BF)],
        tokens,
        projector,
        combiner.T,
        expander,
        reducer.T,
        affines,
    )
    gathered = lax.all_to_all(pack, "dp", 0, 0, tiled=True).reshape(D, pack_width)
    attention_blocks = {0: gathered[:, :bw]}
    feed_blocks = {0: gathered[:, bw:]}
    bits = [1 << i for i in range(1, mp.bit_length() - 1)] + [1]
    for blocks in (attention_blocks, feed_blocks):
        for bit in bits:
            for r in list(blocks):
                blocks[r ^ bit] = swap(blocks[r], bit)
    names = list(range(mp))

    def attend_outs():
        return [((seq, bw), BF), ((cl, rows), BF), ((cl, rows), F32), ((heads, rows), F32)]

    kept = call(
        lambda *refs: attend_kernel(mp, chunk, *refs),
        attend_outs() * mp,
        info,
        tokens,
        query_in,
        *(attention_blocks[r] for r in names),
        scratch=[((seq, rows), F32), ((seq, rows), BF)],
        smem=1,
    )
    kept = [kept[4 * r : 4 * r + 4] for r in names]
    own_out, grad_one, *feed_grads = call(
        lambda *refs: feed_kernel(mp, *refs),
        [((rows, D), BF), ((rows, D), F32)] + [((D, 2 * fl + LANES), BF)] * mp,
        info,
        tokens,
        cotangent,
        *(kept[r][2] for r in names),
        *(attention_blocks[r] for r in names),
        *(feed_blocks[r] for r in names),
        scratch=[((mp, rows, fl), F32), ((mp, rows, fl), BF)],
        smem=1,
    )
    *attention_grads, input_part = call(
        lambda *refs: attend_back_kernel(mp, chunk, *refs),
        [((D, bw), BF)] * mp + [((seq, D), BF)],
        info,
        tokens,
        query_in,
        grad_one,
        *(x for r in names for x in (attention_blocks[r], *kept[r])),
        scratch=[((seq, rows), BF), ((seq, bw), F32), ((seq, D), F32)],
        smem=1,
    )

    def reduce_blocks(grads):
        left = dict(zip(names, grads, strict=True))
        for bit in reversed(bits):
            for r in [r for r in left if not r & bit]:
                left[r] = left[r] + swap(left.pop(r ^ bit), bit)
        return left[0]

    own_grads = jnp.concatenate(
        [reduce_blocks(attention_grads), reduce_blocks(feed_grads)], axis=1
    )
    sent = lax.all_to_all(own_grads.reshape(dp, dl, pack_width), "dp", 0, 0, tiled=True)
    masters = (
        (projector, projector_mean, projector_square),
        (combiner.T, combiner_mean.T, combiner_square.T),
        (expander, expander_mean, expander_square),
        (reducer.T, reducer_mean.T, reducer_square.T),
        (affines, affines_mean, affines_square),
    )
    rates = (
        (D ** (-0.5), 0.0001),
        (max(1, D * 8 // SEQ) ** (-0.5), 0.0001),
        (D ** (-0.5), 0.0001),
        (FF ** (-0.5), 0.0001),
        (0.4, 0.0),
    )
    flat = [x for three in masters for x in three]
    *fresh, new_pack = call(
        lambda *refs: update_kernel(rates, *refs),
        [(x.shape, F32) for x in flat] + [((dp, dl, bw + 2 * fl), BF)],
        sent.reshape(D, pack_width),
        *flat,
    )
    new_low = lax.all_to_all(new_pack, "dp", 0, 0, tiled=True).reshape(D, bw + 2 * fl)
    projector_copy, combiner_copy, expander_copy, reducer_copy = call(
        finish_kernel,
        [((3, cl, D), BF), ((cl, D), BF), ((D, fl), BF), ((fl, D), BF)],
        new_low,
    )
    for i in (3, 4, 5, 9, 10, 11):
        fresh[i] = fresh[i].T
    layer_out = lax.all_gather(own_out, "mp", axis=0, tiled=True)
    for bit in bits:
        input_part = input_part + swap(input_part, bit)
    return (
        layer_out,
        input_part.astype(F32),
        *fresh,
        jnp.swapaxes(projector_copy, 1, 2),
        combiner_copy,
        expander_copy,
        reducer_copy,
    )


def solution(mesh):
    rows = P("dp", None)
    by_weight = [P(None, "dp", "mp"), P("mp", "dp"), P("dp", "mp"), P("mp", "dp"), P(None, "dp")]
    threes = [spec for spec in by_weight for _ in range(3)]
    return jax.shard_map(
        body,
        mesh=mesh,
        in_specs=(rows, rows, P("dp"), *threes),
        out_specs=(
            rows,
            rows,
            *threes,
            P(None, None, "mp"),
            P("mp", None),
            P(None, "mp"),
            P("mp", None),
        ),
        check_vma=False,
    )
```

```python
import math

import jax
import jax.numpy as jnp
from jax import lax
from jax.experimental import pallas as pl
from jax.experimental.pallas import tpu as pltpu
from jax.sharding import PartitionSpec as P

D = 256
FF = 2048
HD = 32
SEQ = 1024
WROW = 32
STEP = 5
LANES = 128
LOG2E = 1.4426950408889634
INTERPRET = False
BF = jnp.bfloat16
F32 = jnp.float32


def dot(a, b):
    return jnp.dot(a, b, preferred_element_type=F32)


def dot_nt(a, b):
    return lax.dot_general(a, b, (((1,), (1,)), ((), ())), preferred_element_type=F32)


def flip(x):
    if x.dtype == BF:
        return x.astype(F32).T.astype(BF)
    return x.T


def lane_of(shape):
    return lax.broadcasted_iota(jnp.int32, shape, 1)


def row_of(shape):
    return lax.broadcasted_iota(jnp.int32, shape, 0)


def place_rows(x, start, total):
    parts = []
    if start:
        parts.append(jnp.zeros((start, x.shape[1]), x.dtype))
    parts.append(x)
    if total - start - x.shape[0]:
        parts.append(jnp.zeros((total - start - x.shape[0], x.shape[1]), x.dtype))
    return jnp.concatenate(parts, axis=0) if len(parts) > 1 else x


def call(kernel, outs, *args, scratch=(), smem=0, fetched=False, flops=0):
    vm = pl.BlockSpec(memory_space=pltpu.VMEM)
    given = pl.BlockSpec(memory_space=pl.ANY) if fetched else vm
    buffers = [pltpu.VMEM(s, d) for s, d in scratch]
    if fetched:
        buffers = [pltpu.VMEM(x.shape, x.dtype) for x in args] + buffers
        buffers.append(pltpu.SemaphoreType.DMA((len(args),)))
    sm = pl.BlockSpec(memory_space=pltpu.SMEM)
    return pl.pallas_call(
        kernel,
        out_shape=[jax.ShapeDtypeStruct(s, d) for s, d in outs],
        in_specs=[sm] * smem + [given] * (len(args) - smem),
        out_specs=[vm] * len(outs),
        scratch_shapes=buffers,
        cost_estimate=pl.CostEstimate(flops=flops, transcendentals=0, bytes_accessed=0) if flops else None,
        compiler_params=pltpu.CompilerParams(vmem_limit_bytes=24 * 2**20),
        interpret=INTERPRET,
    )(*args)


def prepare_kernel(*refs):
    given, outs, held, arrived = refs[:6], refs[6:8], refs[8:14], refs[14]
    fetches = [
        pltpu.make_async_copy(source, target, arrived.at[i])
        for i, (source, target) in enumerate(zip(given, held, strict=True))
    ]
    for fetch in fetches:
        fetch.start()
    tokens, projector, combiner_t, expander, reducer_t, affines = held
    pack, query_in = outs
    seq, width = tokens.shape
    dl = expander.shape[0]
    half = width // 2
    rows = seq // WROW
    shape = (max(rows, WROW), half)
    channel = lane_of(shape)
    exponent = (2 * (channel // 2)).astype(F32) / half
    angles = (row_of(shape) + 1).astype(F32) * jnp.exp(-math.log(10000.0) * exponent)
    table = jnp.where(channel % 2 == 0, jnp.sin(angles), jnp.cos(angles))
    for fetch in fetches:
        fetch.wait()
    gains = jnp.concatenate([affines[...], jnp.zeros((LANES - 4, dl), F32)], axis=0).T
    high = gains.astype(BF).astype(F32)
    rest = pltpu.roll(gains - high, 4, 1)
    tail = jnp.where(lane_of(high.shape) < 4, high, rest).astype(BF)
    low = [projector[i].astype(BF) for i in range(3)] + [combiner_t[...].astype(BF)]
    whole = jnp.concatenate(
        low + [expander[...].astype(BF), reducer_t[...].astype(BF), tail], axis=1
    )
    for i in range(pack.shape[0]):
        pack[i] = whole
    for i in range(rows):
        lower = i * WROW
        spot = jnp.concatenate(
            [jnp.broadcast_to(table[i : i + 1], (WROW, half)), table[:WROW]], axis=1
        )
        part = tokens[lower : lower + WROW, :].astype(F32) + spot
        query_in[lower : lower + WROW, :] = part.astype(BF)


def key_bias(length, start, count, lanes):
    place = row_of((count, lanes)) + start
    return jnp.where(place < length, 0.0, -1e30).astype(F32)


def attend_kernel(blocks, chunk, info, tokens, query_in, *refs):
    ins, outs, scores = refs[:blocks], refs[blocks:-1], refs[-1]
    seq = tokens.shape[0]
    length, offset = info[0], info[1]
    fold = HD**-0.5 * LOG2E
    for b in range(blocks):
        block = ins[b][...]
        z, q_t, context_t, inverse, raised = outs[5 * b : 5 * b + 5]
        bw = block.shape[1]
        cl = bw // 4
        rows = q_t.shape[1]
        from_query = dot(query_in[...], block)
        from_token = dot(tokens[...], block)
        z[...] = jnp.where(lane_of((1, bw)) < 2 * cl, from_query, from_token).astype(BF)
        own = query_in[pl.ds(pl.multiple_of(offset, 8), rows), :]
        q_all = flip(dot(own, block).astype(BF))
        q_t[...] = q_all[:cl]
        z_t = flip(z[...])
        for h in range(cl // HD):
            lower = h * HD
            side = place_rows(q_all[lower : lower + HD], cl + lower, bw)
            peak = jnp.full((1, rows), -jnp.inf, F32)
            for c in range(0, seq, chunk):
                part = dot(z[c : c + chunk, :], side) * fold + key_bias(length, c, chunk, rows)
                scores[c : c + chunk, :] = part
                peak = jnp.maximum(peak, jnp.max(part, axis=0, keepdims=True))
            total = jnp.zeros((1, rows), F32)
            for c in range(0, seq, chunk):
                part = jnp.exp2(scores[c : c + chunk, :] - peak)
                total = total + jnp.sum(part, axis=0, keepdims=True)
                raised[h, c : c + chunk, :] = part.astype(BF)
            mixed = dot(z_t[2 * cl + lower : 2 * cl + lower + HD], raised[h])
            scale = 1.0 / total
            context_t[lower : lower + HD, :] = mixed * scale
            inverse[h : h + 1, :] = scale


def norm(x):
    average = jnp.mean(x, axis=-1, keepdims=True)
    centred = x - average
    scale = lax.rsqrt(jnp.mean(centred * centred, axis=-1, keepdims=True) + 1e-05)
    return centred * scale, scale


def norm_back(grad, unit, scale, gains):
    inner = grad * gains
    mean_one = jnp.mean(inner, axis=-1, keepdims=True)
    mean_two = jnp.mean(inner * unit, axis=-1, keepdims=True)
    back = scale * (inner - mean_one - unit * mean_two)
    gain_grad = jnp.sum(grad * unit, axis=0, keepdims=True)
    bias_grad = jnp.sum(grad, axis=0, keepdims=True)
    return back, gain_grad, bias_grad


def feed_kernel(blocks, info, tokens, cotangent, *refs):
    contexts, attention_blocks, feed_blocks = (
        refs[i * blocks : (i + 1) * blocks] for i in range(3)
    )
    layer_out, grad_one, *grads = refs[3 * blocks : 4 * blocks + 2]
    pre_all, hidden_all = refs[4 * blocks + 2 :]
    rows, width = layer_out.shape
    length, offset = info[0], pl.multiple_of(info[1], 8)
    bw = attention_blocks[0].shape[1]
    cl = bw // 4
    fl = (feed_blocks[0].shape[1] - LANES) // 2
    own = tokens[pl.ds(offset, rows), :].astype(F32)
    attention = jnp.zeros((rows, width), F32)
    for b in range(blocks):
        context = flip(place_rows(contexts[b][...].astype(BF), 3 * cl, bw))
        attention = attention + dot_nt(context, attention_blocks[b][...])
    pieces = feed_blocks[0][:, 2 * fl :].astype(F32).T
    gain_one, bias_one, gain_two, bias_two = (
        pieces[i : i + 1] + pieces[i + 4 : i + 5] for i in range(4)
    )
    unit_one, scale_one = norm(own + attention)
    first = unit_one * gain_one + bias_one
    first_low = first.astype(BF)
    feed = jnp.zeros((rows, width), F32)
    for b in range(blocks):
        pre = dot(first_low, feed_blocks[b][:, :fl])
        inner = 0.7978845608 * (pre + 0.044715 * (pre * pre * pre))
        hidden = (0.5 * pre * (1.0 + jnp.tanh(inner))).astype(BF)
        pre_all[b] = pre
        hidden_all[b] = hidden
        feed = feed + dot_nt(hidden, feed_blocks[b][:, fl : 2 * fl])
    unit_two, scale_two = norm(first + feed)
    layer_out[...] = (unit_two * gain_two + bias_two).astype(BF)
    live = (row_of((rows, width)) + offset) < length
    seed = jnp.where(live, cotangent[pl.ds(offset, rows), :].astype(F32), 0.0)
    grad_two, d_gain_two, d_bias_two = norm_back(seed, unit_two, scale_two, gain_two)
    grad_two_low = grad_two.astype(BF)
    grad_two_t = flip(grad_two_low)
    first_t = flip(first_low)
    grad_first = grad_two
    for b in range(blocks):
        grad_hidden = dot(grad_two_low, feed_blocks[b][:, fl : 2 * fl])
        pre = pre_all[b]
        square = pre * pre
        bend = jnp.tanh(0.7978845608 * (pre + 0.044715 * (square * pre)))
        slope = 0.5 * (1.0 + bend) + (0.5 * pre) * (1.0 - bend * bend) * (
            0.7978845608 * (1.0 + 0.134145 * square)
        )
        grad_pre = (grad_hidden * slope).astype(BF)
        grads[b][:, :fl] = dot(first_t, grad_pre).astype(BF)
        grads[b][:, fl : 2 * fl] = dot(grad_two_t, hidden_all[b]).astype(BF)
        grad_first = grad_first + dot_nt(grad_pre, feed_blocks[b][:, :fl])
    back, d_gain_one, d_bias_one = norm_back(grad_first, unit_one, scale_one, gain_one)
    grad_one[...] = back
    stacked = jnp.concatenate(
        [d_gain_one, d_bias_one, d_gain_two, d_bias_two, jnp.zeros((LANES - 4, width), F32)], axis=0
    )
    columns = stacked.T.astype(BF)
    for b in range(blocks):
        grads[b][:, 2 * fl :] = columns


def attend_back_kernel(blocks, chunk, info, tokens, query_in, grad_one, *refs):
    ins = refs[: 6 * blocks]
    rest = refs[6 * blocks :]
    earlier = rest[0] if len(rest) == blocks + 5 else None
    outs = rest[-blocks - 4 : -4]
    input_part, score_grads, sums, total = rest[-4:]
    seq, width = tokens.shape
    rows = grad_one.shape[0]
    offset = pl.multiple_of(info[1], 8)
    scaling = HD**-0.5
    grad_low = grad_one[...].astype(BF)
    grad_t = flip(grad_low)
    own_t = flip(query_in[pl.ds(offset, rows), :])
    query_in_t = flip(query_in[...])
    tokens_t = flip(tokens[...])
    own_total = grad_one[...] if earlier is None else jnp.zeros((rows, width), F32)
    for b in range(blocks):
        block_ref, z, q_t, context_ref, inverse, raised = ins[6 * b : 6 * b + 6]
        block = block_ref[...]
        bw = block.shape[1]
        cl = bw // 4
        lane = lane_of((1, bw))
        context_t = context_ref[...]
        grad_context_t = dot(grad_low, block).T[3 * cl :]
        scaled = [
            (grad_context_t[h * HD : (h + 1) * HD] * inverse[h : h + 1, :]).astype(BF)
            for h in range(cl // HD)
        ]
        z_t = flip(z[...])
        q_side = flip(place_rows(q_t[...], cl, bw)).astype(F32)
        grad_side = flip(place_rows(jnp.concatenate(scaled, axis=0), 2 * cl, bw)).astype(F32)
        query_grads = []
        for h in range(cl // HD):
            lower = h * HD
            delta = jnp.sum(
                scaled[h].astype(F32) * context_t[lower : lower + HD], axis=0, keepdims=True
            )
            side_g = place_rows(scaled[h], 2 * cl + lower, bw)
            mask_q = (lane >= cl + lower) & (lane < cl + lower + HD)
            mask_g = (lane >= 2 * cl + lower) & (lane < 2 * cl + lower + HD)
            q_head = jnp.where(mask_q, q_side, 0.0).astype(BF)
            g_head = jnp.where(mask_g, grad_side, 0.0).astype(BF)
            for c in range(0, seq, chunk):
                weights = raised[h, c : c + chunk, :]
                slopes = weights.astype(F32) * (dot(z[c : c + chunk, :], side_g) - delta)
                slopes = slopes.astype(BF)
                score_grads[c : c + chunk, :] = slopes
                piece = dot(slopes, q_head) + dot(weights, g_head)
                if h:
                    piece = piece + sums[c : c + chunk, :]
                sums[c : c + chunk, :] = piece
            query_grads.append(
                (dot(z_t[cl + lower : cl + lower + HD], score_grads[...]) * scaling).astype(BF)
            )
        both = (sums[...] * jnp.where(lane < 2 * cl, scaling, 1.0)).astype(BF)
        query_grad = flip(place_rows(jnp.concatenate(query_grads, axis=0), 0, bw))
        context = flip(place_rows(context_t.astype(BF), 3 * cl, bw))
        of_query = dot(query_in_t, both)
        of_token = dot(tokens_t, both)
        weight_grad = dot(own_t, query_grad) + dot(grad_t, context)
        outs[b][...] = (weight_grad + jnp.where(lane < 2 * cl, of_query, of_token)).astype(BF)
        part = dot_nt(both, block)
        if b:
            part = part + total[...]
        elif earlier is not None:
            part = part + earlier[...]
        total[...] = part
        own_total = own_total + dot_nt(query_grad, block)
    total[pl.ds(offset, rows), :] += own_total
    input_part[...] = total[...].astype(input_part.dtype)


def merge_kernel(*refs):
    *ins, out = refs
    bw = ins[0].shape[1]
    out[:, :bw] = (ins[0][...].astype(F32) + ins[1][...].astype(F32)).astype(BF)
    total = ins[2][...].astype(F32)
    for extra in ins[3:]:
        total = total + extra[...].astype(F32)
    out[:, bw:] = total.astype(BF)


def adamw(weight, moment_one, moment_two, grad, step_rate, decay_rate):
    mean_next = 0.5 * moment_one + 0.5 * grad
    square_next = 0.5 * moment_two + 0.5 * grad * grad
    correct = 1.0 - 0.5**STEP
    direction = mean_next / correct / (jnp.sqrt(square_next / correct) + 1e-08)
    weight_next = weight - step_rate * (direction + decay_rate * weight)
    return (weight_next, mean_next, square_next)


def update_kernel(rates, sent, *refs):
    ins, outs, pack = refs[:15], refs[15:30], refs[30]
    dl = pack.shape[1]
    sources = sent.shape[0] // dl
    grad = sent[:dl, :].astype(F32)
    for i in range(1, sources):
        grad = grad + sent[i * dl : (i + 1) * dl, :].astype(F32)
    cl = ins[0].shape[2]
    fl = ins[6].shape[1]
    fresh = []
    for i in range(3):
        fresh.append(
            adamw(*(ins[k][i] for k in range(3)), grad[:, i * cl : (i + 1) * cl], *rates[0])
        )
        for k in range(3):
            outs[k][i] = fresh[-1][k]
    start = 3 * cl
    for j, size in ((1, cl), (2, fl), (3, fl)):
        fresh.append(
            adamw(*(ins[3 * j + k][...] for k in range(3)), grad[:, start : start + size], *rates[j])
        )
        for k in range(3):
            outs[3 * j + k][...] = fresh[-1][k]
        start += size
    small = grad[:, start:].T[:4]
    for k, value in enumerate(adamw(*(ins[12 + k][...] for k in range(3)), small, *rates[4])):
        outs[12 + k][...] = value
    whole = jnp.concatenate([new[0].astype(BF) for new in fresh], axis=1)
    for i in range(pack.shape[0]):
        pack[i] = whole


def finish_kernel(copies, projector_t, combiner, expander, reducer):
    cl = combiner.shape[0]
    fl = reducer.shape[0]
    for i in range(3):
        projector_t[i] = flip(copies[:, i * cl : (i + 1) * cl])
    combiner[...] = flip(copies[:, 3 * cl : 4 * cl])
    expander[...] = copies[:, 4 * cl : 4 * cl + fl]
    reducer[...] = flip(copies[:, 4 * cl + fl : 4 * cl + 2 * fl])


def body(
    tokens,
    cotangent,
    lengths,
    projector,
    projector_mean,
    projector_square,
    combiner,
    combiner_mean,
    combiner_square,
    expander,
    expander_mean,
    expander_square,
    reducer,
    reducer_mean,
    reducer_square,
    affines,
    affines_mean,
    affines_square,
):
    mp = lax.axis_size("mp")
    dp = lax.axis_size("dp")
    me = lax.axis_index("mp")
    seq = tokens.shape[0]
    if lengths.shape[0] != 1 or mp & (mp - 1):
        raise ValueError("unsupported mesh")
    rows = seq // mp
    dl = expander.shape[0]
    cl = projector.shape[2]
    fl = expander.shape[1]
    bw = 4 * cl
    heads = cl // HD
    chunk = 256
    info = jnp.stack([lengths[0], me.astype(jnp.int32) * rows])

    def swap(x, bit):
        return lax.ppermute(x, "mp", [(i, i ^ bit) for i in range(mp)])

    pack_width = bw + 2 * fl + LANES
    pack, query_in = call(
        prepare_kernel,
        [((dp, dl, pack_width), BF), ((seq, D), BF)],
        tokens,
        projector,
        combiner.T,
        expander,
        reducer.T,
        affines,
        fetched=True,
    )
    gathered = lax.all_to_all(pack, "dp", 0, 0, tiled=True).reshape(D, pack_width)
    names = list(range(mp))
    near, far = names[:2], names[2:]
    chip_bits = [1 << i for i in range(1, mp.bit_length() - 1)]
    attention_blocks = {0: gathered[:, :bw]}
    feed_blocks = {0: gathered[:, bw:]}
    attention_blocks[1] = swap(attention_blocks[0], 1)
    feed_blocks[0], attention_blocks[1] = lax.optimization_barrier(
        (feed_blocks[0], attention_blocks[1])
    )
    for blocks in (attention_blocks, feed_blocks):
        for bit in chip_bits:
            for r in [r for r in blocks if not r & 1]:
                blocks[r ^ bit] = swap(blocks[r], bit)
    def attend(group):
        made = call(
            lambda *refs: attend_kernel(len(group), chunk, *refs),
            [
                ((seq, bw), BF),
                ((cl, rows), BF),
                ((cl, rows), F32),
                ((heads, rows), F32),
                ((heads, seq, rows), BF),
            ]
            * len(group),
            info,
            tokens,
            query_in,
            *(attention_blocks[r] for r in group),
            scratch=[((seq, rows), F32)],
            smem=1,
            flops=4 * len(group) * (heads + 1) * seq * rows * D,
        )
        return {r: list(made[5 * i : 5 * i + 5]) for i, r in enumerate(group)}

    kept = attend(near)
    even = [attention_blocks[r] for r in far[::2]]
    *even, kept[0][2] = lax.optimization_barrier((*even, kept[0][2]))
    attention_blocks.update(zip(far[::2], even, strict=True))
    for r in far[::2]:
        attention_blocks[r ^ 1] = swap(attention_blocks[r], 1)
    kept.update(attend(far))
    even = [feed_blocks[r] for r in far[::2]]
    *even, kept[far[0]][2] = lax.optimization_barrier((*even, kept[far[0]][2]))
    feed_blocks.update(zip(far[::2], even, strict=True))
    for r in names[::2]:
        feed_blocks[r ^ 1] = swap(feed_blocks[r], 1)
    own_out, grad_one, *feed_grads = call(
        lambda *refs: feed_kernel(mp, *refs),
        [((rows, D), BF), ((rows, D), F32)]
        + [((D, 2 * fl + LANES), BF)] * mp,
        info,
        tokens,
        cotangent,
        *(kept[r][2] for r in names),
        *(attention_blocks[r] for r in names),
        *(feed_blocks[r] for r in names),
        scratch=[((mp, rows, fl), F32), ((mp, rows, fl), BF)],
        smem=1,
        flops=12 * mp * rows * D * fl,
    )

    def attend_back(group, earlier, dtype):
        return call(
            lambda *refs: attend_back_kernel(len(group), chunk, *refs),
            [((D, bw), BF)] * len(group) + [((seq, D), dtype)],
            info,
            tokens,
            query_in,
            grad_one,
            *(x for r in group for x in (attention_blocks[r], *kept[r])),
            *earlier,
            scratch=[((seq, rows), BF), ((seq, bw), F32), ((seq, D), F32)],
            smem=1,
            flops=8 * len(group) * (heads + 1) * seq * rows * D,
        )

    def reduce_blocks(left, order):
        left = dict(left)
        for bit in order:
            for r in [r for r in left if not r & bit]:
                left[r] = left[r] + swap(left.pop(r ^ bit), bit)
        return left

    down = chip_bits[::-1]
    feed_grads = reduce_blocks(zip(names, feed_grads, strict=True), [1])
    feed_grads, grad_one = lax.optimization_barrier((feed_grads, grad_one))
    *far_grads, far_part = attend_back(far, (), F32)
    *near_grads, input_part = attend_back(near, (far_part,), BF)
    attention_grads = zip(names, near_grads + far_grads, strict=True)
    bits = [*chip_bits, 1]
    attention_grads = reduce_blocks(attention_grads, down)
    feed_grads = reduce_blocks(feed_grads, down[:-1])
    [own_grads] = call(
        merge_kernel,
        [((D, pack_width), BF)],
        attention_grads[0],
        swap(attention_grads[1], 1),
        feed_grads[0],
        *(swap(feed_grads[r], r) for r in down[-1:]),
    )
    sent = lax.all_to_all(own_grads.reshape(dp, dl, pack_width), "dp", 0, 0, tiled=True)
    masters = (
        (projector, projector_mean, projector_square),
        (combiner.T, combiner_mean.T, combiner_square.T),
        (expander, expander_mean, expander_square),
        (reducer.T, reducer_mean.T, reducer_square.T),
        (affines, affines_mean, affines_square),
    )
    rates = (
        (D ** (-0.5), 0.0001),
        (max(1, D * 8 // SEQ) ** (-0.5), 0.0001),
        (D ** (-0.5), 0.0001),
        (FF ** (-0.5), 0.0001),
        (0.4, 0.0),
    )
    flat = [x for three in masters for x in three]
    *fresh, new_pack = call(
        lambda *refs: update_kernel(rates, *refs),
        [(x.shape, F32) for x in flat] + [((dp, dl, bw + 2 * fl), BF)],
        sent.reshape(D, pack_width),
        *flat,
    )
    new_low = lax.all_to_all(new_pack, "dp", 0, 0, tiled=True).reshape(D, bw + 2 * fl)
    projector_copy, combiner_copy, expander_copy, reducer_copy = call(
        finish_kernel,
        [((3, cl, D), BF), ((cl, D), BF), ((D, fl), BF), ((fl, D), BF)],
        new_low,
    )
    for i in (3, 4, 5, 9, 10, 11):
        fresh[i] = fresh[i].T
    layer_out = lax.all_gather(own_out, "mp", axis=0, tiled=True)
    for bit in bits:
        input_part = input_part + swap(input_part, bit)
    return (
        layer_out,
        input_part.astype(F32),
        *fresh,
        jnp.swapaxes(projector_copy, 1, 2),
        combiner_copy,
        expander_copy,
        reducer_copy,
    )


def solution(mesh):
    rows = P("dp", None)
    by_weight = [P(None, "dp", "mp"), P("mp", "dp"), P("dp", "mp"), P("mp", "dp"), P(None, "dp")]
    threes = [spec for spec in by_weight for _ in range(3)]
    return jax.shard_map(
        body,
        mesh=mesh,
        in_specs=(rows, rows, P("dp"), *threes),
        out_specs=(
            rows,
            rows,
            *threes,
            P(None, None, "mp"),
            P("mp", None),
            P(None, "mp"),
            P("mp", None),
        ),
        check_vma=False,
    )
```

```python
import math

import jax
import jax.numpy as jnp
from jax import lax
from jax.experimental import pallas as pl
from jax.experimental.pallas import tpu as pltpu
from jax.sharding import PartitionSpec as P

D = 256
FF = 2048
HD = 32
SEQ = 1024
WROW = 32
STEP = 5
LANES = 128
LOG2E = 1.4426950408889634
INTERPRET = False
BF = jnp.bfloat16
F32 = jnp.float32


def dot(a, b):
    return jnp.dot(a, b, preferred_element_type=F32)


def dot_nt(a, b):
    return lax.dot_general(a, b, (((1,), (1,)), ((), ())), preferred_element_type=F32)


def flip(x):
    if x.dtype == BF:
        return x.astype(F32).T.astype(BF)
    return x.T


def lane_of(shape):
    return lax.broadcasted_iota(jnp.int32, shape, 1)


def row_of(shape):
    return lax.broadcasted_iota(jnp.int32, shape, 0)


def place_rows(x, start, total):
    parts = []
    if start:
        parts.append(jnp.zeros((start, x.shape[1]), x.dtype))
    parts.append(x)
    if total - start - x.shape[0]:
        parts.append(jnp.zeros((total - start - x.shape[0], x.shape[1]), x.dtype))
    return jnp.concatenate(parts, axis=0) if len(parts) > 1 else x


def call(kernel, outs, *args, scratch=(), smem=0, flops=0):
    vm = pl.BlockSpec(memory_space=pltpu.VMEM)
    sm = pl.BlockSpec(memory_space=pltpu.SMEM)
    return pl.pallas_call(
        kernel,
        out_shape=[jax.ShapeDtypeStruct(s, d) for s, d in outs],
        in_specs=[sm] * smem + [vm] * (len(args) - smem),
        out_specs=[vm] * len(outs),
        scratch_shapes=[pltpu.VMEM(s, d) for s, d in scratch],
        cost_estimate=pl.CostEstimate(flops=flops, transcendentals=0, bytes_accessed=0)
        if flops
        else None,
        compiler_params=pltpu.CompilerParams(vmem_limit_bytes=24 * 2**20),
        interpret=INTERPRET,
    )(*args)


def prepare_kernel(shares, info, tokens, tokens_out, query_in, order, whole):
    seq, width = tokens.shape
    half = width // 2
    rows = seq // WROW
    shape = (max(rows, WROW), half)
    channel = lane_of(shape)
    exponent = (2 * (channel // 2)).astype(F32) / half
    angles = (row_of(shape) + 1).astype(F32) * jnp.exp(-math.log(10000.0) * exponent)
    table = jnp.where(channel % 2 == 0, jnp.sin(angles), jnp.cos(angles))
    for i in range(rows):
        lower = i * WROW
        spot = jnp.concatenate(
            [jnp.broadcast_to(table[i : i + 1], (WROW, half)), table[:WROW]], axis=1
        )
        part = tokens[lower : lower + WROW, :].astype(F32) + spot
        whole[lower : lower + WROW, :] = part.astype(BF)
    share = width // shares
    bits = shares.bit_length() - 1
    place = lane_of((width, width))
    slot = place // share
    source = jnp.zeros_like(slot)
    for k in range(bits):
        source = source + (((slot >> k) & 1) << (bits - 1 - k))
    source = (source ^ info[2]) * share + place % share
    order[...] = jnp.where(row_of((width, width)) == source, 1.0, 0.0).astype(BF)
    query_in[...] = dot(whole[...], order[...]).astype(BF)
    tokens_out[...] = dot(tokens[...], order[...]).astype(BF)


def stack(upper, lower):
    return jnp.concatenate([upper[...], lower[...]], axis=0)


def key_bias(length, start, count, lanes):
    place = row_of((count, lanes)) + start
    return jnp.where(place < length, 0.0, -1e30).astype(F32)


def attend_kernel(blocks, chunk, info, tokens, query_in, *refs):
    ins, outs, scores = refs[: 2 * blocks], refs[2 * blocks : -1], refs[-1]
    seq = tokens.shape[0]
    length, offset = info[0], info[1]
    fold = HD**-0.5 * LOG2E
    for b in range(blocks):
        block = stack(*ins[2 * b : 2 * b + 2])
        z, q_t, context_t, inverse, raised = outs[5 * b : 5 * b + 5]
        bw = block.shape[1]
        cl = bw // 4
        rows = q_t.shape[1]
        from_query = dot(query_in[...], block)
        from_token = dot(tokens[...], block)
        z[...] = jnp.where(lane_of((1, bw)) < 2 * cl, from_query, from_token).astype(BF)
        own = query_in[pl.ds(pl.multiple_of(offset, 8), rows), :]
        q_all = flip(dot(own, block).astype(BF))
        q_t[...] = q_all[:cl]
        z_t = flip(z[...])
        for h in range(cl // HD):
            lower = h * HD
            side = place_rows(q_all[lower : lower + HD], cl + lower, bw)
            peak = jnp.full((1, rows), -jnp.inf, F32)
            for c in range(0, seq, chunk):
                part = dot(z[c : c + chunk, :], side) * fold + key_bias(length, c, chunk, rows)
                scores[c : c + chunk, :] = part
                peak = jnp.maximum(peak, jnp.max(part, axis=0, keepdims=True))
            total = jnp.zeros((1, rows), F32)
            for c in range(0, seq, chunk):
                part = jnp.exp2(scores[c : c + chunk, :] - peak)
                total = total + jnp.sum(part, axis=0, keepdims=True)
                raised[h, c : c + chunk, :] = part.astype(BF)
            mixed = dot(z_t[2 * cl + lower : 2 * cl + lower + HD], raised[h])
            scale = 1.0 / total
            context_t[lower : lower + HD, :] = mixed * scale
            inverse[h : h + 1, :] = scale


def norm(x):
    average = jnp.mean(x, axis=-1, keepdims=True)
    centred = x - average
    scale = lax.rsqrt(jnp.mean(centred * centred, axis=-1, keepdims=True) + 1e-05)
    return centred * scale, scale


def norm_back(grad, unit, scale, gains):
    inner = grad * gains
    mean_one = jnp.mean(inner, axis=-1, keepdims=True)
    mean_two = jnp.mean(inner * unit, axis=-1, keepdims=True)
    back = scale * (inner - mean_one - unit * mean_two)
    gain_grad = jnp.sum(grad * unit, axis=0, keepdims=True)
    bias_grad = jnp.sum(grad, axis=0, keepdims=True)
    return back, gain_grad, bias_grad


def feed_kernel(blocks, info, tokens, cotangent, *refs):
    order, contexts, pairs = refs[0], refs[1 : blocks + 1], refs[blocks + 1 : 5 * blocks + 1]
    attention_pairs, feed_pairs = pairs[: 2 * blocks], pairs[2 * blocks :]
    layer_out, grad_one, *grads = refs[5 * blocks + 1 : 7 * blocks + 3]
    pre_all, hidden_all = refs[7 * blocks + 3 :]
    attention_blocks = [stack(*attention_pairs[2 * b : 2 * b + 2]) for b in range(blocks)]
    halves = [feed_pairs[2 * b : 2 * b + 2] for b in range(blocks)]
    rows, width = layer_out.shape
    length, offset = info[0], pl.multiple_of(info[1], 8)
    bw = attention_blocks[0].shape[1]
    cl = bw // 4
    fl = (feed_pairs[0].shape[1] - LANES) // 2
    half = width // 2
    first_blocks = [stack(up.at[:, :fl], low.at[:, :fl]) for up, low in halves]
    second_blocks = [stack(up.at[:, fl : 2 * fl], low.at[:, fl : 2 * fl]) for up, low in halves]
    own = tokens[pl.ds(offset, rows), :].astype(F32)
    attention = jnp.zeros((rows, width), F32)
    for b in range(blocks):
        context = flip(place_rows(contexts[b][...].astype(BF), 3 * cl, bw))
        attention = attention + dot_nt(context, attention_blocks[b])
    tail = [x[:, 2 * fl :].astype(F32) for x in halves[0]]
    pieces = jnp.concatenate(tail, axis=0).T
    gain_one, bias_one, gain_two, bias_two = (
        pieces[i : i + 1] + pieces[i + 4 : i + 5] for i in range(4)
    )
    unit_one, scale_one = norm(own + attention)
    first = unit_one * gain_one + bias_one
    first_low = first.astype(BF)
    feed = jnp.zeros((rows, width), F32)
    for b in range(blocks):
        pre = dot(first_low, first_blocks[b])
        inner = 0.7978845608 * (pre + 0.044715 * (pre * pre * pre))
        hidden = (0.5 * pre * (1.0 + jnp.tanh(inner))).astype(BF)
        pre_all[b] = pre
        hidden_all[b] = hidden
        feed = feed + dot_nt(hidden, second_blocks[b])
    unit_two, scale_two = norm(first + feed)
    layer_out[...] = dot_nt((unit_two * gain_two + bias_two).astype(BF), order[...]).astype(BF)
    live = (row_of((rows, width)) + offset) < length
    seed = jnp.where(live, dot(cotangent[pl.ds(offset, rows), :], order[...]), 0.0)
    grad_two, d_gain_two, d_bias_two = norm_back(seed, unit_two, scale_two, gain_two)
    grad_two_low = grad_two.astype(BF)
    grad_two_t = flip(grad_two_low)
    first_t = flip(first_low)
    grad_first = grad_two
    for b in range(blocks):
        grad_hidden = dot(grad_two_low, second_blocks[b])
        pre = pre_all[b]
        square = pre * pre
        bend = jnp.tanh(0.7978845608 * (pre + 0.044715 * (square * pre)))
        slope = 0.5 * (1.0 + bend) + (0.5 * pre) * (1.0 - bend * bend) * (
            0.7978845608 * (1.0 + 0.134145 * square)
        )
        grad_pre = (grad_hidden * slope).astype(BF)
        for side in range(2):
            part = slice(side * half, (side + 1) * half)
            out = grads[2 * b + side]
            out[:, :fl] = dot(first_t[part], grad_pre).astype(BF)
            out[:, fl : 2 * fl] = dot(grad_two_t[part], hidden_all[b]).astype(BF)
        grad_first = grad_first + dot_nt(grad_pre, first_blocks[b])
    back, d_gain_one, d_bias_one = norm_back(grad_first, unit_one, scale_one, gain_one)
    grad_one[...] = back
    stacked = jnp.concatenate(
        [d_gain_one, d_bias_one, d_gain_two, d_bias_two, jnp.zeros((LANES - 4, width), F32)], axis=0
    )
    columns = stacked.T.astype(BF)
    for b in range(blocks):
        grads[2 * b][:, 2 * fl :] = columns[:half]
        grads[2 * b + 1][:, 2 * fl :] = columns[half:]


def attend_back_kernel(blocks, chunk, info, tokens, query_in, grad_one, *refs):
    order, ins = refs[0], refs[1 : 7 * blocks + 1]
    rest = refs[7 * blocks + 1 :]
    earlier = rest[0] if len(rest) == blocks + 5 else None
    outs = rest[-blocks - 4 : -4]
    input_part, score_grads, sums, total = rest[-4:]
    seq, width = tokens.shape
    rows = grad_one.shape[0]
    offset = pl.multiple_of(info[1], 8)
    scaling = HD**-0.5
    grad_low = grad_one[...].astype(BF)
    grad_t = flip(grad_low)
    own_t = flip(query_in[pl.ds(offset, rows), :])
    query_in_t = flip(query_in[...])
    tokens_t = flip(tokens[...])
    own_total = grad_one[...] if earlier is None else jnp.zeros((rows, width), F32)
    for b in range(blocks):
        upper, lower_half, z, q_t, context_ref, inverse, raised = ins[7 * b : 7 * b + 7]
        block = stack(upper, lower_half)
        bw = block.shape[1]
        cl = bw // 4
        lane = lane_of((1, bw))
        context_t = context_ref[...]
        grad_context_t = dot(grad_low, block).T[3 * cl :]
        scaled = [
            (grad_context_t[h * HD : (h + 1) * HD] * inverse[h : h + 1, :]).astype(BF)
            for h in range(cl // HD)
        ]
        z_t = flip(z[...])
        q_side = flip(place_rows(q_t[...], cl, bw)).astype(F32)
        grad_side = flip(place_rows(jnp.concatenate(scaled, axis=0), 2 * cl, bw)).astype(F32)
        query_grads = []
        for h in range(cl // HD):
            lower = h * HD
            delta = jnp.sum(
                scaled[h].astype(F32) * context_t[lower : lower + HD], axis=0, keepdims=True
            )
            side_g = place_rows(scaled[h], 2 * cl + lower, bw)
            mask_q = (lane >= cl + lower) & (lane < cl + lower + HD)
            mask_g = (lane >= 2 * cl + lower) & (lane < 2 * cl + lower + HD)
            q_head = jnp.where(mask_q, q_side, 0.0).astype(BF)
            g_head = jnp.where(mask_g, grad_side, 0.0).astype(BF)
            for c in range(0, seq, chunk):
                weights = raised[h, c : c + chunk, :]
                slopes = weights.astype(F32) * (dot(z[c : c + chunk, :], side_g) - delta)
                slopes = slopes.astype(BF)
                score_grads[c : c + chunk, :] = slopes
                piece = dot(slopes, q_head) + dot(weights, g_head)
                if h:
                    piece = piece + sums[c : c + chunk, :]
                sums[c : c + chunk, :] = piece
            query_grads.append(
                (dot(z_t[cl + lower : cl + lower + HD], score_grads[...]) * scaling).astype(BF)
            )
        both = (sums[...] * jnp.where(lane < 2 * cl, scaling, 1.0)).astype(BF)
        query_grad = flip(place_rows(jnp.concatenate(query_grads, axis=0), 0, bw))
        context = flip(place_rows(context_t.astype(BF), 3 * cl, bw))
        of_query = dot(query_in_t, both)
        of_token = dot(tokens_t, both)
        weight_grad = dot(own_t, query_grad) + dot(grad_t, context)
        outs[b][...] = (weight_grad + jnp.where(lane < 2 * cl, of_query, of_token)).astype(BF)
        part = dot_nt(both, block)
        if b:
            part = part + total[...]
        elif earlier is not None:
            part = part + earlier[...]
        total[...] = part
        own_total = own_total + dot_nt(query_grad, block)
    total[pl.ds(offset, rows), :] += own_total
    if input_part.dtype == F32:
        input_part[...] = total[...]
    else:
        input_part[...] = dot_nt(total[...].astype(BF), order[...]).astype(BF)


def merge_kernel(*refs):
    *ins, keep, send = refs
    bw = ins[0].shape[1]
    rows = keep.shape[0]
    for i, out in enumerate((keep, send)):
        part = slice(i * rows, (i + 1) * rows)
        low, high = ([x[part, :].astype(F32) for x in group] for group in (ins[:2], ins[2:]))
        out[:, :bw] = (low[0] + low[1]).astype(BF)
        out[:, bw:] = sum(high[1:], high[0]).astype(BF)


def adamw(weight, moment_one, moment_two, grad, step_rate, decay_rate):
    mean_next = 0.5 * moment_one + 0.5 * grad
    square_next = 0.5 * moment_two + 0.5 * grad * grad
    correct = 1.0 - 0.5**STEP
    direction = mean_next / correct / (jnp.sqrt(square_next / correct) + 1e-08)
    weight_next = weight - step_rate * (direction + decay_rate * weight)
    return (weight_next, mean_next, square_next)


def update_kernel(rates, kept, came, *refs):
    ins, outs, pack = refs[:15], refs[15:30], refs[30]
    grad = kept[...].astype(F32) + came[...].astype(F32)
    cl = ins[0].shape[2]
    fl = ins[6].shape[1]
    fresh = []
    for i in range(3):
        fresh.append(
            adamw(*(ins[k][i] for k in range(3)), grad[:, i * cl : (i + 1) * cl], *rates[0])
        )
        for k in range(3):
            outs[k][i] = fresh[-1][k]
    start = 3 * cl
    for j, size in ((1, cl), (2, fl), (3, fl)):
        fresh.append(
            adamw(*(ins[3 * j + k][...] for k in range(3)), grad[:, start : start + size], *rates[j])
        )
        for k in range(3):
            outs[3 * j + k][...] = fresh[-1][k]
        start += size
    small = grad[:, start:].T[:4]
    for k, value in enumerate(adamw(*(ins[12 + k][...] for k in range(3)), small, *rates[4])):
        outs[12 + k][...] = value
    whole = jnp.concatenate([new[0].astype(BF) for new in fresh], axis=1)
    for i in range(pack.shape[0]):
        pack[i] = whole


def finish_kernel(copies, gathered, projector_t, combiner, expander, reducer, layer_out):
    layer_out[...] = gathered[...]
    cl = combiner.shape[0]
    fl = reducer.shape[0]
    for i in range(3):
        projector_t[i] = flip(copies[:, i * cl : (i + 1) * cl])
    combiner[...] = flip(copies[:, 3 * cl : 4 * cl])
    expander[...] = copies[:, 4 * cl : 4 * cl + fl]
    reducer[...] = flip(copies[:, 4 * cl + fl : 4 * cl + 2 * fl])


def body(
    tokens,
    cotangent,
    lengths,
    projector,
    projector_mean,
    projector_square,
    combiner,
    combiner_mean,
    combiner_square,
    expander,
    expander_mean,
    expander_square,
    reducer,
    reducer_mean,
    reducer_square,
    affines,
    affines_mean,
    affines_square,
):
    mp = lax.axis_size("mp")
    dp = lax.axis_size("dp")
    me = lax.axis_index("mp")
    seq = tokens.shape[0]
    if lengths.shape[0] != 1 or mp & (mp - 1):
        raise ValueError("unsupported mesh")
    rows = seq // mp
    dl = expander.shape[0]
    cl = projector.shape[2]
    fl = expander.shape[1]
    bw = 4 * cl
    heads = cl // HD
    chunk = 256
    spot = lax.axis_index("dp")
    info = jnp.stack([lengths[0], me.astype(jnp.int32) * rows, spot.astype(jnp.int32)])

    def swap(x, bit, axis="mp"):
        return lax.ppermute(x, axis, [(i, i ^ bit) for i in range(lax.axis_size(axis))])

    high = lax.reduce_precision(affines, 8, 7)
    tail = jnp.concatenate([high, affines - high], axis=0).T
    pack = jnp.concatenate(
        [
            *(projector[i] for i in range(3)),
            combiner.T,
            expander,
            reducer.T,
            jnp.pad(tail, ((0, 0), (0, LANES - 8))),
        ],
        axis=1,
    ).astype(BF)
    pack_width = pack.shape[1]
    names = list(range(mp))
    near, far = names[:2], names[2:]
    chip_bits = [1 << i for i in range(1, mp.bit_length() - 1)]
    down = chip_bits[::-1]
    line_bits = [1 << i for i in range(1, dp.bit_length() - 1)]
    tokens_in, query_in, order = call(
        lambda *refs: prepare_kernel(dp, *refs),
        [((seq, D), BF), ((seq, D), BF), ((D, D), BF)],
        info,
        tokens,
        scratch=[((seq, D), BF)],
        smem=1,
    )
    for bit in line_bits[::-1]:
        came = swap(pack, bit, "dp")
        if bit == line_bits[-1]:
            came, order = lax.optimization_barrier((came, order))
        pack = jnp.concatenate([pack, came], axis=0)

    def cross(part):
        halves = {0: part}
        for bit in chip_bits:
            for r in list(halves):
                halves[r ^ bit] = swap(halves[r], bit)
        return halves

    def pair(blocks, group):
        for r in group:
            blocks[r ^ 1] = [swap(x, 1) for x in blocks[r]]

    attention_half, feed_half = pack[:, :bw], pack[:, bw:]
    upper = cross(attention_half)
    attention_blocks = {r: [x, swap(x, 1, "dp")] for r, x in upper.items()}
    feed_upper = cross(feed_half)
    feed_other, attention_blocks[0][1], attention_blocks[2][0] = lax.optimization_barrier(
        (swap(feed_half, 1, "dp"), attention_blocks[0][1], attention_blocks[2][0])
    )
    feed_lower = cross(feed_other)
    feed_blocks = {r: [feed_upper[r], feed_lower[r]] for r in feed_upper}
    pair(attention_blocks, names[:1])
    pair(feed_blocks, names[:1])

    def attend(group):
        made = call(
            lambda *refs: attend_kernel(len(group), chunk, *refs),
            [
                ((seq, bw), BF),
                ((cl, rows), BF),
                ((cl, rows), F32),
                ((heads, rows), F32),
                ((heads, seq, rows), BF),
            ]
            * len(group),
            info,
            tokens_in,
            query_in,
            *(x for r in group for x in attention_blocks[r]),
            scratch=[((seq, rows), F32)],
            smem=1,
            flops=4 * len(group) * (heads + 1) * seq * rows * D,
        )
        return {r: list(made[5 * i : 5 * i + 5]) for i, r in enumerate(group)}

    kept = attend(near)
    for blocks in (attention_blocks, feed_blocks):
        for r in far[::2]:
            *blocks[r], kept[0][2] = lax.optimization_barrier((*blocks[r], kept[0][2]))
        pair(blocks, far[::2])
    kept.update(attend(far))
    own_out, grad_one, *feed_grads = call(
        lambda *refs: feed_kernel(mp, *refs),
        [((rows, D), BF), ((rows, D), F32)]
        + [((D // 2, 2 * fl + LANES), BF)] * (2 * mp),
        info,
        tokens_in,
        cotangent,
        order,
        *(kept[r][2] for r in names),
        *(x for r in names for x in attention_blocks[r]),
        *(x for r in names for x in feed_blocks[r]),
        scratch=[((mp, rows, fl), F32), ((mp, rows, fl), BF)],
        smem=1,
        flops=12 * mp * rows * D * fl,
    )

    def attend_back(group, earlier, dtype):
        return call(
            lambda *refs: attend_back_kernel(len(group), chunk, *refs),
            [((D, bw), BF)] * len(group) + [((seq, D), dtype)],
            info,
            tokens_in,
            query_in,
            grad_one,
            order,
            *(x for r in group for x in (*attention_blocks[r], *kept[r])),
            *earlier,
            scratch=[((seq, rows), BF), ((seq, bw), F32), ((seq, D), F32)],
            smem=1,
            flops=8 * len(group) * (heads + 1) * seq * rows * D,
        )

    def reduce_blocks(left, order):
        left = dict(left)
        for bit in order:
            for r in sorted({r & ~bit for r in left if r & bit}):
                came = swap(left.pop(r ^ bit), bit)
                left[r] = left[r] + came if r in left else came
        return left

    down = chip_bits[::-1]
    own_side, other_side = (
        reduce_blocks(zip(names, feed_grads[i::2], strict=True), [1]) for i in range(2)
    )
    own_side, other_side, grad_one = lax.optimization_barrier((own_side, other_side, grad_one))
    other_side = reduce_blocks(other_side, down)[0]
    own_side = reduce_blocks(own_side, down[:-1])
    came = [swap(own_side[r], r) for r in down[-1:]]
    *far_grads, far_part = attend_back(far, (), F32)
    far_grads = reduce_blocks(zip(far, far_grads, strict=True), [1])
    far_grads, far_part = lax.optimization_barrier((far_grads, far_part))
    far_grads = reduce_blocks(far_grads, down)[0]
    [side_grad, near_part] = attend_back(near[1:], (far_part,), F32)
    other_side, near_part = lax.optimization_barrier((other_side, near_part))
    came.insert(0, swap(other_side, 1, "dp"))
    [own_grad, input_part] = attend_back(near[:1], (near_part,), BF)
    near_grads = own_grad + swap(side_grad, 1) + far_grads
    half = D // 2
    keep, send = call(
        merge_kernel,
        [((half // 2, pack_width), BF)] * 2,
        near_grads[:half],
        swap(near_grads[half:], 1, "dp"),
        own_side[0],
        *came,
    )
    for bit in line_bits:
        arrived = swap(send, bit, "dp")
        if bit != line_bits[-1]:
            summed = keep + arrived
            half = summed.shape[0] // 2
            keep, send = summed[:half], summed[half:]
    bits = [*chip_bits, 1]
    masters = (
        (projector, projector_mean, projector_square),
        (combiner.T, combiner_mean.T, combiner_square.T),
        (expander, expander_mean, expander_square),
        (reducer.T, reducer_mean.T, reducer_square.T),
        (affines, affines_mean, affines_square),
    )
    rates = (
        (D ** (-0.5), 0.0001),
        (max(1, D * 8 // SEQ) ** (-0.5), 0.0001),
        (D ** (-0.5), 0.0001),
        (FF ** (-0.5), 0.0001),
        (0.4, 0.0),
    )
    flat = [x for three in masters for x in three]
    *fresh, new_pack = call(
        lambda *refs: update_kernel(rates, *refs),
        [(x.shape, F32) for x in flat] + [((dp, dl, bw + 2 * fl), BF)],
        keep,
        arrived,
        *flat,
    )
    new_low = lax.all_to_all(new_pack, "dp", 0, 0, tiled=True).reshape(D, bw + 2 * fl)
    projector_copy, combiner_copy, expander_copy, reducer_copy, layer_out = call(
        finish_kernel,
        [((3, cl, D), BF), ((cl, D), BF), ((D, fl), BF), ((fl, D), BF), ((seq, D), BF)],
        new_low,
        lax.all_gather(own_out, "mp", axis=0, tiled=True),
    )
    for i in (3, 4, 5, 9, 10, 11):
        fresh[i] = fresh[i].T
    for bit in bits:
        input_part = input_part + swap(input_part, bit)
    return (
        layer_out,
        input_part.astype(F32),
        *fresh,
        jnp.swapaxes(projector_copy, 1, 2),
        combiner_copy,
        expander_copy,
        reducer_copy,
    )


def solution(mesh):
    rows = P("dp", None)
    by_weight = [P(None, "dp", "mp"), P("mp", "dp"), P("dp", "mp"), P("mp", "dp"), P(None, "dp")]
    threes = [spec for spec in by_weight for _ in range(3)]
    return jax.shard_map(
        body,
        mesh=mesh,
        in_specs=(rows, rows, P("dp"), *threes),
        out_specs=(
            rows,
            rows,
            *threes,
            P(None, None, "mp"),
            P("mp", None),
            P(None, "mp"),
            P("mp", None),
        ),
        check_vma=False,
    )
```

```python
import math

import jax
import jax.numpy as jnp
from jax import lax
from jax.experimental import pallas as pl
from jax.experimental.pallas import tpu as pltpu
from jax.sharding import PartitionSpec as P

D = 256
FF = 2048
HD = 32
SEQ = 1024
WROW = 32
STEP = 5
LANES = 128
LOG2E = 1.4426950408889634
INTERPRET = False
BF = jnp.bfloat16
F32 = jnp.float32


def dot(a, b):
    return jnp.dot(a, b, preferred_element_type=F32)


def dot_nt(a, b):
    return lax.dot_general(a, b, (((1,), (1,)), ((), ())), preferred_element_type=F32)


def flip(x):
    return x.T


def lane_of(shape):
    return lax.broadcasted_iota(jnp.int32, shape, 1)


def row_of(shape):
    return lax.broadcasted_iota(jnp.int32, shape, 0)


def place_rows(x, start, total):
    parts = []
    if start:
        parts.append(jnp.zeros((start, x.shape[1]), x.dtype))
    parts.append(x)
    if total - start - x.shape[0]:
        parts.append(jnp.zeros((total - start - x.shape[0], x.shape[1]), x.dtype))
    return jnp.concatenate(parts, axis=0) if len(parts) > 1 else x


def call(kernel, outs, *args, scratch=(), smem=0, flops=0):
    vm = pl.BlockSpec(memory_space=pltpu.VMEM)
    sm = pl.BlockSpec(memory_space=pltpu.SMEM)
    return pl.pallas_call(
        kernel,
        out_shape=[jax.ShapeDtypeStruct(s, d) for s, d in outs],
        in_specs=[sm] * smem + [vm] * (len(args) - smem),
        out_specs=[vm] * len(outs),
        scratch_shapes=[pltpu.VMEM(s, d) for s, d in scratch],
        cost_estimate=pl.CostEstimate(flops=flops, transcendentals=0, bytes_accessed=0)
        if flops
        else None,
        compiler_params=pltpu.CompilerParams(vmem_limit_bytes=24 * 2**20),
        interpret=INTERPRET,
    )(*args)


def pack_kernel(*refs):
    given, pack, held, arrived = refs[:5], refs[5], refs[6:11], refs[11]
    fetches = [
        pltpu.make_async_copy(source, target, arrived.at[i])
        for i, (source, target) in enumerate(zip(given, held, strict=True))
    ]
    for fetch in fetches:
        fetch.start()
    projector, combiner_t, expander, reducer_t, affines = held
    dl, fl = expander.shape
    cl = combiner_t.shape[1]
    for fetch in fetches:
        fetch.wait()
    gains = jnp.concatenate([affines[...], jnp.zeros((LANES - 4, dl), F32)], axis=0).T
    high = gains.astype(BF).astype(F32)
    rest = pltpu.roll(gains - high, 4, 1)
    tail = jnp.where(lane_of(high.shape) < 4, high, rest).astype(BF)
    low = [projector[i].astype(BF) for i in range(3)] + [combiner_t[...].astype(BF)]
    pack[:, : 4 * cl] = jnp.concatenate(low, axis=1)
    pack[:, 4 * cl : 4 * cl + fl] = expander[...].astype(BF)
    pack[:, 4 * cl + fl : 4 * cl + 2 * fl] = reducer_t[...].astype(BF)
    pack[:, 4 * cl + 2 * fl :] = tail


def prepare_kernel(shares, info, tokens, tokens_out, query_in, tokens_t, query_t, order, whole):
    seq, width = tokens.shape
    half = width // 2
    rows = seq // WROW
    shape = (max(rows, WROW), half)
    channel = lane_of(shape)
    exponent = (2 * (channel // 2)).astype(F32) / half
    angles = (row_of(shape) + 1).astype(F32) * jnp.exp(-math.log(10000.0) * exponent)
    table = jnp.where(channel % 2 == 0, jnp.sin(angles), jnp.cos(angles))
    for i in range(rows):
        lower = i * WROW
        spot = jnp.concatenate(
            [jnp.broadcast_to(table[i : i + 1], (WROW, half)), table[:WROW]], axis=1
        )
        part = tokens[lower : lower + WROW, :].astype(F32) + spot
        whole[lower : lower + WROW, :] = part.astype(BF)
    share = width // shares
    bits = shares.bit_length() - 1
    place = lane_of((width, width))
    slot = place // share
    source = jnp.zeros_like(slot)
    for k in range(bits):
        source = source + (((slot >> k) & 1) << (bits - 1 - k))
    source = (source ^ info[2]) * share + place % share
    order[...] = jnp.where(row_of((width, width)) == source, 1.0, 0.0).astype(BF)
    for source_ref, out, out_t in ((whole, query_in, query_t), (tokens, tokens_out, tokens_t)):
        moved = dot(source_ref[...], order[...]).astype(BF)
        out[...] = moved
        out_t[...] = flip(moved)


def stack(upper, lower):
    return jnp.concatenate([upper[...], lower[...]], axis=0)


def attend_kernel(blocks, chunk, info, tokens, query_in, *refs):
    ins, outs, scores = refs[: 2 * blocks], refs[2 * blocks : -1], refs[-1]
    seq = tokens.shape[0]
    length, offset = info[0], info[1]
    fold = HD**-0.5 * LOG2E
    whole = [stack(*ins[2 * b : 2 * b + 2]) for b in range(blocks)]
    bw = whole[0].shape[1]
    cl = bw // 4
    mid = 2 * cl
    from_query = dot(query_in[...], jnp.concatenate([x[:, :mid] for x in whole], axis=1))
    from_token = dot(tokens[...], jnp.concatenate([x[:, mid:] for x in whole], axis=1))
    dead = jnp.where(row_of((seq, 1)) < length, 0.0, 1.0)
    for b in range(blocks):
        block = whole[b]
        z, z_t, q_t, context_t, inverse, raised = outs[6 * b : 6 * b + 6]
        rows = q_t.shape[1]
        left = from_query[:, b * mid : (b + 1) * mid]
        z[:, :mid] = jnp.where(lane_of((1, mid)) == 0, dead, left).astype(BF)
        z[:, mid:] = from_token[:, b * mid : (b + 1) * mid].astype(BF)
        own = query_in[pl.ds(pl.multiple_of(offset, 8), rows), :]
        q_all = flip(dot(own, block).astype(BF))
        q_t[...] = q_all[:cl]
        z_t[...] = flip(z[...])
        for h in range(cl // HD):
            lower = h * HD
            side = place_rows(q_all[lower : lower + HD], cl + lower, bw)
            side = jnp.where(row_of(side.shape) == 0, -1e30, side.astype(F32)).astype(BF)
            peak = jnp.full((1, rows), -jnp.inf, F32)
            for c in range(0, seq, chunk):
                part = dot(z[c : c + chunk, :], side)
                scores[c : c + chunk, :] = part
                peak = jnp.maximum(peak, jnp.max(part, axis=0, keepdims=True))
            total = jnp.zeros((1, rows), F32)
            for c in range(0, seq, chunk):
                part = jnp.exp2((scores[c : c + chunk, :] - peak) * fold)
                total = total + jnp.sum(part, axis=0, keepdims=True)
                raised[h, c : c + chunk, :] = part.astype(BF)
            mixed = dot(z_t[2 * cl + lower : 2 * cl + lower + HD, :], raised[h])
            scale = 1.0 / total
            context_t[lower : lower + HD, :] = mixed * scale
            inverse[h : h + 1, :] = scale


def norm(x):
    average = jnp.mean(x, axis=-1, keepdims=True)
    centred = x - average
    scale = lax.rsqrt(jnp.mean(centred * centred, axis=-1, keepdims=True) + 1e-05)
    return centred * scale, scale


def norm_back(grad, unit, scale, gains):
    inner = grad * gains
    mean_one = jnp.mean(inner, axis=-1, keepdims=True)
    mean_two = jnp.mean(inner * unit, axis=-1, keepdims=True)
    back = scale * (inner - mean_one - unit * mean_two)
    gain_grad = jnp.sum(grad * unit, axis=0, keepdims=True)
    bias_grad = jnp.sum(grad, axis=0, keepdims=True)
    return back, gain_grad, bias_grad


def feed_kernel(blocks, info, tokens, cotangent, *refs):
    order, contexts, pairs = refs[0], refs[1 : blocks + 1], refs[blocks + 1 : 5 * blocks + 1]
    attention_pairs, feed_pairs = pairs[: 2 * blocks], pairs[2 * blocks :]
    layer_out, grad_one, *grads = refs[5 * blocks + 1 : 7 * blocks + 3]
    slopes, hidden_all = refs[7 * blocks + 3 :]
    attention_blocks = [stack(*attention_pairs[2 * b : 2 * b + 2]) for b in range(blocks)]
    halves = [feed_pairs[2 * b : 2 * b + 2] for b in range(blocks)]
    rows, width = layer_out.shape
    length, offset = info[0], pl.multiple_of(info[1], 8)
    bw = attention_blocks[0].shape[1]
    cl = bw // 4
    fl = (feed_pairs[0].shape[1] - LANES) // 2
    half = width // 2
    first_blocks = [stack(up.at[:, :fl], low.at[:, :fl]) for up, low in halves]
    second_blocks = [stack(up.at[:, fl : 2 * fl], low.at[:, fl : 2 * fl]) for up, low in halves]
    own = tokens[pl.ds(offset, rows), :].astype(F32)
    attention = jnp.zeros((rows, width), F32)
    for b in range(blocks):
        context = flip(place_rows(contexts[b][...].astype(BF), 3 * cl, bw))
        attention = attention + dot_nt(context, attention_blocks[b])
    tail = [x[:, 2 * fl :].astype(F32) for x in halves[0]]
    pieces = jnp.concatenate(tail, axis=0).T
    gain_one, bias_one, gain_two, bias_two = (
        pieces[i : i + 1] + pieces[i + 4 : i + 5] for i in range(4)
    )
    unit_one, scale_one = norm(own + attention)
    first = unit_one * gain_one + bias_one
    first_low = first.astype(BF)
    feed = jnp.zeros((rows, width), F32)
    for b in range(blocks):
        pre = dot(first_low, first_blocks[b])
        square = pre * pre
        half_pre = 0.5 * pre
        bend = jnp.tanh(pre * (0.7978845608 + 0.035677408 * square))
        hidden = (half_pre + half_pre * bend).astype(BF)
        steep = 0.7978845608 + 0.107032224 * square
        slopes[b] = (0.5 + 0.5 * bend) + half_pre * (1.0 - bend * bend) * steep
        hidden_all[b] = hidden
        feed = feed + dot_nt(hidden, second_blocks[b])
    unit_two, scale_two = norm(first + feed)
    layer_out[...] = dot_nt((unit_two * gain_two + bias_two).astype(BF), order[...]).astype(BF)
    live = (row_of((rows, width)) + offset) < length
    seed = jnp.where(live, dot(cotangent[pl.ds(offset, rows), :], order[...]), 0.0)
    grad_two, d_gain_two, d_bias_two = norm_back(seed, unit_two, scale_two, gain_two)
    grad_two_low = grad_two.astype(BF)
    grad_two_t = flip(grad_two_low)
    first_t = flip(first_low)
    grad_first = grad_two
    for b in range(blocks):
        grad_hidden = dot(grad_two_low, second_blocks[b])
        grad_pre = (grad_hidden * slopes[b]).astype(BF)
        for side in range(2):
            part = slice(side * half, (side + 1) * half)
            out = grads[2 * b + side]
            out[:, :fl] = dot(first_t[part], grad_pre).astype(BF)
            out[:, fl : 2 * fl] = dot(grad_two_t[part], hidden_all[b]).astype(BF)
        grad_first = grad_first + dot_nt(grad_pre, first_blocks[b])
    back, d_gain_one, d_bias_one = norm_back(grad_first, unit_one, scale_one, gain_one)
    grad_one[...] = back
    stacked = jnp.concatenate(
        [d_gain_one, d_bias_one, d_gain_two, d_bias_two, jnp.zeros((LANES - 4, width), F32)], axis=0
    )
    columns = stacked.T.astype(BF)
    for b in range(blocks):
        grads[2 * b][:, 2 * fl :] = columns[:half]
        grads[2 * b + 1][:, 2 * fl :] = columns[half:]


def attend_back_kernel(blocks, chunk, first, last, info, query_in, tokens_t, query_t, grad_one, *refs):
    made = blocks + 4 + last
    order, ins = refs[0], refs[1 : 8 * blocks + 1]
    rest = refs[8 * blocks + 1 :]
    earlier = None if first else rest[0]
    seq, width = query_in.shape
    score_grads, sums, total = rest[-3:]
    outs = rest[len(rest) - made : -3]
    rows = grad_one.shape[0]
    offset = pl.multiple_of(info[1], 8)
    scaling = HD**-0.5
    grad_low = grad_one[...].astype(BF)
    grad_t = flip(grad_low)
    own_t = flip(query_in[pl.ds(offset, rows), :])
    own_total = grad_one[...] if earlier is None else jnp.zeros((rows, width), F32)
    for b in range(blocks):
        upper, lower_half, z, z_t, q_t, context_ref, inverse, raised = ins[8 * b : 8 * b + 8]
        block = stack(upper, lower_half)
        bw = block.shape[1]
        cl = bw // 4
        lane = lane_of((1, bw))
        context_t = context_ref[...]
        grad_context_t = dot(grad_low, block).T[3 * cl :]
        scaled = [
            (grad_context_t[h * HD : (h + 1) * HD] * inverse[h : h + 1, :]).astype(BF)
            for h in range(cl // HD)
        ]
        q_side = flip(place_rows(q_t[...], cl, bw)).astype(F32)
        grad_side = flip(place_rows(jnp.concatenate(scaled, axis=0), 2 * cl, bw)).astype(F32)
        heads = range(cl // HD)
        sides, deltas, right = [], [], []
        for h in heads:
            lower = h * HD
            deltas.append(
                jnp.sum(
                    scaled[h].astype(F32) * context_t[lower : lower + HD], axis=0, keepdims=True
                )
            )
            sides.append(place_rows(scaled[h], 2 * cl + lower, bw))
            for start, side in ((cl, q_side), (2 * cl, grad_side)):
                mask = (lane >= start + lower) & (lane < start + lower + HD)
                right.append(jnp.where(mask, side, 0.0).astype(BF))
        right = jnp.concatenate(right, axis=0)
        for c in range(0, seq, chunk):
            keys = z[c : c + chunk, :]
            left = []
            for h in heads:
                weights = raised[h, c : c + chunk, :]
                slopes = (weights.astype(F32) * (dot(keys, sides[h]) - deltas[h])).astype(BF)
                score_grads[h, c : c + chunk, :] = slopes
                left += [slopes, weights]
            sums[c : c + chunk, :] = dot(jnp.concatenate(left, axis=1), right)
        query_grads = [
            (dot(z_t[cl + h * HD : cl + (h + 1) * HD, :], score_grads[h]) * scaling).astype(BF)
            for h in heads
        ]
        both = (sums[...] * jnp.where(lane < 2 * cl, scaling, 1.0)).astype(BF)
        query_grad = flip(place_rows(jnp.concatenate(query_grads, axis=0), 0, bw))
        context = flip(place_rows(context_t.astype(BF), 3 * cl, bw))
        of_query = dot(query_t[...], both)
        of_token = dot(tokens_t[...], both)
        weight_grad = dot(own_t, query_grad) + dot(grad_t, context)
        outs[b][...] = (weight_grad + jnp.where(lane < 2 * cl, of_query, of_token)).astype(BF)
        part = dot_nt(both, block)
        if b:
            part = part + total[...]
        elif earlier is not None:
            part = part + earlier[...]
        total[...] = part
        own_total = own_total + dot_nt(query_grad, block)
    total[pl.ds(offset, rows), :] += own_total
    if not last:
        outs[-1][...] = total[...]
        return
    total[...] = dot_nt(total[...].astype(BF), order[...])
    half = seq // 2
    for out, core in zip(outs[-2:], (info[3], 1 - info[3]), strict=True):
        out[...] = total[pl.ds(pl.multiple_of(core * half, 8), half), :].astype(BF)


def merge_kernel(*refs):
    *ins, keep, send = refs
    bw = ins[0].shape[1]
    rows = keep.shape[0]
    for i, out in enumerate((keep, send)):
        part = slice(i * rows, (i + 1) * rows)
        low, high = ([x[part, :].astype(F32) for x in group] for group in (ins[:2], ins[2:]))
        out[:, :bw] = (low[0] + low[1]).astype(BF)
        out[:, bw:] = sum(high[1:], high[0]).astype(BF)


def adamw(weight, moment_one, moment_two, grad, step_rate, decay_rate):
    mean_next = 0.5 * moment_one + 0.5 * grad
    square_next = 0.5 * moment_two + 0.5 * grad * grad
    correct = 1.0 - 0.5**STEP
    direction = mean_next / correct / (jnp.sqrt(square_next / correct) + 1e-08)
    weight_next = weight - step_rate * (direction + decay_rate * weight)
    return (weight_next, mean_next, square_next)


def update_kernel(rates, kept, came, *refs):
    ins, outs, pack = refs[:13], refs[13:26], refs[26]
    grad = kept[...].astype(F32) + came[...].astype(F32)
    cl = ins[0].shape[2]
    fl = ins[6].shape[1]
    fresh = []
    for i in range(3):
        fresh.append(
            adamw(*(ins[k][i] for k in range(3)), grad[:, i * cl : (i + 1) * cl], *rates[0])
        )
        for k in range(3):
            outs[k][i] = fresh[-1][k]
    start = 3 * cl
    for j, size in ((1, cl), (2, fl), (3, fl)):
        fresh.append(
            adamw(*(ins[3 * j + k][...] for k in range(3)), grad[:, start : start + size], *rates[j])
        )
        for k in range(3):
            outs[3 * j + k][...] = fresh[-1][k]
        start += size
    small = grad[:, start:].T[:4]
    for k, value in enumerate(adamw(*(ins[12][k] for k in range(3)), small, *rates[4])):
        outs[12][k] = value
    whole = jnp.concatenate([new[0].astype(BF) for new in fresh], axis=1)
    for i in range(pack.shape[0]):
        pack[i] = whole


def assemble_kernel(info, mine, other, *refs):
    *pieces, input_grad, layer_out = refs
    half = mine.shape[0]
    for part, core in ((mine, info[3]), (other, 1 - info[3])):
        input_grad[pl.ds(pl.multiple_of(core * half, 8), half), :] = part[...].astype(F32)
    rows = pieces[0].shape[0]
    for r, piece in enumerate(pieces):
        layer_out[pl.ds(pl.multiple_of((info[4] ^ r) * rows, 16), rows), :] = piece[...]


def finish_kernel(copies, projector_t, combiner, expander, reducer):
    cl = combiner.shape[0]
    fl = reducer.shape[0]
    for i in range(3):
        projector_t[i] = flip(copies[:, i * cl : (i + 1) * cl])
    combiner[...] = flip(copies[:, 3 * cl : 4 * cl])
    expander[...] = copies[:, 4 * cl : 4 * cl + fl]
    reducer[...] = flip(copies[:, 4 * cl + fl : 4 * cl + 2 * fl])


def body(
    tokens,
    cotangent,
    lengths,
    projector,
    projector_mean,
    projector_square,
    combiner,
    combiner_mean,
    combiner_square,
    expander,
    expander_mean,
    expander_square,
    reducer,
    reducer_mean,
    reducer_square,
    affines,
    affines_mean,
    affines_square,
):
    mp = lax.axis_size("mp")
    dp = lax.axis_size("dp")
    me = lax.axis_index("mp")
    seq = tokens.shape[0]
    if lengths.shape[0] != 1 or mp & (mp - 1):
        raise ValueError("unsupported mesh")
    rows = seq // mp
    dl = expander.shape[0]
    cl = projector.shape[2]
    fl = expander.shape[1]
    bw = 4 * cl
    heads = cl // HD
    chunk = 256
    spot = lax.axis_index("dp")
    me, spot = me.astype(jnp.int32), spot.astype(jnp.int32)
    info = jnp.stack([lengths[0], me * rows, spot, me & 1, me])

    def swap(x, bit, axis="mp"):
        return lax.ppermute(x, axis, [(i, i ^ bit) for i in range(lax.axis_size(axis))])

    pack_width = bw + 2 * fl + LANES
    shares = [projector, combiner.T, expander, reducer.T, affines]
    [pack] = pl.pallas_call(
        pack_kernel,
        out_shape=[jax.ShapeDtypeStruct((dl, pack_width), BF)],
        in_specs=[pl.BlockSpec(memory_space=pltpu.HBM)] * len(shares),
        out_specs=[pl.BlockSpec(memory_space=pltpu.VMEM)],
        scratch_shapes=[
            *(pltpu.VMEM(x.shape, x.dtype) for x in shares),
            pltpu.SemaphoreType.DMA((len(shares),)),
        ],
        interpret=INTERPRET,
    )(*(pltpu.with_memory_space_constraint(x, pltpu.HBM) for x in shares))
    names = list(range(mp))
    near, far = names[:2], names[2:]
    chip_bits = [1 << i for i in range(1, mp.bit_length() - 1)]
    down = chip_bits[::-1]
    line_bits = [1 << i for i in range(1, dp.bit_length() - 1)]
    tokens_in, query_in, tokens_t, query_t, order = call(
        lambda *refs: prepare_kernel(dp, *refs),
        [((seq, D), BF)] * 2 + [((D, seq), BF)] * 2 + [((D, D), BF)],
        info,
        tokens,
        scratch=[((seq, D), BF)],
        smem=1,
    )
    small = jnp.stack([affines, affines_mean, affines_square])
    for bit in line_bits[::-1]:
        came = swap(pack, bit, "dp")
        if bit == line_bits[-1]:
            came, order, small = lax.optimization_barrier((came, order, small))
        pack = jnp.concatenate([pack, came], axis=0)

    def cross(part):
        halves = {0: part}
        for bit in chip_bits:
            for r in list(halves):
                halves[r ^ bit] = swap(halves[r], bit)
        return halves

    def pair(blocks, group):
        for r in group:
            blocks[r ^ 1] = [swap(x, 1) for x in blocks[r]]

    attention_half, feed_half = pack[:, :bw], pack[:, bw:]
    upper = cross(attention_half)
    attention_blocks = {r: [x, swap(x, 1, "dp")] for r, x in upper.items()}
    feed_upper = cross(feed_half)
    feed_other, attention_blocks[0][1], attention_blocks[2][0] = lax.optimization_barrier(
        (swap(feed_half, 1, "dp"), attention_blocks[0][1], attention_blocks[2][0])
    )
    feed_lower = cross(feed_other)
    feed_blocks = {r: [feed_upper[r], feed_lower[r]] for r in feed_upper}
    pair(attention_blocks, names[:1])
    pair(feed_blocks, names[:1])

    def attend(group):
        made = call(
            lambda *refs: attend_kernel(len(group), chunk, *refs),
            [
                ((seq, bw), BF),
                ((bw, seq), BF),
                ((cl, rows), BF),
                ((cl, rows), F32),
                ((heads, rows), F32),
                ((heads, seq, rows), BF),
            ]
            * len(group),
            info,
            tokens_in,
            query_in,
            *(x for r in group for x in attention_blocks[r]),
            scratch=[((seq, rows), F32)],
            smem=1,
            flops=4 * len(group) * (heads + 1) * seq * rows * D,
        )
        return {r: list(made[6 * i : 6 * i + 6]) for i, r in enumerate(group)}

    kept = attend(near)
    for r in far[::2]:
        attention_blocks[r][1], kept[0][3] = lax.optimization_barrier(
            (attention_blocks[r][1], kept[0][3])
        )
    pair(attention_blocks, far[::2])
    for r in far[::2]:
        feed_blocks[r], attention_blocks[r ^ 1] = lax.optimization_barrier(
            (feed_blocks[r], attention_blocks[r ^ 1])
        )
    pair(feed_blocks, far[::2])
    kept.update(attend(far))
    own_out, grad_one, *feed_grads = call(
        lambda *refs: feed_kernel(mp, *refs),
        [((rows, D), BF), ((rows, D), F32)]
        + [((D // 2, 2 * fl + LANES), BF)] * (2 * mp),
        info,
        tokens_in,
        cotangent,
        order,
        *(kept[r][3] for r in names),
        *(x for r in names for x in attention_blocks[r]),
        *(x for r in names for x in feed_blocks[r]),
        scratch=[((mp, rows, fl), F32), ((mp, rows, fl), BF)],
        smem=1,
        flops=12 * mp * rows * D * fl,
    )

    def attend_back(group, earlier=(), last=False):
        return call(
            lambda *refs: attend_back_kernel(len(group), chunk, not earlier, last, *refs),
            [((D, bw), BF)] * len(group)
            + ([((seq // 2, D), BF)] * 2 if last else [((seq, D), F32)]),
            info,
            query_in,
            tokens_t,
            query_t,
            grad_one,
            order,
            *(x for r in group for x in (*attention_blocks[r], *kept[r])),
            *earlier,
            scratch=[((heads, seq, rows), BF), ((seq, bw), F32), ((seq, D), F32)],
            smem=1,
            flops=8 * len(group) * (heads + 1) * seq * rows * D,
        )

    def reduce_blocks(left, order):
        left = dict(left)
        for bit in order:
            for r in sorted({r & ~bit for r in left if r & bit}):
                came = swap(left.pop(r ^ bit), bit)
                left[r] = left[r] + came if r in left else came
        return left

    down = chip_bits[::-1]
    own_side, other_side = (
        reduce_blocks(zip(names, feed_grads[i::2], strict=True), [1]) for i in range(2)
    )
    other_side, grad_one = lax.optimization_barrier((other_side, grad_one))
    other_side = reduce_blocks(other_side, down)[0]
    *far_grads, far_part = attend_back(far)
    far_grads = reduce_blocks(zip(far, far_grads, strict=True), [1])
    far_grads, far_part = lax.optimization_barrier((far_grads, far_part))
    far_grads = reduce_blocks(far_grads, down)[0]
    [side_grad, near_part] = attend_back(near[1:], (far_part,))
    other_side, own_side, far_grads, near_part = lax.optimization_barrier(
        (other_side, own_side, far_grads, near_part)
    )
    own_side = reduce_blocks(own_side, down[:-1])
    came = [swap(other_side, 1, "dp"), *(swap(own_side[r], r) for r in down[-1:])]
    [own_grad, mine, theirs] = attend_back(near[:1], (near_part,), last=True)
    near_grads = own_grad + swap(side_grad, 1) + far_grads
    half = D // 2
    keep, send = call(
        merge_kernel,
        [((half // 2, pack_width), BF)] * 2,
        near_grads[:half],
        swap(near_grads[half:], 1, "dp"),
        own_side[0],
        *came,
    )
    for bit in line_bits:
        arrived = swap(send, bit, "dp")
        if bit != line_bits[-1]:
            summed = keep + arrived
            half = summed.shape[0] // 2
            keep, send = summed[:half], summed[half:]
    masters = (
        (projector, projector_mean, projector_square),
        (combiner.T, combiner_mean.T, combiner_square.T),
        (expander, expander_mean, expander_square),
        (reducer.T, reducer_mean.T, reducer_square.T),
    )
    rates = (
        (D ** (-0.5), 0.0001),
        (max(1, D * 8 // SEQ) ** (-0.5), 0.0001),
        (D ** (-0.5), 0.0001),
        (FF ** (-0.5), 0.0001),
        (0.4, 0.0),
    )
    flat = [x for three in masters for x in three]
    *fresh, fresh_small, new_pack = call(
        lambda *refs: update_kernel(rates, *refs),
        [(x.shape, F32) for x in (*flat, small)] + [((dp, dl, bw + 2 * fl), BF)],
        keep,
        arrived,
        *flat,
        small,
    )
    new_low = lax.all_to_all(new_pack, "dp", 0, 0, tiled=True).reshape(D, bw + 2 * fl)
    projector_copy, combiner_copy, expander_copy, reducer_copy = call(
        finish_kernel,
        [((3, cl, D), BF), ((cl, D), BF), ((D, fl), BF), ((fl, D), BF)],
        new_low,
    )
    for i in (3, 4, 5, 9, 10, 11):
        fresh[i] = fresh[i].T
    mine = mine + swap(theirs, 1)
    pieces = {0: own_out}
    for bit in chip_bits:
        mine = mine + swap(mine, bit)
        for r in list(pieces):
            pieces[r ^ bit] = swap(pieces[r], bit)
    for r in list(pieces):
        pieces[r ^ 1] = swap(pieces[r], 1)
    input_grad, layer_out = call(
        assemble_kernel,
        [((seq, D), F32), ((seq, D), BF)],
        info,
        mine,
        swap(mine, 1),
        *(pieces[r] for r in names),
        smem=1,
    )
    return (
        layer_out,
        input_grad,
        *fresh,
        *fresh_small,
        jnp.swapaxes(projector_copy, 1, 2),
        combiner_copy,
        expander_copy,
        reducer_copy,
    )


def solution(mesh):
    rows = P("dp", None)
    by_weight = [P(None, "dp", "mp"), P("mp", "dp"), P("dp", "mp"), P("mp", "dp"), P(None, "dp")]
    threes = [spec for spec in by_weight for _ in range(3)]
    return jax.shard_map(
        body,
        mesh=mesh,
        in_specs=(rows, rows, P("dp"), *threes),
        out_specs=(
            rows,
            rows,
            *threes,
            P(None, None, "mp"),
            P("mp", None),
            P(None, "mp"),
            P("mp", None),
        ),
        check_vma=False,
    )
```

```python
import math

import jax
import jax.numpy as jnp
from jax import lax
from jax.experimental import pallas as pl
from jax.experimental.pallas import tpu as pltpu
from jax.sharding import PartitionSpec as P

D = 256
FF = 2048
HD = 32
SEQ = 1024
WROW = 32
STEP = 5
LANES = 128
LOG2E = 1.4426950408889634
INTERPRET = False
BF = jnp.bfloat16
F32 = jnp.float32


def dot(a, b):
    return jnp.dot(a, b, preferred_element_type=F32)


def dot_nt(a, b):
    return lax.dot_general(a, b, (((1,), (1,)), ((), ())), preferred_element_type=F32)


def flip(x):
    return x.T


def lane_of(shape):
    return lax.broadcasted_iota(jnp.int32, shape, 1)


def row_of(shape):
    return lax.broadcasted_iota(jnp.int32, shape, 0)


def place_rows(x, start, total):
    parts = []
    if start:
        parts.append(jnp.zeros((start, x.shape[1]), x.dtype))
    parts.append(x)
    if total - start - x.shape[0]:
        parts.append(jnp.zeros((total - start - x.shape[0], x.shape[1]), x.dtype))
    return jnp.concatenate(parts, axis=0) if len(parts) > 1 else x


def call(kernel, outs, *args, scratch=(), smem=0, flops=0):
    vm = pl.BlockSpec(memory_space=pltpu.VMEM)
    sm = pl.BlockSpec(memory_space=pltpu.SMEM)
    return pl.pallas_call(
        kernel,
        out_shape=[jax.ShapeDtypeStruct(s, d) for s, d in outs],
        in_specs=[sm] * smem + [vm] * (len(args) - smem),
        out_specs=[vm] * len(outs),
        scratch_shapes=[pltpu.VMEM(s, d) for s, d in scratch],
        cost_estimate=pl.CostEstimate(flops=flops, transcendentals=0, bytes_accessed=0)
        if flops
        else None,
        compiler_params=pltpu.CompilerParams(vmem_limit_bytes=24 * 2**20),
        interpret=INTERPRET,
    )(*args)


def pack_kernel(*refs):
    given, pack, held, arrived = refs[:5], refs[5], refs[6:11], refs[11]
    fetches = [
        pltpu.make_async_copy(source, target, arrived.at[i])
        for i, (source, target) in enumerate(zip(given, held, strict=True))
    ]
    for fetch in fetches:
        fetch.start()
    projector, combiner_t, expander, reducer_t, affines = held
    dl, fl = expander.shape
    cl = combiner_t.shape[1]
    for fetch in fetches:
        fetch.wait()
    gains = jnp.concatenate([affines[...], jnp.zeros((LANES - 4, dl), F32)], axis=0).T
    high = gains.astype(BF).astype(F32)
    rest = pltpu.roll(gains - high, 4, 1)
    tail = jnp.where(lane_of(high.shape) < 4, high, rest).astype(BF)
    low = [projector[i].astype(BF) for i in range(3)] + [combiner_t[...].astype(BF)]
    pack[:, : 4 * cl] = jnp.concatenate(low, axis=1)
    pack[:, 4 * cl : 4 * cl + fl] = expander[...].astype(BF)
    pack[:, 4 * cl + fl : 4 * cl + 2 * fl] = reducer_t[...].astype(BF)
    pack[:, 4 * cl + 2 * fl :] = tail


def prepare_kernel(shares, info, tokens, tokens_out, query_in, tokens_t, query_t, order, whole):
    seq, width = tokens.shape
    half = width // 2
    rows = seq // WROW
    shape = (max(rows, WROW), half)
    channel = lane_of(shape)
    exponent = (2 * (channel // 2)).astype(F32) / half
    angles = (row_of(shape) + 1).astype(F32) * jnp.exp(-math.log(10000.0) * exponent)
    table = jnp.where(channel % 2 == 0, jnp.sin(angles), jnp.cos(angles))
    for i in range(rows):
        lower = i * WROW
        spot = jnp.concatenate(
            [jnp.broadcast_to(table[i : i + 1], (WROW, half)), table[:WROW]], axis=1
        )
        part = tokens[lower : lower + WROW, :].astype(F32) + spot
        whole[lower : lower + WROW, :] = part.astype(BF)
    share = width // shares
    bits = shares.bit_length() - 1
    place = lane_of((width, width))
    slot = place // share
    source = jnp.zeros_like(slot)
    for k in range(bits):
        source = source + (((slot >> k) & 1) << (bits - 1 - k))
    source = (source ^ info[2]) * share + place % share
    order[...] = jnp.where(row_of((width, width)) == source, 1.0, 0.0).astype(BF)
    for source_ref, out, out_t in ((whole, query_in, query_t), (tokens, tokens_out, tokens_t)):
        moved = dot(source_ref[...], order[...]).astype(BF)
        out[...] = moved
        out_t[...] = flip(moved)


def stack(upper, lower):
    return jnp.concatenate([upper[...], lower[...]], axis=0)


def attend_kernel(blocks, chunk, info, tokens, query_in, *refs):
    ins, outs, scores = refs[: 2 * blocks], refs[2 * blocks : -1], refs[-1]
    seq = tokens.shape[0]
    length, offset = info[0], info[1]
    fold = HD**-0.5 * LOG2E
    whole = [stack(*ins[2 * b : 2 * b + 2]) for b in range(blocks)]
    bw = whole[0].shape[1]
    cl = bw // 4
    mid = 2 * cl
    from_query = dot(query_in[...], jnp.concatenate([x[:, :mid] for x in whole], axis=1))
    from_token = dot(tokens[...], jnp.concatenate([x[:, mid:] for x in whole], axis=1))
    dead = jnp.where(row_of((seq, 1)) < length, 0.0, 1.0)
    work = []
    for b in range(blocks):
        block = whole[b]
        z, z_t, q_t, context_t, inverse, raised = outs[6 * b : 6 * b + 6]
        rows = q_t.shape[1]
        left = from_query[:, b * mid : (b + 1) * mid]
        z[:, :mid] = jnp.where(lane_of((1, mid)) == 0, dead, left).astype(BF)
        z[:, mid:] = from_token[:, b * mid : (b + 1) * mid].astype(BF)
        own = query_in[pl.ds(pl.multiple_of(offset, 8), rows), :]
        q_all = flip(dot(own, block).astype(BF))
        q_t[...] = q_all[:cl]
        z_t[...] = flip(z[...])
        for h in range(cl // HD):
            lower = h * HD
            side = place_rows(q_all[lower : lower + HD], cl + lower, bw)
            side = jnp.where(row_of(side.shape) == 0, -1e30, side.astype(F32)).astype(BF)
            work.append((b, h, side))
    def score(i):
        b, h, side = work[i]
        z = outs[6 * b]
        peak = jnp.full((1, rows), -jnp.inf, F32)
        for c in range(0, seq, chunk):
            part = dot(z[c : c + chunk, :], side)
            scores[i, c : c + chunk, :] = part
            peak = jnp.maximum(peak, jnp.max(part, axis=0, keepdims=True))
        return peak

    def mix(i):
        b, h, side = work[i]
        z, z_t, q_t, context_t, inverse, raised = outs[6 * b : 6 * b + 6]
        lower = h * HD
        mixed = dot(z_t[2 * cl + lower : 2 * cl + lower + HD, :], raised[h])
        context_t[lower : lower + HD, :] = mixed * inverse[h : h + 1, :]

    peak = score(0)
    for i, (b, h, side) in enumerate(work):
        inverse, raised = outs[6 * b + 4 : 6 * b + 6]
        after = score(i + 1) if i + 1 < len(work) else None
        total = jnp.zeros((1, rows), F32)
        for c in range(0, seq, chunk):
            part = jnp.exp2((scores[i, c : c + chunk, :] - peak) * fold)
            total = total + jnp.sum(part, axis=0, keepdims=True)
            raised[h, c : c + chunk, :] = part.astype(BF)
        inverse[h : h + 1, :] = 1.0 / total
        peak = after
        if i:
            mix(i - 1)
    mix(len(work) - 1)


def norm(x):
    average = jnp.mean(x, axis=-1, keepdims=True)
    centred = x - average
    scale = lax.rsqrt(jnp.mean(centred * centred, axis=-1, keepdims=True) + 1e-05)
    return centred * scale, scale


def norm_back(grad, unit, scale, gains):
    inner = grad * gains
    mean_one = jnp.mean(inner, axis=-1, keepdims=True)
    mean_two = jnp.mean(inner * unit, axis=-1, keepdims=True)
    back = scale * (inner - mean_one - unit * mean_two)
    gain_grad = jnp.sum(grad * unit, axis=0, keepdims=True)
    bias_grad = jnp.sum(grad, axis=0, keepdims=True)
    return back, gain_grad, bias_grad


def feed_kernel(blocks, info, tokens, cotangent, *refs):
    order, contexts, pairs = refs[0], refs[1 : blocks + 1], refs[blocks + 1 : 5 * blocks + 1]
    attention_pairs, feed_pairs = pairs[: 2 * blocks], pairs[2 * blocks :]
    layer_out, grad_one, *grads = refs[5 * blocks + 1 : 7 * blocks + 3]
    slopes, hidden_all = refs[7 * blocks + 3 :]
    attention_blocks = [stack(*attention_pairs[2 * b : 2 * b + 2]) for b in range(blocks)]
    halves = [feed_pairs[2 * b : 2 * b + 2] for b in range(blocks)]
    rows, width = layer_out.shape
    length, offset = info[0], pl.multiple_of(info[1], 8)
    bw = attention_blocks[0].shape[1]
    cl = bw // 4
    fl = (feed_pairs[0].shape[1] - LANES) // 2
    half = width // 2
    first_blocks = [stack(up.at[:, :fl], low.at[:, :fl]) for up, low in halves]
    second_blocks = [stack(up.at[:, fl : 2 * fl], low.at[:, fl : 2 * fl]) for up, low in halves]
    own = tokens[pl.ds(offset, rows), :].astype(F32)
    context = flip(jnp.concatenate([ref[...].astype(BF) for ref in contexts], axis=0))
    combiner = jnp.concatenate([attention_blocks[b][:, 3 * cl :] for b in range(blocks)], axis=1)
    attention = dot_nt(context, combiner)
    tail = [x[:, 2 * fl :].astype(F32) for x in halves[0]]
    pieces = jnp.concatenate(tail, axis=0).T
    gain_one, bias_one, gain_two, bias_two = (
        pieces[i : i + 1] + pieces[i + 4 : i + 5] for i in range(4)
    )
    unit_one, scale_one = norm(own + attention)
    first = unit_one * gain_one + bias_one
    first_low = first.astype(BF)
    feed = jnp.zeros((rows, width), F32)
    after = dot(first_low, first_blocks[0])
    for b in range(blocks):
        pre = after
        if b + 1 < blocks:
            after = dot(first_low, first_blocks[b + 1])
        square = pre * pre
        half_pre = 0.5 * pre
        bend = jnp.tanh(pre * (0.7978845608 + 0.035677408 * square))
        hidden = (half_pre + half_pre * bend).astype(BF)
        steep = 0.7978845608 + 0.107032224 * square
        slopes[b] = (0.5 + 0.5 * bend) + half_pre * (1.0 - bend * bend) * steep
        hidden_all[b] = hidden
        feed = feed + dot_nt(hidden, second_blocks[b])
    unit_two, scale_two = norm(first + feed)
    layer_out[...] = dot_nt((unit_two * gain_two + bias_two).astype(BF), order[...]).astype(BF)
    live = (row_of((rows, width)) + offset) < length
    seed = jnp.where(live, dot(cotangent[pl.ds(offset, rows), :], order[...]), 0.0)
    grad_two, d_gain_two, d_bias_two = norm_back(seed, unit_two, scale_two, gain_two)
    grad_two_low = grad_two.astype(BF)
    grad_two_t = flip(grad_two_low)
    first_t = flip(first_low)
    grad_first = grad_two
    after = dot(grad_two_low, second_blocks[0])
    for b in range(blocks):
        grad_hidden = after
        if b + 1 < blocks:
            after = dot(grad_two_low, second_blocks[b + 1])
        grad_pre = (grad_hidden * slopes[b]).astype(BF)
        for side in range(2):
            part = slice(side * half, (side + 1) * half)
            out = grads[2 * b + side]
            out[:, :fl] = dot(first_t[part], grad_pre).astype(BF)
            out[:, fl : 2 * fl] = dot(grad_two_t[part], hidden_all[b]).astype(BF)
        grad_first = grad_first + dot_nt(grad_pre, first_blocks[b])
    back, d_gain_one, d_bias_one = norm_back(grad_first, unit_one, scale_one, gain_one)
    grad_one[...] = back
    stacked = jnp.concatenate(
        [d_gain_one, d_bias_one, d_gain_two, d_bias_two, jnp.zeros((LANES - 4, width), F32)], axis=0
    )
    columns = stacked.T.astype(BF)
    for b in range(blocks):
        grads[2 * b][:, 2 * fl :] = columns[:half]
        grads[2 * b + 1][:, 2 * fl :] = columns[half:]


def attend_back_kernel(blocks, chunk, first, last, info, query_in, tokens_t, query_t, grad_one, *refs):
    made = blocks + 4 + last
    order, ins = refs[0], refs[1 : 8 * blocks + 1]
    rest = refs[8 * blocks + 1 :]
    earlier = None if first else rest[0]
    seq, width = query_in.shape
    score_grads, sums, total = rest[-3:]
    outs = rest[len(rest) - made : -3]
    rows = grad_one.shape[0]
    offset = pl.multiple_of(info[1], 8)
    scaling = HD**-0.5
    grad_low = grad_one[...].astype(BF)
    grad_t = flip(grad_low)
    own_t = flip(query_in[pl.ds(offset, rows), :])
    own_total = grad_one[...] if earlier is None else jnp.zeros((rows, width), F32)
    for b in range(blocks):
        upper, lower_half, z, z_t, q_t, context_ref, inverse, raised = ins[8 * b : 8 * b + 8]
        block = stack(upper, lower_half)
        bw = block.shape[1]
        cl = bw // 4
        lane = lane_of((1, bw))
        context_t = context_ref[...]
        grad_context_t = dot(grad_low, block).T[3 * cl :]
        scaled = [
            (grad_context_t[h * HD : (h + 1) * HD] * inverse[h : h + 1, :]).astype(BF)
            for h in range(cl // HD)
        ]
        q_side = flip(place_rows(q_t[...], cl, bw)).astype(F32)
        grad_side = flip(place_rows(jnp.concatenate(scaled, axis=0), 2 * cl, bw)).astype(F32)
        heads = range(cl // HD)
        sides, deltas, right = [], [], []
        for h in heads:
            lower = h * HD
            deltas.append(
                jnp.sum(
                    scaled[h].astype(F32) * context_t[lower : lower + HD], axis=0, keepdims=True
                )
            )
            sides.append(place_rows(scaled[h], 2 * cl + lower, bw))
            for start, side in ((cl, q_side), (2 * cl, grad_side)):
                mask = (lane >= start + lower) & (lane < start + lower + HD)
                right.append(jnp.where(mask, side, 0.0).astype(BF))
        right = jnp.concatenate(right, axis=0)
        for c in range(0, seq, chunk):
            keys = z[c : c + chunk, :]
            left = []
            for h in heads:
                weights = raised[h, c : c + chunk, :]
                slopes = (weights.astype(F32) * (dot(keys, sides[h]) - deltas[h])).astype(BF)
                score_grads[h, c : c + chunk, :] = slopes
                left += [slopes, weights]
            sums[c : c + chunk, :] = dot(jnp.concatenate(left, axis=1), right)
        query_grads = [
            (dot(z_t[cl + h * HD : cl + (h + 1) * HD, :], score_grads[h]) * scaling).astype(BF)
            for h in heads
        ]
        both = (sums[...] * jnp.where(lane < 2 * cl, scaling, 1.0)).astype(BF)
        query_grad = flip(place_rows(jnp.concatenate(query_grads, axis=0), 0, bw))
        context = flip(place_rows(context_t.astype(BF), 3 * cl, bw))
        of_query = dot(query_t[...], both)
        of_token = dot(tokens_t[...], both)
        weight_grad = dot(own_t, query_grad) + dot(grad_t, context)
        outs[b][...] = (weight_grad + jnp.where(lane < 2 * cl, of_query, of_token)).astype(BF)
        part = dot_nt(both, block)
        if b:
            part = part + total[...]
        elif earlier is not None:
            part = part + earlier[...]
        total[...] = part
        own_total = own_total + dot_nt(query_grad, block)
    total[pl.ds(offset, rows), :] += own_total
    if not last:
        outs[-1][...] = total[...]
        return
    total[...] = dot_nt(total[...].astype(BF), order[...])
    half = seq // 2
    for out, core in zip(outs[-2:], (info[3], 1 - info[3]), strict=True):
        out[...] = total[pl.ds(pl.multiple_of(core * half, 8), half), :].astype(BF)


def merge_kernel(*refs):
    *ins, keep, send = refs
    bw = ins[0].shape[1]
    rows = keep.shape[0]
    for i, out in enumerate((keep, send)):
        part = slice(i * rows, (i + 1) * rows)
        low, high = ([x[part, :].astype(F32) for x in group] for group in (ins[:2], ins[2:]))
        out[:, :bw] = (low[0] + low[1]).astype(BF)
        out[:, bw:] = sum(high[1:], high[0]).astype(BF)


def adamw(weight, moment_one, moment_two, grad, step_rate, decay_rate):
    mean_next = 0.5 * moment_one + 0.5 * grad
    square_next = 0.5 * moment_two + 0.5 * grad * grad
    correct = 1.0 - 0.5**STEP
    direction = mean_next / correct / (jnp.sqrt(square_next / correct) + 1e-08)
    weight_next = weight - step_rate * (direction + decay_rate * weight)
    return (weight_next, mean_next, square_next)


def update_kernel(rates, kept, came, *refs):
    ins, outs, pack = refs[:13], refs[13:26], refs[26]
    grad = kept[...].astype(F32) + came[...].astype(F32)
    cl = ins[0].shape[2]
    fl = ins[6].shape[1]
    fresh = []
    for i in range(3):
        fresh.append(
            adamw(*(ins[k][i] for k in range(3)), grad[:, i * cl : (i + 1) * cl], *rates[0])
        )
        for k in range(3):
            outs[k][i] = fresh[-1][k]
    start = 3 * cl
    for j, size in ((1, cl), (2, fl), (3, fl)):
        fresh.append(
            adamw(*(ins[3 * j + k][...] for k in range(3)), grad[:, start : start + size], *rates[j])
        )
        for k in range(3):
            outs[3 * j + k][...] = fresh[-1][k]
        start += size
    small = grad[:, start:].T[:4]
    for k, value in enumerate(adamw(*(ins[12][k] for k in range(3)), small, *rates[4])):
        outs[12][k] = value
    whole = jnp.concatenate([new[0].astype(BF) for new in fresh], axis=1)
    pack[...] = whole


def assemble_kernel(info, mine, other, *refs):
    *pieces, input_grad, layer_out = refs
    half = mine.shape[0]
    for part, core in ((mine, info[3]), (other, 1 - info[3])):
        input_grad[pl.ds(pl.multiple_of(core * half, 8), half), :] = part[...].astype(F32)
    rows = pieces[0].shape[0]
    for r, piece in enumerate(pieces):
        layer_out[pl.ds(pl.multiple_of((info[4] ^ r) * rows, 16), rows), :] = piece[...]


def finish_kernel(order, *refs):
    *pieces, projector_t, combiner, expander, reducer = refs
    copies = jnp.concatenate([piece[...] for piece in pieces], axis=0)
    copies = dot(order[...], copies).astype(BF)
    cl = combiner.shape[0]
    fl = reducer.shape[0]
    for i in range(3):
        projector_t[i] = flip(copies[:, i * cl : (i + 1) * cl])
    combiner[...] = flip(copies[:, 3 * cl : 4 * cl])
    expander[...] = copies[:, 4 * cl : 4 * cl + fl]
    reducer[...] = flip(copies[:, 4 * cl + fl : 4 * cl + 2 * fl])


def body(
    tokens,
    cotangent,
    lengths,
    projector,
    projector_mean,
    projector_square,
    combiner,
    combiner_mean,
    combiner_square,
    expander,
    expander_mean,
    expander_square,
    reducer,
    reducer_mean,
    reducer_square,
    affines,
    affines_mean,
    affines_square,
):
    mp = lax.axis_size("mp")
    dp = lax.axis_size("dp")
    me = lax.axis_index("mp")
    seq = tokens.shape[0]
    if lengths.shape[0] != 1 or mp & (mp - 1):
        raise ValueError("unsupported mesh")
    rows = seq // mp
    dl = expander.shape[0]
    cl = projector.shape[2]
    fl = expander.shape[1]
    bw = 4 * cl
    heads = cl // HD
    chunk = 256
    spot = lax.axis_index("dp")
    me, spot = me.astype(jnp.int32), spot.astype(jnp.int32)
    info = jnp.stack([lengths[0], me * rows, spot, me & 1, me])

    def swap(x, bit, axis="mp"):
        return lax.ppermute(x, axis, [(i, i ^ bit) for i in range(lax.axis_size(axis))])

    pack_width = bw + 2 * fl + LANES
    shares = [projector, combiner.T, expander, reducer.T, affines]
    [pack] = pl.pallas_call(
        pack_kernel,
        out_shape=[jax.ShapeDtypeStruct((dl, pack_width), BF)],
        in_specs=[pl.BlockSpec(memory_space=pltpu.HBM)] * len(shares),
        out_specs=[pl.BlockSpec(memory_space=pltpu.VMEM)],
        scratch_shapes=[
            *(pltpu.VMEM(x.shape, x.dtype) for x in shares),
            pltpu.SemaphoreType.DMA((len(shares),)),
        ],
        interpret=INTERPRET,
    )(*(pltpu.with_memory_space_constraint(x, pltpu.HBM) for x in shares))
    names = list(range(mp))
    near, far = names[:2], names[2:]
    chip_bits = [1 << i for i in range(1, mp.bit_length() - 1)]
    down = chip_bits[::-1]
    line_bits = [1 << i for i in range(1, dp.bit_length() - 1)]
    tokens_in, query_in, tokens_t, query_t, order = call(
        lambda *refs: prepare_kernel(dp, *refs),
        [((seq, D), BF)] * 2 + [((D, seq), BF)] * 2 + [((D, D), BF)],
        info,
        tokens,
        scratch=[((seq, D), BF)],
        smem=1,
    )
    small = jnp.stack([affines, affines_mean, affines_square])
    for bit in line_bits[::-1]:
        came = swap(pack, bit, "dp")
        if bit == line_bits[-1]:
            came, order, small = lax.optimization_barrier((came, order, small))
        pack = jnp.concatenate([pack, came], axis=0)

    def cross(part):
        halves = {0: part}
        for bit in chip_bits:
            for r in list(halves):
                halves[r ^ bit] = swap(halves[r], bit)
        return halves

    def pair(blocks, group):
        for r in group:
            blocks[r ^ 1] = [swap(x, 1) for x in blocks[r]]

    attention_half, feed_half = pack[:, :bw], pack[:, bw:]
    upper = cross(attention_half)
    attention_blocks = {r: [x, swap(x, 1, "dp")] for r, x in upper.items()}
    feed_upper = cross(feed_half)
    feed_other, attention_blocks[0][1], attention_blocks[2][0] = lax.optimization_barrier(
        (swap(feed_half, 1, "dp"), attention_blocks[0][1], attention_blocks[2][0])
    )
    feed_lower = cross(feed_other)
    feed_blocks = {r: [feed_upper[r], feed_lower[r]] for r in feed_upper}
    pair(attention_blocks, names[:1])
    pair(feed_blocks, names[:1])

    def attend(group):
        made = call(
            lambda *refs: attend_kernel(len(group), chunk, *refs),
            [
                ((seq, bw), BF),
                ((bw, seq), BF),
                ((cl, rows), BF),
                ((cl, rows), F32),
                ((heads, rows), F32),
                ((heads, seq, rows), BF),
            ]
            * len(group),
            info,
            tokens_in,
            query_in,
            *(x for r in group for x in attention_blocks[r]),
            scratch=[((len(group) * heads, seq, rows), F32)],
            smem=1,
            flops=4 * len(group) * (heads + 1) * seq * rows * D,
        )
        return {r: list(made[6 * i : 6 * i + 6]) for i, r in enumerate(group)}

    kept = attend(near)
    for r in far[::2]:
        attention_blocks[r][1], kept[0][3] = lax.optimization_barrier(
            (attention_blocks[r][1], kept[0][3])
        )
    pair(attention_blocks, far[::2])
    for r in far[::2]:
        feed_blocks[r], attention_blocks[r ^ 1] = lax.optimization_barrier(
            (feed_blocks[r], attention_blocks[r ^ 1])
        )
    pair(feed_blocks, far[::2])
    kept.update(attend(far))
    own_out, grad_one, *feed_grads = call(
        lambda *refs: feed_kernel(mp, *refs),
        [((rows, D), BF), ((rows, D), F32)]
        + [((D // 2, 2 * fl + LANES), BF)] * (2 * mp),
        info,
        tokens_in,
        cotangent,
        order,
        *(kept[r][3] for r in names),
        *(x for r in names for x in attention_blocks[r]),
        *(x for r in names for x in feed_blocks[r]),
        scratch=[((mp, rows, fl), F32), ((mp, rows, fl), BF)],
        smem=1,
        flops=12 * mp * rows * D * fl,
    )

    def attend_back(group, earlier=(), last=False):
        return call(
            lambda *refs: attend_back_kernel(len(group), chunk, not earlier, last, *refs),
            [((D, bw), BF)] * len(group)
            + ([((seq // 2, D), BF)] * 2 if last else [((seq, D), F32)]),
            info,
            query_in,
            tokens_t,
            query_t,
            grad_one,
            order,
            *(x for r in group for x in (*attention_blocks[r], *kept[r])),
            *earlier,
            scratch=[((heads, seq, rows), BF), ((seq, bw), F32), ((seq, D), F32)],
            smem=1,
            flops=8 * len(group) * (heads + 1) * seq * rows * D,
        )

    def reduce_blocks(left, order):
        left = dict(left)
        for bit in order:
            for r in sorted({r & ~bit for r in left if r & bit}):
                came = swap(left.pop(r ^ bit), bit)
                left[r] = left[r] + came if r in left else came
        return left

    down = chip_bits[::-1]
    own_side, other_side = (
        reduce_blocks(zip(names, feed_grads[i::2], strict=True), [1]) for i in range(2)
    )
    other_side, grad_one = lax.optimization_barrier((other_side, grad_one))
    other_side = reduce_blocks(other_side, down)[0]
    *far_grads, far_part = attend_back(far)
    far_grads = reduce_blocks(zip(far, far_grads, strict=True), [1])
    far_grads, far_part = lax.optimization_barrier((far_grads, far_part))
    far_grads = reduce_blocks(far_grads, down)[0]
    [side_grad, near_part] = attend_back(near[1:], (far_part,))
    other_side, own_side, far_grads, near_part = lax.optimization_barrier(
        (other_side, own_side, far_grads, near_part)
    )
    own_side = reduce_blocks(own_side, down[:-1])
    came = [swap(other_side, 1, "dp"), *(swap(own_side[r], r) for r in down[-1:])]
    [own_grad, mine, theirs] = attend_back(near[:1], (near_part,), last=True)
    near_grads = own_grad + swap(side_grad, 1) + far_grads
    half = D // 2
    keep, send = call(
        merge_kernel,
        [((half // 2, pack_width), BF)] * 2,
        near_grads[:half],
        swap(near_grads[half:], 1, "dp"),
        own_side[0],
        *came,
    )
    theirs, keep = lax.optimization_barrier((theirs, keep))
    mine = mine + swap(theirs, 1)
    for bit in line_bits:
        arrived = swap(send, bit, "dp")
        if bit != line_bits[-1]:
            summed = keep + arrived
            half = summed.shape[0] // 2
            keep, send = summed[:half], summed[half:]
    masters = (
        (projector, projector_mean, projector_square),
        (combiner.T, combiner_mean.T, combiner_square.T),
        (expander, expander_mean, expander_square),
        (reducer.T, reducer_mean.T, reducer_square.T),
    )
    rates = (
        (D ** (-0.5), 0.0001),
        (max(1, D * 8 // SEQ) ** (-0.5), 0.0001),
        (D ** (-0.5), 0.0001),
        (FF ** (-0.5), 0.0001),
        (0.4, 0.0),
    )
    flat = [x for three in masters for x in three]
    *fresh, fresh_small, new_pack = call(
        lambda *refs: update_kernel(rates, *refs),
        [(x.shape, F32) for x in (*flat, small)] + [((dl, bw + 2 * fl), BF)],
        keep,
        arrived,
        *flat,
        small,
    )
    copies = [new_pack]
    for bit in line_bits[::-1]:
        copies += [swap(x, bit, "dp") for x in copies]
    copies += [swap(x, 1, "dp") for x in copies]
    own_out, _ = lax.optimization_barrier((own_out, arrived))
    pieces = {0: own_out}
    for bit in chip_bits:
        mine = mine + swap(mine, bit)
        for r in list(pieces):
            pieces[r ^ bit] = swap(pieces[r], bit)
    for r in list(pieces):
        pieces[r ^ 1] = swap(pieces[r], 1)
    input_grad, layer_out = call(
        assemble_kernel,
        [((seq, D), F32), ((seq, D), BF)],
        info,
        mine,
        swap(mine, 1),
        *(pieces[r] for r in names),
        smem=1,
    )
    copies[-1], input_grad = lax.optimization_barrier((copies[-1], input_grad))
    projector_copy, combiner_copy, expander_copy, reducer_copy = call(
        finish_kernel,
        [((3, cl, D), BF), ((cl, D), BF), ((D, fl), BF), ((fl, D), BF)],
        order,
        *copies,
    )
    for i in (3, 4, 5, 9, 10, 11):
        fresh[i] = fresh[i].T
    return (
        layer_out,
        input_grad,
        *fresh,
        *fresh_small,
        jnp.swapaxes(projector_copy, 1, 2),
        combiner_copy,
        expander_copy,
        reducer_copy,
    )


def solution(mesh):
    rows = P("dp", None)
    by_weight = [P(None, "dp", "mp"), P("mp", "dp"), P("dp", "mp"), P("mp", "dp"), P(None, "dp")]
    threes = [spec for spec in by_weight for _ in range(3)]
    return jax.shard_map(
        body,
        mesh=mesh,
        in_specs=(rows, rows, P("dp"), *threes),
        out_specs=(
            rows,
            rows,
            *threes,
            P(None, None, "mp"),
            P("mp", None),
            P(None, "mp"),
            P("mp", None),
        ),
        check_vma=False,
    )
```

```python
import math

import jax
import jax.numpy as jnp
from jax import lax
from jax.experimental import pallas as pl
from jax.experimental.pallas import tpu as pltpu
from jax.sharding import PartitionSpec as P

D = 256
FF = 2048
HD = 32
SEQ = 1024
WROW = 32
STEP = 5
LANES = 128
LOG2E = 1.4426950408889634
INTERPRET = False
BF = jnp.bfloat16
F32 = jnp.float32


def dot(a, b):
    return jnp.dot(a, b, preferred_element_type=F32)


def dot_nt(a, b):
    return lax.dot_general(a, b, (((1,), (1,)), ((), ())), preferred_element_type=F32)


def flip(x):
    return x.T


def lane_of(shape):
    return lax.broadcasted_iota(jnp.int32, shape, 1)


def row_of(shape):
    return lax.broadcasted_iota(jnp.int32, shape, 0)


def place_rows(x, start, total):
    parts = []
    if start:
        parts.append(jnp.zeros((start, x.shape[1]), x.dtype))
    parts.append(x)
    if total - start - x.shape[0]:
        parts.append(jnp.zeros((total - start - x.shape[0], x.shape[1]), x.dtype))
    return jnp.concatenate(parts, axis=0) if len(parts) > 1 else x


def call(kernel, outs, *args, scratch=(), smem=0, flops=0):
    vm = pl.BlockSpec(memory_space=pltpu.VMEM)
    sm = pl.BlockSpec(memory_space=pltpu.SMEM)
    return pl.pallas_call(
        kernel,
        out_shape=[jax.ShapeDtypeStruct(s, d) for s, d in outs],
        in_specs=[sm] * smem + [vm] * (len(args) - smem),
        out_specs=[vm] * len(outs),
        scratch_shapes=[pltpu.VMEM(s, d) for s, d in scratch],
        cost_estimate=pl.CostEstimate(flops=flops, transcendentals=0, bytes_accessed=0)
        if flops
        else None,
        compiler_params=pltpu.CompilerParams(vmem_limit_bytes=24 * 2**20),
        interpret=INTERPRET,
    )(*args)


def pack_kernel(*refs):
    given, pack, held, arrived = refs[:5], refs[5], refs[6:11], refs[11]
    fetches = [
        pltpu.make_async_copy(source, target, arrived.at[i])
        for i, (source, target) in enumerate(zip(given, held, strict=True))
    ]
    for fetch in fetches:
        fetch.start()
    projector, combiner_t, expander, reducer_t, affines = held
    dl, fl = expander.shape
    cl = combiner_t.shape[1]
    for fetch in fetches:
        fetch.wait()
    gains = jnp.concatenate([affines[...], jnp.zeros((LANES - 4, dl), F32)], axis=0).T
    high = gains.astype(BF).astype(F32)
    rest = pltpu.roll(gains - high, 4, 1)
    tail = jnp.where(lane_of(high.shape) < 4, high, rest).astype(BF)
    low = [projector[i].astype(BF) for i in range(3)] + [combiner_t[...].astype(BF)]
    pack[:, : 4 * cl] = jnp.concatenate(low, axis=1)
    pack[:, 4 * cl : 4 * cl + fl] = expander[...].astype(BF)
    pack[:, 4 * cl + fl : 4 * cl + 2 * fl] = reducer_t[...].astype(BF)
    pack[:, 4 * cl + 2 * fl :] = tail


def prepare_kernel(shares, info, tokens, tokens_out, query_in, tokens_t, query_t, order, whole):
    seq, width = tokens.shape
    half = width // 2
    rows = seq // WROW
    shape = (max(rows, WROW), half)
    channel = lane_of(shape)
    exponent = (2 * (channel // 2)).astype(F32) / half
    angles = (row_of(shape) + 1).astype(F32) * jnp.exp(-math.log(10000.0) * exponent)
    table = jnp.where(channel % 2 == 0, jnp.sin(angles), jnp.cos(angles))
    for i in range(rows):
        lower = i * WROW
        spot = jnp.concatenate(
            [jnp.broadcast_to(table[i : i + 1], (WROW, half)), table[:WROW]], axis=1
        )
        part = tokens[lower : lower + WROW, :].astype(F32) + spot
        whole[lower : lower + WROW, :] = part.astype(BF)
    share = width // shares
    bits = shares.bit_length() - 1
    place = lane_of((width, width))
    slot = place // share
    source = jnp.zeros_like(slot)
    for k in range(bits):
        source = source + (((slot >> k) & 1) << (bits - 1 - k))
    source = (source ^ info[2]) * share + place % share
    order[...] = jnp.where(row_of((width, width)) == source, 1.0, 0.0).astype(BF)
    for source_ref, out, out_t in ((whole, query_in, query_t), (tokens, tokens_out, tokens_t)):
        moved = dot(source_ref[...], order[...]).astype(BF)
        out[...] = moved
        out_t[...] = flip(moved)


def stack(upper, lower):
    return jnp.concatenate([upper[...], lower[...]], axis=0)


def attend_kernel(blocks, chunk, info, tokens, query_in, *refs):
    ins, outs, scores = refs[: 2 * blocks], refs[2 * blocks : -1], refs[-1]
    seq = tokens.shape[0]
    length, offset = info[0], info[1]
    fold = HD**-0.5 * LOG2E
    whole = [stack(*ins[2 * b : 2 * b + 2]) for b in range(blocks)]
    bw = whole[0].shape[1]
    cl = bw // 4
    mid = 2 * cl
    from_query = dot(query_in[...], jnp.concatenate([x[:, :mid] for x in whole], axis=1))
    from_token = dot(tokens[...], jnp.concatenate([x[:, mid:] for x in whole], axis=1))
    dead = jnp.where(row_of((seq, 1)) < length, 0.0, 1.0)
    work = []
    for b in range(blocks):
        block = whole[b]
        z, z_t, q_t, context_t, inverse, raised = outs[6 * b : 6 * b + 6]
        rows = q_t.shape[1]
        left = from_query[:, b * mid : (b + 1) * mid]
        z[:, :mid] = jnp.where(lane_of((1, mid)) == 0, dead, left).astype(BF)
        z[:, mid:] = from_token[:, b * mid : (b + 1) * mid].astype(BF)
        own = query_in[pl.ds(pl.multiple_of(offset, 8), rows), :]
        q_all = flip(dot(own, block).astype(BF))
        q_t[...] = q_all[:cl]
        z_t[...] = flip(z[...])
        for h in range(cl // HD):
            lower = h * HD
            side = place_rows(q_all[lower : lower + HD], cl + lower, bw)
            side = jnp.where(row_of(side.shape) == 0, -1e30, side.astype(F32)).astype(BF)
            work.append((b, h, side))
    def score(i):
        b, h, side = work[i]
        z = outs[6 * b]
        peak = jnp.full((1, rows), -jnp.inf, F32)
        for c in range(0, seq, chunk):
            part = dot(z[c : c + chunk, :], side)
            scores[i, c : c + chunk, :] = part
            peak = jnp.maximum(peak, jnp.max(part, axis=0, keepdims=True))
        return peak

    def mix(i):
        b, h, side = work[i]
        z, z_t, q_t, context_t, inverse, raised = outs[6 * b : 6 * b + 6]
        lower = h * HD
        mixed = dot(z_t[2 * cl + lower : 2 * cl + lower + HD, :], raised[h])
        context_t[lower : lower + HD, :] = mixed * inverse[h : h + 1, :]

    peak = score(0)
    for i, (b, h, side) in enumerate(work):
        inverse, raised = outs[6 * b + 4 : 6 * b + 6]
        after = score(i + 1) if i + 1 < len(work) else None
        total = jnp.zeros((1, rows), F32)
        for c in range(0, seq, chunk):
            part = jnp.exp2((scores[i, c : c + chunk, :] - peak) * fold)
            total = total + jnp.sum(part, axis=0, keepdims=True)
            raised[h, c : c + chunk, :] = part.astype(BF)
        inverse[h : h + 1, :] = 1.0 / total
        peak = after
        if i:
            mix(i - 1)
    mix(len(work) - 1)


def norm(x):
    average = jnp.mean(x, axis=-1, keepdims=True)
    centred = x - average
    scale = lax.rsqrt(jnp.mean(centred * centred, axis=-1, keepdims=True) + 1e-05)
    return centred * scale, scale


def norm_back(grad, unit, scale, gains):
    inner = grad * gains
    mean_one = jnp.mean(inner, axis=-1, keepdims=True)
    mean_two = jnp.mean(inner * unit, axis=-1, keepdims=True)
    back = scale * (inner - mean_one - unit * mean_two)
    gain_grad = jnp.sum(grad * unit, axis=0, keepdims=True)
    bias_grad = jnp.sum(grad, axis=0, keepdims=True)
    return back, gain_grad, bias_grad


def feed_kernel(blocks, info, tokens, cotangent, *refs):
    order, contexts, pairs = refs[0], refs[1 : blocks + 1], refs[blocks + 1 : 5 * blocks + 1]
    attention_pairs, feed_pairs = pairs[: 2 * blocks], pairs[2 * blocks :]
    layer_out, grad_one, *grads = refs[5 * blocks + 1 : 7 * blocks + 3]
    slopes, hidden_all = refs[7 * blocks + 3 :]
    attention_blocks = [stack(*attention_pairs[2 * b : 2 * b + 2]) for b in range(blocks)]
    halves = [feed_pairs[2 * b : 2 * b + 2] for b in range(blocks)]
    rows, width = layer_out.shape
    length, offset = info[0], pl.multiple_of(info[1], 8)
    bw = attention_blocks[0].shape[1]
    cl = bw // 4
    fl = (feed_pairs[0].shape[1] - LANES) // 2
    half = width // 2
    first_blocks = [stack(up.at[:, :fl], low.at[:, :fl]) for up, low in halves]
    second_blocks = [stack(up.at[:, fl : 2 * fl], low.at[:, fl : 2 * fl]) for up, low in halves]
    own = tokens[pl.ds(offset, rows), :].astype(F32)
    context = flip(jnp.concatenate([ref[...].astype(BF) for ref in contexts], axis=0))
    combiner = jnp.concatenate([attention_blocks[b][:, 3 * cl :] for b in range(blocks)], axis=1)
    attention = dot_nt(context, combiner)
    tail = [x[:, 2 * fl :].astype(F32) for x in halves[0]]
    pieces = jnp.concatenate(tail, axis=0).T
    gain_one, bias_one, gain_two, bias_two = (
        pieces[i : i + 1] + pieces[i + 4 : i + 5] for i in range(4)
    )
    unit_one, scale_one = norm(own + attention)
    first = unit_one * gain_one + bias_one
    first_low = first.astype(BF)
    feed = jnp.zeros((rows, width), F32)
    after = dot(first_low, first_blocks[0])
    for b in range(blocks):
        pre = after
        if b + 1 < blocks:
            after = dot(first_low, first_blocks[b + 1])
        square = pre * pre
        half_pre = 0.5 * pre
        bend = jnp.tanh(pre * (0.7978845608 + 0.035677408 * square))
        hidden = (half_pre + half_pre * bend).astype(BF)
        steep = 0.7978845608 + 0.107032224 * square
        slopes[b] = (0.5 + 0.5 * bend) + half_pre * (1.0 - bend * bend) * steep
        hidden_all[b] = hidden
        feed = feed + dot_nt(hidden, second_blocks[b])
    unit_two, scale_two = norm(first + feed)
    layer_out[...] = dot_nt((unit_two * gain_two + bias_two).astype(BF), order[...]).astype(BF)
    live = (row_of((rows, width)) + offset) < length
    seed = jnp.where(live, dot(cotangent[pl.ds(offset, rows), :], order[...]), 0.0)
    grad_two, d_gain_two, d_bias_two = norm_back(seed, unit_two, scale_two, gain_two)
    grad_two_low = grad_two.astype(BF)
    grad_two_t = flip(grad_two_low)
    first_t = flip(first_low)
    grad_first = grad_two
    after = dot(grad_two_low, second_blocks[0])
    for b in range(blocks):
        grad_hidden = after
        if b + 1 < blocks:
            after = dot(grad_two_low, second_blocks[b + 1])
        grad_pre = (grad_hidden * slopes[b]).astype(BF)
        for side in range(2):
            part = slice(side * half, (side + 1) * half)
            out = grads[2 * b + side]
            out[:, :fl] = dot(first_t[part], grad_pre).astype(BF)
            out[:, fl : 2 * fl] = dot(grad_two_t[part], hidden_all[b]).astype(BF)
        grad_first = grad_first + dot_nt(grad_pre, first_blocks[b])
    back, d_gain_one, d_bias_one = norm_back(grad_first, unit_one, scale_one, gain_one)
    grad_one[...] = back
    stacked = jnp.concatenate(
        [d_gain_one, d_bias_one, d_gain_two, d_bias_two, jnp.zeros((LANES - 4, width), F32)], axis=0
    )
    columns = stacked.T.astype(BF)
    for b in range(blocks):
        grads[2 * b][:, 2 * fl :] = columns[:half]
        grads[2 * b + 1][:, 2 * fl :] = columns[half:]


def attend_back_kernel(blocks, chunk, first, last, info, query_in, tokens_t, query_t, grad_one, *refs):
    made = blocks + 4 + last
    order, ins = refs[0], refs[1 : 8 * blocks + 1]
    rest = refs[8 * blocks + 1 :]
    earlier = None if first else rest[0]
    seq, width = query_in.shape
    score_grads, sums, total = rest[-3:]
    outs = rest[len(rest) - made : -3]
    rows = grad_one.shape[0]
    offset = pl.multiple_of(info[1], 8)
    scaling = HD**-0.5
    grad_low = grad_one[...].astype(BF)
    grad_t = flip(grad_low)
    own_t = flip(query_in[pl.ds(offset, rows), :])
    own_total = grad_one[...] if earlier is None else jnp.zeros((rows, width), F32)
    for b in range(blocks):
        upper, lower_half, z, z_t, q_t, context_ref, inverse, raised = ins[8 * b : 8 * b + 8]
        block = stack(upper, lower_half)
        bw = block.shape[1]
        cl = bw // 4
        lane = lane_of((1, bw))
        context_t = context_ref[...]
        grad_context_t = dot(grad_low, block).T[3 * cl :]
        scaled = [
            (grad_context_t[h * HD : (h + 1) * HD] * inverse[h : h + 1, :]).astype(BF)
            for h in range(cl // HD)
        ]
        q_side = flip(place_rows(q_t[...], cl, bw)).astype(F32)
        grad_side = flip(place_rows(jnp.concatenate(scaled, axis=0), 2 * cl, bw)).astype(F32)
        heads = range(cl // HD)
        sides, deltas, right = [], [], []
        for h in heads:
            lower = h * HD
            deltas.append(
                jnp.sum(
                    scaled[h].astype(F32) * context_t[lower : lower + HD], axis=0, keepdims=True
                )
            )
            sides.append(place_rows(scaled[h], 2 * cl + lower, bw))
            for start, side in ((cl, q_side), (2 * cl, grad_side)):
                mask = (lane >= start + lower) & (lane < start + lower + HD)
                right.append(jnp.where(mask, side, 0.0).astype(BF))
        right = jnp.concatenate(right, axis=0)
        for c in range(0, seq, chunk):
            keys = z[c : c + chunk, :]
            left = []
            for h in heads:
                weights = raised[h, c : c + chunk, :]
                slopes = (weights.astype(F32) * (dot(keys, sides[h]) - deltas[h])).astype(BF)
                score_grads[h, c : c + chunk, :] = slopes
                left += [slopes, weights]
            sums[c : c + chunk, :] = dot(jnp.concatenate(left, axis=1), right)
        query_grads = [
            (dot(z_t[cl + h * HD : cl + (h + 1) * HD, :], score_grads[h]) * scaling).astype(BF)
            for h in heads
        ]
        both = (sums[...] * jnp.where(lane < 2 * cl, scaling, 1.0)).astype(BF)
        query_grad = flip(place_rows(jnp.concatenate(query_grads, axis=0), 0, bw))
        context = flip(place_rows(context_t.astype(BF), 3 * cl, bw))
        of_query = dot(query_t[...], both)
        of_token = dot(tokens_t[...], both)
        weight_grad = dot(own_t, query_grad) + dot(grad_t, context)
        outs[b][...] = (weight_grad + jnp.where(lane < 2 * cl, of_query, of_token)).astype(BF)
        part = dot_nt(both, block)
        if b:
            part = part + total[...]
        elif earlier is not None:
            part = part + earlier[...]
        total[...] = part
        own_total = own_total + dot_nt(query_grad, block)
    total[pl.ds(offset, rows), :] += own_total
    if not last:
        outs[-1][...] = total[...]
        return
    total[...] = dot_nt(total[...].astype(BF), order[...])
    half = seq // 2
    for out, core in zip(outs[-2:], (info[3], 1 - info[3]), strict=True):
        out[...] = total[pl.ds(pl.multiple_of(core * half, 8), half), :].astype(BF)


def merge_kernel(shares, *refs):
    ins, outs = refs[:-shares], refs[-shares:]
    bw = ins[0].shape[1]
    rows = outs[0].shape[0]
    low, high = ([x[...].astype(F32) for x in group] for group in (ins[:2], ins[2:]))
    low, high = low[0] + low[1], sum(high[1:], high[0])
    for i, out in enumerate(outs):
        part = slice(i * rows, (i + 1) * rows)
        out[:, :bw] = low[part].astype(BF)
        out[:, bw:] = high[part].astype(BF)


def adamw(weight, moment_one, moment_two, grad, step_rate, decay_rate):
    mean_next = 0.5 * moment_one + 0.5 * grad
    square_next = 0.5 * moment_two + 0.5 * grad * grad
    correct = 1.0 - 0.5**STEP
    direction = mean_next / correct / (jnp.sqrt(square_next / correct) + 1e-08)
    weight_next = weight - step_rate * (direction + decay_rate * weight)
    return (weight_next, mean_next, square_next)


def update_kernel(rates, count, *refs):
    grad = sum((x[...].astype(F32) for x in refs[1:count]), refs[0][...].astype(F32))
    refs = refs[count:]
    ins, outs, pack = refs[:13], refs[13:26], refs[26]
    cl = ins[0].shape[2]
    fl = ins[6].shape[1]
    fresh = []
    for i in range(3):
        fresh.append(
            adamw(*(ins[k][i] for k in range(3)), grad[:, i * cl : (i + 1) * cl], *rates[0])
        )
        for k in range(3):
            outs[k][i] = fresh[-1][k]
    start = 3 * cl
    for j, size in ((1, cl), (2, fl), (3, fl)):
        fresh.append(
            adamw(*(ins[3 * j + k][...] for k in range(3)), grad[:, start : start + size], *rates[j])
        )
        for k in range(3):
            outs[3 * j + k][...] = fresh[-1][k]
        start += size
    small = grad[:, start:].T[:4]
    for k, value in enumerate(adamw(*(ins[12][k] for k in range(3)), small, *rates[4])):
        outs[12][k] = value
    whole = jnp.concatenate([new[0].astype(BF) for new in fresh], axis=1)
    pack[...] = whole


def assemble_kernel(info, mine, other, *refs):
    *pieces, input_grad, layer_out = refs
    half = mine.shape[0]
    for part, core in ((mine, info[3]), (other, 1 - info[3])):
        input_grad[pl.ds(pl.multiple_of(core * half, 8), half), :] = part[...].astype(F32)
    rows = pieces[0].shape[0]
    for r, piece in enumerate(pieces):
        layer_out[pl.ds(pl.multiple_of((info[4] ^ r) * rows, 16), rows), :] = piece[...]


def finish_kernel(order, *refs):
    *pieces, projector_t, combiner, expander, reducer = refs
    copies = jnp.concatenate([piece[...] for piece in pieces], axis=0)
    copies = dot(order[...], copies).astype(BF)
    cl = combiner.shape[0]
    fl = reducer.shape[0]
    for i in range(3):
        projector_t[i] = flip(copies[:, i * cl : (i + 1) * cl])
    combiner[...] = flip(copies[:, 3 * cl : 4 * cl])
    expander[...] = copies[:, 4 * cl : 4 * cl + fl]
    reducer[...] = flip(copies[:, 4 * cl + fl : 4 * cl + 2 * fl])


def body(
    tokens,
    cotangent,
    lengths,
    projector,
    projector_mean,
    projector_square,
    combiner,
    combiner_mean,
    combiner_square,
    expander,
    expander_mean,
    expander_square,
    reducer,
    reducer_mean,
    reducer_square,
    affines,
    affines_mean,
    affines_square,
):
    mp = lax.axis_size("mp")
    dp = lax.axis_size("dp")
    me = lax.axis_index("mp")
    seq = tokens.shape[0]
    if lengths.shape[0] != 1 or mp & (mp - 1):
        raise ValueError("unsupported mesh")
    rows = seq // mp
    dl = expander.shape[0]
    cl = projector.shape[2]
    fl = expander.shape[1]
    bw = 4 * cl
    heads = cl // HD
    chunk = 256
    spot = lax.axis_index("dp")
    me, spot = me.astype(jnp.int32), spot.astype(jnp.int32)
    info = jnp.stack([lengths[0], me * rows, spot, me & 1, me])

    def swap(x, bit, axis="mp"):
        return lax.ppermute(x, axis, [(i, i ^ bit) for i in range(lax.axis_size(axis))])

    pack_width = bw + 2 * fl + LANES
    shares = [projector, combiner.T, expander, reducer.T, affines]
    [pack] = pl.pallas_call(
        pack_kernel,
        out_shape=[jax.ShapeDtypeStruct((dl, pack_width), BF)],
        in_specs=[pl.BlockSpec(memory_space=pltpu.HBM)] * len(shares),
        out_specs=[pl.BlockSpec(memory_space=pltpu.VMEM)],
        scratch_shapes=[
            *(pltpu.VMEM(x.shape, x.dtype) for x in shares),
            pltpu.SemaphoreType.DMA((len(shares),)),
        ],
        interpret=INTERPRET,
    )(*(pltpu.with_memory_space_constraint(x, pltpu.HBM) for x in shares))
    names = list(range(mp))
    near, far = names[:2], names[2:]
    chip_bits = [1 << i for i in range(1, mp.bit_length() - 1)]
    down = chip_bits[::-1]
    line_bits = [1 << i for i in range(1, dp.bit_length() - 1)]
    tokens_in, query_in, tokens_t, query_t, order = call(
        lambda *refs: prepare_kernel(dp, *refs),
        [((seq, D), BF)] * 2 + [((D, seq), BF)] * 2 + [((D, D), BF)],
        info,
        tokens,
        scratch=[((seq, D), BF)],
        smem=1,
    )
    small = jnp.stack([affines, affines_mean, affines_square])
    line = [pack]
    for bit in line_bits[::-1]:
        line += [swap(x, bit, "dp") for x in line]
    line[-1], order, small = lax.optimization_barrier((line[-1], order, small))
    pack = jnp.concatenate(line, axis=0)

    def cross(part):
        halves = {0: part}
        for bit in chip_bits:
            for r in list(halves):
                halves[r ^ bit] = swap(halves[r], bit)
        return halves

    def pair(blocks, group):
        for r in group:
            blocks[r ^ 1] = [swap(x, 1) for x in blocks[r]]

    attention_half, feed_half = pack[:, :bw], pack[:, bw:]
    upper = cross(attention_half)
    attention_blocks = {r: [x, swap(x, 1, "dp")] for r, x in upper.items()}
    feed_upper = cross(feed_half)
    feed_other, attention_blocks[0][1], attention_blocks[2][0] = lax.optimization_barrier(
        (swap(feed_half, 1, "dp"), attention_blocks[0][1], attention_blocks[2][0])
    )
    feed_lower = cross(feed_other)
    feed_blocks = {r: [feed_upper[r], feed_lower[r]] for r in feed_upper}
    pair(attention_blocks, names[:1])
    pair(feed_blocks, names[:1])

    def attend(group):
        made = call(
            lambda *refs: attend_kernel(len(group), chunk, *refs),
            [
                ((seq, bw), BF),
                ((bw, seq), BF),
                ((cl, rows), BF),
                ((cl, rows), F32),
                ((heads, rows), F32),
                ((heads, seq, rows), BF),
            ]
            * len(group),
            info,
            tokens_in,
            query_in,
            *(x for r in group for x in attention_blocks[r]),
            scratch=[((len(group) * heads, seq, rows), F32)],
            smem=1,
            flops=4 * len(group) * (heads + 1) * seq * rows * D,
        )
        return {r: list(made[6 * i : 6 * i + 6]) for i, r in enumerate(group)}

    kept = attend(near)
    for r in far[::2]:
        attention_blocks[r][1], kept[0][3] = lax.optimization_barrier(
            (attention_blocks[r][1], kept[0][3])
        )
    pair(attention_blocks, far[::2])
    for r in far[::2]:
        feed_blocks[r], attention_blocks[r ^ 1] = lax.optimization_barrier(
            (feed_blocks[r], attention_blocks[r ^ 1])
        )
    pair(feed_blocks, far[::2])
    kept.update(attend(far))
    own_out, grad_one, *feed_grads = call(
        lambda *refs: feed_kernel(mp, *refs),
        [((rows, D), BF), ((rows, D), F32)]
        + [((D // 2, 2 * fl + LANES), BF)] * (2 * mp),
        info,
        tokens_in,
        cotangent,
        order,
        *(kept[r][3] for r in names),
        *(x for r in names for x in attention_blocks[r]),
        *(x for r in names for x in feed_blocks[r]),
        scratch=[((mp, rows, fl), F32), ((mp, rows, fl), BF)],
        smem=1,
        flops=12 * mp * rows * D * fl,
    )

    def attend_back(group, earlier=(), last=False):
        return call(
            lambda *refs: attend_back_kernel(len(group), chunk, not earlier, last, *refs),
            [((D, bw), BF)] * len(group)
            + ([((seq // 2, D), BF)] * 2 if last else [((seq, D), F32)]),
            info,
            query_in,
            tokens_t,
            query_t,
            grad_one,
            order,
            *(x for r in group for x in (*attention_blocks[r], *kept[r])),
            *earlier,
            scratch=[((heads, seq, rows), BF), ((seq, bw), F32), ((seq, D), F32)],
            smem=1,
            flops=8 * len(group) * (heads + 1) * seq * rows * D,
        )

    def reduce_blocks(left, order):
        left = dict(left)
        for bit in order:
            for r in sorted({r & ~bit for r in left if r & bit}):
                came = swap(left.pop(r ^ bit), bit)
                left[r] = left[r] + came if r in left else came
        return left

    down = chip_bits[::-1]
    own_side, other_side = (
        reduce_blocks(zip(names, feed_grads[i::2], strict=True), [1]) for i in range(2)
    )
    other_side, grad_one = lax.optimization_barrier((other_side, grad_one))
    other_side = reduce_blocks(other_side, down)[0]
    *far_grads, side_grad, near_part = attend_back([*far, near[1]])
    far_grads = reduce_blocks(zip(far, far_grads, strict=True), [1])
    far_grads, other_side, own_side, near_part = lax.optimization_barrier(
        (far_grads, other_side, own_side, near_part)
    )
    far_grads = reduce_blocks(far_grads, down)[0]
    own_side = reduce_blocks(own_side, down[:-1])
    came = [swap(other_side, 1, "dp"), *(swap(own_side[r], r) for r in down[-1:])]
    [own_grad, mine, theirs] = attend_back(near[:1], (near_part,), last=True)
    near_grads = own_grad + swap(side_grad, 1) + far_grads
    half = D // 2
    shares = call(
        lambda *refs: merge_kernel(dp // 2, *refs),
        [((dl, pack_width), BF)] * (dp // 2),
        near_grads[:half],
        swap(near_grads[half:], 1, "dp"),
        own_side[0],
        *came,
    )
    first, *others = shares
    theirs, first = lax.optimization_barrier((theirs, first))
    shares = [first, *others]
    mine = mine + swap(theirs, 1)
    sums = shares[:1]
    for bit in line_bits:
        half = len(shares) // 2
        arrived = [swap(x, bit, "dp") for x in shares[half:]]
        sums.append(arrived[0])
        shares = [shares[0], *(x + y for x, y in zip(shares[1:half], arrived[1:], strict=True))]
    arrived = sums[-1]
    masters = (
        (projector, projector_mean, projector_square),
        (combiner.T, combiner_mean.T, combiner_square.T),
        (expander, expander_mean, expander_square),
        (reducer.T, reducer_mean.T, reducer_square.T),
    )
    rates = (
        (D ** (-0.5), 0.0001),
        (max(1, D * 8 // SEQ) ** (-0.5), 0.0001),
        (D ** (-0.5), 0.0001),
        (FF ** (-0.5), 0.0001),
        (0.4, 0.0),
    )
    flat = [x for three in masters for x in three]
    *fresh, fresh_small, new_pack = call(
        lambda *refs: update_kernel(rates, len(sums), *refs),
        [(x.shape, F32) for x in (*flat, small)] + [((dl, bw + 2 * fl), BF)],
        *sums,
        *flat,
        small,
    )
    copies = [new_pack]
    for bit in line_bits[::-1]:
        copies += [swap(x, bit, "dp") for x in copies]
    copies += [swap(x, 1, "dp") for x in copies]
    own_out, _ = lax.optimization_barrier((own_out, arrived))
    pieces = {0: own_out}
    for bit in chip_bits:
        mine = mine + swap(mine, bit)
        for r in list(pieces):
            pieces[r ^ bit] = swap(pieces[r], bit)
    late = {r: lax.optimization_barrier((x, copies[2]))[0] if r else x for r, x in pieces.items()}
    for r, x in late.items():
        pieces[r], pieces[r ^ 1] = x, swap(x, 1)
    mine, _ = lax.optimization_barrier((mine, copies[2]))
    input_grad, layer_out = call(
        assemble_kernel,
        [((seq, D), F32), ((seq, D), BF)],
        info,
        mine,
        swap(mine, 1),
        *(pieces[r] for r in names),
        smem=1,
    )
    copies[-1], input_grad = lax.optimization_barrier((copies[-1], input_grad))
    projector_copy, combiner_copy, expander_copy, reducer_copy = call(
        finish_kernel,
        [((3, cl, D), BF), ((cl, D), BF), ((D, fl), BF), ((fl, D), BF)],
        order,
        *copies,
    )
    for i in (3, 4, 5, 9, 10, 11):
        fresh[i] = fresh[i].T
    return (
        layer_out,
        input_grad,
        *fresh,
        *fresh_small,
        jnp.swapaxes(projector_copy, 1, 2),
        combiner_copy,
        expander_copy,
        reducer_copy,
    )


def solution(mesh):
    rows = P("dp", None)
    by_weight = [P(None, "dp", "mp"), P("mp", "dp"), P("dp", "mp"), P("mp", "dp"), P(None, "dp")]
    threes = [spec for spec in by_weight for _ in range(3)]
    return jax.shard_map(
        body,
        mesh=mesh,
        in_specs=(rows, rows, P("dp"), *threes),
        out_specs=(
            rows,
            rows,
            *threes,
            P(None, None, "mp"),
            P("mp", None),
            P(None, "mp"),
            P("mp", None),
        ),
        check_vma=False,
    )
```

```python
import math

import jax
import jax.numpy as jnp
from jax import lax
from jax.experimental import pallas as pl
from jax.experimental.pallas import tpu as pltpu
from jax.sharding import PartitionSpec as P

D = 256
FF = 2048
HD = 32
SEQ = 1024
WROW = 32
STEP = 5
LANES = 128
LOG2E = 1.4426950408889634
INTERPRET = False
BF = jnp.bfloat16
F32 = jnp.float32


def dot(a, b):
    return jnp.dot(a, b, preferred_element_type=F32)


def dot_nt(a, b):
    return lax.dot_general(a, b, (((1,), (1,)), ((), ())), preferred_element_type=F32)


def flip(x):
    return x.T


def lane_of(shape):
    return lax.broadcasted_iota(jnp.int32, shape, 1)


def row_of(shape):
    return lax.broadcasted_iota(jnp.int32, shape, 0)


def place_rows(x, start, total):
    parts = []
    if start:
        parts.append(jnp.zeros((start, x.shape[1]), x.dtype))
    parts.append(x)
    if total - start - x.shape[0]:
        parts.append(jnp.zeros((total - start - x.shape[0], x.shape[1]), x.dtype))
    return jnp.concatenate(parts, axis=0) if len(parts) > 1 else x


def call(kernel, outs, *args, scratch=(), smem=0, flops=0):
    vm = pl.BlockSpec(memory_space=pltpu.VMEM)
    sm = pl.BlockSpec(memory_space=pltpu.SMEM)
    return pl.pallas_call(
        kernel,
        out_shape=[jax.ShapeDtypeStruct(s, d) for s, d in outs],
        in_specs=[sm] * smem + [vm] * (len(args) - smem),
        out_specs=[vm] * len(outs),
        scratch_shapes=[pltpu.VMEM(s, d) for s, d in scratch],
        cost_estimate=pl.CostEstimate(flops=flops, transcendentals=0, bytes_accessed=0)
        if flops
        else None,
        compiler_params=pltpu.CompilerParams(vmem_limit_bytes=24 * 2**20),
        interpret=INTERPRET,
    )(*args)


def pack_kernel(*refs):
    given, pack, held, arrived = refs[:5], refs[5], refs[6:11], refs[11]
    fetches = [
        pltpu.make_async_copy(source, target, arrived.at[i])
        for i, (source, target) in enumerate(zip(given, held, strict=True))
    ]
    for fetch in fetches:
        fetch.start()
    projector, combiner_t, expander, reducer_t, affines = held
    dl, fl = expander.shape
    cl = combiner_t.shape[1]
    for fetch in fetches:
        fetch.wait()
    gains = jnp.concatenate([affines[...], jnp.zeros((LANES - 4, dl), F32)], axis=0).T
    high = gains.astype(BF).astype(F32)
    rest = pltpu.roll(gains - high, 4, 1)
    tail = jnp.where(lane_of(high.shape) < 4, high, rest).astype(BF)
    low = [projector[i].astype(BF) for i in range(3)] + [combiner_t[...].astype(BF)]
    pack[:, : 4 * cl] = jnp.concatenate(low, axis=1)
    pack[:, 4 * cl : 4 * cl + fl] = expander[...].astype(BF)
    pack[:, 4 * cl + fl : 4 * cl + 2 * fl] = reducer_t[...].astype(BF)
    pack[:, 4 * cl + 2 * fl :] = tail


def prepare_kernel(shares, info, tokens, tokens_out, query_in, tokens_t, query_t, order, whole):
    seq, width = tokens.shape
    half = width // 2
    rows = seq // WROW
    shape = (max(rows, WROW), half)
    channel = lane_of(shape)
    exponent = (2 * (channel // 2)).astype(F32) / half
    angles = (row_of(shape) + 1).astype(F32) * jnp.exp(-math.log(10000.0) * exponent)
    table = jnp.where(channel % 2 == 0, jnp.sin(angles), jnp.cos(angles))
    for i in range(rows):
        lower = i * WROW
        spot = jnp.concatenate(
            [jnp.broadcast_to(table[i : i + 1], (WROW, half)), table[:WROW]], axis=1
        )
        part = tokens[lower : lower + WROW, :].astype(F32) + spot
        whole[lower : lower + WROW, :] = part.astype(BF)
    share = width // shares
    bits = shares.bit_length() - 1
    place = lane_of((width, width))
    slot = place // share
    source = jnp.zeros_like(slot)
    for k in range(bits):
        source = source + (((slot >> k) & 1) << (bits - 1 - k))
    source = (source ^ info[2]) * share + place % share
    order[...] = jnp.where(row_of((width, width)) == source, 1.0, 0.0).astype(BF)
    for source_ref, out, out_t in ((whole, query_in, query_t), (tokens, tokens_out, tokens_t)):
        moved = dot(source_ref[...], order[...]).astype(BF)
        out[...] = moved
        out_t[...] = flip(moved)


def stack(upper, lower):
    return jnp.concatenate([upper[...], lower[...]], axis=0)


def attend_kernel(blocks, chunk, info, tokens, query_in, *refs):
    ins, outs, scores = refs[: 2 * blocks], refs[2 * blocks : -1], refs[-1]
    seq = tokens.shape[0]
    length, offset = info[0], info[1]
    fold = HD**-0.5 * LOG2E
    whole = [stack(*ins[2 * b : 2 * b + 2]) for b in range(blocks)]
    bw = whole[0].shape[1]
    cl = bw // 4
    mid = 2 * cl
    from_query = dot(query_in[...], jnp.concatenate([x[:, :mid] for x in whole], axis=1))
    from_token = dot(tokens[...], jnp.concatenate([x[:, mid:] for x in whole], axis=1))
    dead = jnp.where(row_of((seq, 1)) < length, 0.0, 1.0)
    work = []
    for b in range(blocks):
        block = whole[b]
        z, z_t, q_t, context_t, inverse, raised = outs[6 * b : 6 * b + 6]
        rows = q_t.shape[1]
        left = from_query[:, b * mid : (b + 1) * mid]
        z[:, :mid] = jnp.where(lane_of((1, mid)) == 0, dead, left).astype(BF)
        z[:, mid:] = from_token[:, b * mid : (b + 1) * mid].astype(BF)
        own = query_in[pl.ds(pl.multiple_of(offset, 8), rows), :]
        q_all = flip(dot(own, block).astype(BF))
        q_t[...] = q_all[:cl]
        z_t[...] = flip(z[...])
        for h in range(cl // HD):
            lower = h * HD
            side = place_rows(q_all[lower : lower + HD], cl + lower, bw)
            side = jnp.where(row_of(side.shape) == 0, -1e30, side.astype(F32)).astype(BF)
            work.append((b, h, side))
    def score(i):
        b, h, side = work[i]
        z = outs[6 * b]
        peak = jnp.full((1, rows), -jnp.inf, F32)
        for c in range(0, seq, chunk):
            part = dot(z[c : c + chunk, :], side)
            scores[i, c : c + chunk, :] = part
            peak = jnp.maximum(peak, jnp.max(part, axis=0, keepdims=True))
        return peak

    def mix(i):
        b, h, side = work[i]
        z, z_t, q_t, context_t, inverse, raised = outs[6 * b : 6 * b + 6]
        lower = h * HD
        mixed = dot(z_t[2 * cl + lower : 2 * cl + lower + HD, :], raised[h])
        context_t[lower : lower + HD, :] = mixed * inverse[h : h + 1, :]

    peak = score(0)
    for i, (b, h, side) in enumerate(work):
        inverse, raised = outs[6 * b + 4 : 6 * b + 6]
        after = score(i + 1) if i + 1 < len(work) else None
        total = jnp.zeros((1, rows), F32)
        for c in range(0, seq, chunk):
            part = jnp.exp2((scores[i, c : c + chunk, :] - peak) * fold)
            total = total + jnp.sum(part, axis=0, keepdims=True)
            raised[h, c : c + chunk, :] = part.astype(BF)
        inverse[h : h + 1, :] = 1.0 / total
        peak = after
        if i:
            mix(i - 1)
    mix(len(work) - 1)


def norm(x):
    average = jnp.mean(x, axis=-1, keepdims=True)
    centred = x - average
    scale = lax.rsqrt(jnp.mean(centred * centred, axis=-1, keepdims=True) + 1e-05)
    return centred * scale, scale


def norm_back(grad, unit, scale, gains):
    inner = grad * gains
    mean_one = jnp.mean(inner, axis=-1, keepdims=True)
    mean_two = jnp.mean(inner * unit, axis=-1, keepdims=True)
    back = scale * (inner - mean_one - unit * mean_two)
    gain_grad = jnp.sum(grad * unit, axis=0, keepdims=True)
    bias_grad = jnp.sum(grad, axis=0, keepdims=True)
    return back, gain_grad, bias_grad


def feed_kernel(blocks, info, tokens, cotangent, *refs):
    order, contexts, pairs = refs[0], refs[1 : blocks + 1], refs[blocks + 1 : 5 * blocks + 1]
    attention_pairs, feed_pairs = pairs[: 2 * blocks], pairs[2 * blocks :]
    layer_out, grad_one, *grads = refs[5 * blocks + 1 : 7 * blocks + 3]
    slopes, hidden_all = refs[7 * blocks + 3 :]
    attention_blocks = [stack(*attention_pairs[2 * b : 2 * b + 2]) for b in range(blocks)]
    halves = [feed_pairs[2 * b : 2 * b + 2] for b in range(blocks)]
    rows, width = layer_out.shape
    length, offset = info[0], pl.multiple_of(info[1], 8)
    bw = attention_blocks[0].shape[1]
    cl = bw // 4
    fl = (feed_pairs[0].shape[1] - LANES) // 2
    half = width // 2
    first_blocks = [stack(up.at[:, :fl], low.at[:, :fl]) for up, low in halves]
    second_blocks = [stack(up.at[:, fl : 2 * fl], low.at[:, fl : 2 * fl]) for up, low in halves]
    own = tokens[pl.ds(offset, rows), :].astype(F32)
    context = flip(jnp.concatenate([ref[...].astype(BF) for ref in contexts], axis=0))
    combiner = jnp.concatenate([attention_blocks[b][:, 3 * cl :] for b in range(blocks)], axis=1)
    attention = dot_nt(context, combiner)
    tail = [x[:, 2 * fl :].astype(F32) for x in halves[0]]
    pieces = jnp.concatenate(tail, axis=0).T
    gain_one, bias_one, gain_two, bias_two = (
        pieces[i : i + 1] + pieces[i + 4 : i + 5] for i in range(4)
    )
    unit_one, scale_one = norm(own + attention)
    first = unit_one * gain_one + bias_one
    first_low = first.astype(BF)
    feed = jnp.zeros((rows, width), F32)
    after = dot(first_low, first_blocks[0])
    for b in range(blocks):
        pre = after
        if b + 1 < blocks:
            after = dot(first_low, first_blocks[b + 1])
        square = pre * pre
        half_pre = 0.5 * pre
        bend = jnp.tanh(pre * (0.7978845608 + 0.035677408 * square))
        hidden = (half_pre + half_pre * bend).astype(BF)
        steep = 0.7978845608 + 0.107032224 * square
        slopes[b] = (0.5 + 0.5 * bend) + half_pre * (1.0 - bend * bend) * steep
        hidden_all[b] = hidden
        feed = feed + dot_nt(hidden, second_blocks[b])
    unit_two, scale_two = norm(first + feed)
    layer_out[...] = dot_nt((unit_two * gain_two + bias_two).astype(BF), order[...]).astype(BF)
    live = (row_of((rows, width)) + offset) < length
    seed = jnp.where(live, dot(cotangent[pl.ds(offset, rows), :], order[...]), 0.0)
    grad_two, d_gain_two, d_bias_two = norm_back(seed, unit_two, scale_two, gain_two)
    grad_two_low = grad_two.astype(BF)
    grad_two_t = flip(grad_two_low)
    first_t = flip(first_low)
    grad_first = grad_two
    after = dot(grad_two_low, second_blocks[0])
    for b in range(blocks):
        grad_hidden = after
        if b + 1 < blocks:
            after = dot(grad_two_low, second_blocks[b + 1])
        grad_pre = (grad_hidden * slopes[b]).astype(BF)
        for side in range(2):
            part = slice(side * half, (side + 1) * half)
            out = grads[2 * b + side]
            out[:, :fl] = dot(first_t[part], grad_pre).astype(BF)
            out[:, fl : 2 * fl] = dot(grad_two_t[part], hidden_all[b]).astype(BF)
        grad_first = grad_first + dot_nt(grad_pre, first_blocks[b])
    back, d_gain_one, d_bias_one = norm_back(grad_first, unit_one, scale_one, gain_one)
    grad_one[...] = back
    stacked = jnp.concatenate(
        [d_gain_one, d_bias_one, d_gain_two, d_bias_two, jnp.zeros((LANES - 4, width), F32)], axis=0
    )
    columns = stacked.T.astype(BF)
    for b in range(blocks):
        grads[2 * b][:, 2 * fl :] = columns[:half]
        grads[2 * b + 1][:, 2 * fl :] = columns[half:]


def attend_back_kernel(blocks, chunk, first, last, info, query_in, tokens_t, query_t, grad_one, *refs):
    made = blocks + 4 + last
    order, ins = refs[0], refs[1 : 8 * blocks + 1]
    rest = refs[8 * blocks + 1 :]
    earlier = None if first else rest[0]
    seq, width = query_in.shape
    score_grads, total, moved = rest[-3:]
    outs = rest[len(rest) - made : -3]
    rows = grad_one.shape[0]
    offset = pl.multiple_of(info[1], 8)
    scaling = HD**-0.5
    grad_low = grad_one[...].astype(BF)
    bw = ins[2].shape[1]
    cl = bw // 4
    mid = 2 * cl
    heads = range(cl // HD)
    sources = jnp.concatenate([flip(query_in[pl.ds(offset, rows), :]), flip(grad_low)], axis=1)
    own_total = flip(grad_one[...]) if earlier is None else jnp.zeros((width, rows), F32)
    ready = []
    for b in range(blocks):
        upper, lower_half, z, _, _, context_ref, inverse, _ = ins[8 * b : 8 * b + 8]
        block = stack(upper, lower_half)
        grad_context_t = dot(grad_low, block).T[3 * cl :]
        scaled = [
            (grad_context_t[h * HD : (h + 1) * HD] * inverse[h : h + 1, :]).astype(BF)
            for h in heads
        ]
        deltas = [
            jnp.sum(
                scaled[h].astype(F32) * context_ref[h * HD : (h + 1) * HD, :], axis=0, keepdims=True
            )
            for h in heads
        ]
        ready.append((block, scaled, deltas))

    def slope(b):
        z, raised = ins[8 * b + 2], ins[8 * b + 7]
        _, scaled, deltas = ready[b]
        for h in heads:
            side = place_rows(scaled[h], mid + h * HD, bw)
            for c in range(0, seq, chunk):
                weights = raised[h, c : c + chunk, :].astype(F32)
                slopes = weights * (dot(z[c : c + chunk, :], side) - deltas[h])
                score_grads[b, h, c : c + chunk, :] = slopes.astype(BF)

    def close(b):
        z_t, q_t, context_ref, raised = (ins[8 * b + i] for i in (3, 4, 5, 7))
        block, scaled, _ = ready[b]
        keys = [dot_nt(q_t[h * HD : (h + 1) * HD, :], score_grads[b, h]) * scaling for h in heads]
        values = [dot_nt(scaled[h], raised[h]) for h in heads]
        query_grads = [
            dot(z_t[cl + h * HD : cl + (h + 1) * HD, :], score_grads[b, h]) * scaling for h in heads
        ]
        edge = jnp.zeros((cl, seq), BF)
        keys = jnp.concatenate([edge, *(x.astype(BF) for x in keys)], axis=0)
        values = jnp.concatenate([*(x.astype(BF) for x in values), edge], axis=0)
        of_query = dot_nt(query_t[...], keys)
        of_token = dot_nt(tokens_t[...], values)
        part = dot(block, jnp.concatenate([keys, values], axis=0))
        if b:
            part = part + total[...]
        elif earlier is not None:
            part = part + earlier[...]
        total[...] = part
        query_grad = place_rows(jnp.concatenate(query_grads, axis=0).astype(BF), 0, bw)
        context = place_rows(context_ref[...].astype(BF), 3 * cl, bw)
        weight_grad = dot_nt(sources, jnp.concatenate([query_grad, context], axis=1))
        outs[b][:, :mid] = (weight_grad[:, :mid] + of_query).astype(BF)
        outs[b][:, mid:] = (weight_grad[:, mid:] + of_token).astype(BF)
        return dot(block, query_grad)

    slope(0)
    for b in range(1, blocks):
        slope(b)
        own_total = own_total + close(b - 1)
    own_total = own_total + close(blocks - 1)
    own_lanes = pl.ds(pl.multiple_of(info[1], LANES), rows)
    total[:, own_lanes] = total[:, own_lanes] + own_total
    if not last:
        outs[-1][...] = total[...]
        return
    moved[...] = flip(dot(order[...], total[...].astype(BF)).astype(BF))
    half = seq // 2
    for out, core in zip(outs[-2:], (info[3], 1 - info[3]), strict=True):
        out[...] = moved[pl.ds(pl.multiple_of(core * half, 16), half), :]


def merge_kernel(shares, *refs):
    ins, outs = refs[:-shares], refs[-shares:]
    bw = ins[0].shape[1]
    rows = outs[0].shape[0]
    low, high = ([x[...].astype(F32) for x in group] for group in (ins[:2], ins[2:]))
    low, high = low[0] + low[1], sum(high[1:], high[0])
    for i, out in enumerate(outs):
        part = slice(i * rows, (i + 1) * rows)
        out[:, :bw] = low[part].astype(BF)
        out[:, bw:] = high[part].astype(BF)


def adamw(weight, moment_one, moment_two, grad, step_rate, decay_rate):
    mean_next = 0.5 * moment_one + 0.5 * grad
    square_next = 0.5 * moment_two + 0.5 * grad * grad
    correct = 1.0 - 0.5**STEP
    direction = mean_next / correct / (jnp.sqrt(square_next / correct) + 1e-08)
    weight_next = weight - step_rate * (direction + decay_rate * weight)
    return (weight_next, mean_next, square_next)


def update_kernel(rates, count, *refs):
    grad = sum((x[...].astype(F32) for x in refs[1:count]), refs[0][...].astype(F32))
    refs = refs[count:]
    ins, outs, pack = refs[:13], refs[13:26], refs[26]
    cl = ins[0].shape[2]
    fl = ins[6].shape[1]
    fresh = []
    for i in range(3):
        fresh.append(
            adamw(*(ins[k][i] for k in range(3)), grad[:, i * cl : (i + 1) * cl], *rates[0])
        )
        for k in range(3):
            outs[k][i] = fresh[-1][k]
    start = 3 * cl
    for j, size in ((1, cl), (2, fl), (3, fl)):
        fresh.append(
            adamw(*(ins[3 * j + k][...] for k in range(3)), grad[:, start : start + size], *rates[j])
        )
        for k in range(3):
            outs[3 * j + k][...] = fresh[-1][k]
        start += size
    small = grad[:, start:].T[:4]
    for k, value in enumerate(adamw(*(ins[12][k] for k in range(3)), small, *rates[4])):
        outs[12][k] = value
    whole = jnp.concatenate([new[0].astype(BF) for new in fresh], axis=1)
    pack[...] = whole


def assemble_kernel(info, mine, other, *refs):
    *pieces, input_grad, layer_out = refs
    half = mine.shape[0]
    for part, core in ((mine, info[3]), (other, 1 - info[3])):
        input_grad[pl.ds(pl.multiple_of(core * half, 8), half), :] = part[...].astype(F32)
    rows = pieces[0].shape[0]
    for r, piece in enumerate(pieces):
        layer_out[pl.ds(pl.multiple_of((info[4] ^ r) * rows, 16), rows), :] = piece[...]


def finish_kernel(order, *refs):
    *pieces, projector_t, combiner, expander, reducer = refs
    copies = jnp.concatenate([piece[...] for piece in pieces], axis=0)
    copies = dot(order[...], copies).astype(BF)
    cl = combiner.shape[0]
    fl = reducer.shape[0]
    for i in range(3):
        projector_t[i] = flip(copies[:, i * cl : (i + 1) * cl])
    combiner[...] = flip(copies[:, 3 * cl : 4 * cl])
    expander[...] = copies[:, 4 * cl : 4 * cl + fl]
    reducer[...] = flip(copies[:, 4 * cl + fl : 4 * cl + 2 * fl])


def body(
    tokens,
    cotangent,
    lengths,
    projector,
    projector_mean,
    projector_square,
    combiner,
    combiner_mean,
    combiner_square,
    expander,
    expander_mean,
    expander_square,
    reducer,
    reducer_mean,
    reducer_square,
    affines,
    affines_mean,
    affines_square,
):
    mp = lax.axis_size("mp")
    dp = lax.axis_size("dp")
    me = lax.axis_index("mp")
    seq = tokens.shape[0]
    if lengths.shape[0] != 1 or mp & (mp - 1):
        raise ValueError("unsupported mesh")
    rows = seq // mp
    dl = expander.shape[0]
    cl = projector.shape[2]
    fl = expander.shape[1]
    bw = 4 * cl
    heads = cl // HD
    chunk = 256
    spot = lax.axis_index("dp")
    me, spot = me.astype(jnp.int32), spot.astype(jnp.int32)
    info = jnp.stack([lengths[0], me * rows, spot, me & 1, me])

    def swap(x, bit, axis="mp"):
        return lax.ppermute(x, axis, [(i, i ^ bit) for i in range(lax.axis_size(axis))])

    pack_width = bw + 2 * fl + LANES
    shares = [projector, combiner.T, expander, reducer.T, affines]
    [pack] = pl.pallas_call(
        pack_kernel,
        out_shape=[jax.ShapeDtypeStruct((dl, pack_width), BF)],
        in_specs=[pl.BlockSpec(memory_space=pltpu.HBM)] * len(shares),
        out_specs=[pl.BlockSpec(memory_space=pltpu.VMEM)],
        scratch_shapes=[
            *(pltpu.VMEM(x.shape, x.dtype) for x in shares),
            pltpu.SemaphoreType.DMA((len(shares),)),
        ],
        interpret=INTERPRET,
    )(*(pltpu.with_memory_space_constraint(x, pltpu.HBM) for x in shares))
    names = list(range(mp))
    near, far = names[:2], names[2:]
    chip_bits = [1 << i for i in range(1, mp.bit_length() - 1)]
    down = chip_bits[::-1]
    line_bits = [1 << i for i in range(1, dp.bit_length() - 1)]
    tokens_in, query_in, tokens_t, query_t, order = call(
        lambda *refs: prepare_kernel(dp, *refs),
        [((seq, D), BF)] * 2 + [((D, seq), BF)] * 2 + [((D, D), BF)],
        info,
        tokens,
        scratch=[((seq, D), BF)],
        smem=1,
    )
    small = jnp.stack([affines, affines_mean, affines_square])
    line = [pack]
    for bit in line_bits[::-1]:
        line += [swap(x, bit, "dp") for x in line]
    line[-1], order, small = lax.optimization_barrier((line[-1], order, small))
    pack = jnp.concatenate(line, axis=0)

    def cross(part):
        halves = {0: part}
        for bit in chip_bits:
            for r in list(halves):
                halves[r ^ bit] = swap(halves[r], bit)
        return halves

    def pair(blocks, group):
        for r in group:
            blocks[r ^ 1] = [swap(x, 1) for x in blocks[r]]

    attention_half, feed_half = pack[:, :bw], pack[:, bw:]
    upper = cross(attention_half)
    attention_blocks = {r: [x, swap(x, 1, "dp")] for r, x in upper.items()}
    feed_upper = cross(feed_half)
    feed_other, attention_blocks[0][1], attention_blocks[2][0] = lax.optimization_barrier(
        (swap(feed_half, 1, "dp"), attention_blocks[0][1], attention_blocks[2][0])
    )
    feed_lower = cross(feed_other)
    feed_blocks = {r: [feed_upper[r], feed_lower[r]] for r in feed_upper}
    pair(attention_blocks, names[:1])
    pair(feed_blocks, names[:1])

    def attend(group):
        made = call(
            lambda *refs: attend_kernel(len(group), chunk, *refs),
            [
                ((seq, bw), BF),
                ((bw, seq), BF),
                ((cl, rows), BF),
                ((cl, rows), F32),
                ((heads, rows), F32),
                ((heads, seq, rows), BF),
            ]
            * len(group),
            info,
            tokens_in,
            query_in,
            *(x for r in group for x in attention_blocks[r]),
            scratch=[((len(group) * heads, seq, rows), F32)],
            smem=1,
            flops=4 * len(group) * (heads + 1) * seq * rows * D,
        )
        return {r: list(made[6 * i : 6 * i + 6]) for i, r in enumerate(group)}

    kept = attend(near)
    for r in far[::2]:
        attention_blocks[r][1], kept[0][3] = lax.optimization_barrier(
            (attention_blocks[r][1], kept[0][3])
        )
    pair(attention_blocks, far[::2])
    for r in far[::2]:
        feed_blocks[r], attention_blocks[r ^ 1] = lax.optimization_barrier(
            (feed_blocks[r], attention_blocks[r ^ 1])
        )
    pair(feed_blocks, far[::2])
    kept.update(attend(far))
    own_out, grad_one, *feed_grads = call(
        lambda *refs: feed_kernel(mp, *refs),
        [((rows, D), BF), ((rows, D), F32)]
        + [((D // 2, 2 * fl + LANES), BF)] * (2 * mp),
        info,
        tokens_in,
        cotangent,
        order,
        *(kept[r][3] for r in names),
        *(x for r in names for x in attention_blocks[r]),
        *(x for r in names for x in feed_blocks[r]),
        scratch=[((mp, rows, fl), F32), ((mp, rows, fl), BF)],
        smem=1,
        flops=12 * mp * rows * D * fl,
    )

    def attend_back(group, earlier=(), last=False):
        return call(
            lambda *refs: attend_back_kernel(len(group), chunk, not earlier, last, *refs),
            [((D, bw), BF)] * len(group)
            + ([((seq // 2, D), BF)] * 2 if last else [((D, seq), F32)]),
            info,
            query_in,
            tokens_t,
            query_t,
            grad_one,
            order,
            *(x for r in group for x in (*attention_blocks[r], *kept[r])),
            *earlier,
            scratch=[((len(group), heads, seq, rows), BF), ((D, seq), F32), ((seq, D), BF)],
            smem=1,
            flops=8 * len(group) * (heads + 1) * seq * rows * D,
        )

    def reduce_blocks(left, order):
        left = dict(left)
        for bit in order:
            for r in sorted({r & ~bit for r in left if r & bit}):
                came = swap(left.pop(r ^ bit), bit)
                left[r] = left[r] + came if r in left else came
        return left

    down = chip_bits[::-1]
    own_side, other_side = (dict(zip(names, feed_grads[i::2], strict=True)) for i in range(2))
    far_side = reduce_blocks({r: other_side[r] for r in far}, [1])
    far_side, grad_one = lax.optimization_barrier((far_side, grad_one))
    near_side = reduce_blocks({r: other_side[r] for r in near}, [1])
    own_side = reduce_blocks(own_side, [1])
    other_side = reduce_blocks({**far_side, **near_side}, down)[0]
    *far_grads, side_grad, near_part = attend_back([*far, near[1]])
    far_grads = reduce_blocks(zip(far, far_grads, strict=True), [1])
    far_grads, other_side, own_side, near_part = lax.optimization_barrier(
        (far_grads, other_side, own_side, near_part)
    )
    far_grads = reduce_blocks(far_grads, down)[0]
    own_side = reduce_blocks(own_side, down[:-1])
    came = [swap(other_side, 1, "dp"), *(swap(own_side[r], r) for r in down[-1:])]
    [own_grad, mine, theirs] = attend_back(near[:1], (near_part,), last=True)
    near_grads = own_grad + swap(side_grad, 1) + far_grads
    half = D // 2
    shares = call(
        lambda *refs: merge_kernel(dp // 2, *refs),
        [((dl, pack_width), BF)] * (dp // 2),
        near_grads[:half],
        swap(near_grads[half:], 1, "dp"),
        own_side[0],
        *came,
    )
    first, *others = shares
    theirs, first = lax.optimization_barrier((theirs, first))
    shares = [first, *others]
    mine = mine + swap(theirs, 1)
    sums = shares[:1]
    for bit in line_bits:
        half = len(shares) // 2
        arrived = [swap(x, bit, "dp") for x in shares[half:]]
        sums.append(arrived[0])
        shares = [shares[0], *(x + y for x, y in zip(shares[1:half], arrived[1:], strict=True))]
    arrived = sums[-1]
    masters = (
        (projector, projector_mean, projector_square),
        (combiner.T, combiner_mean.T, combiner_square.T),
        (expander, expander_mean, expander_square),
        (reducer.T, reducer_mean.T, reducer_square.T),
    )
    rates = (
        (D ** (-0.5), 0.0001),
        (max(1, D * 8 // SEQ) ** (-0.5), 0.0001),
        (D ** (-0.5), 0.0001),
        (FF ** (-0.5), 0.0001),
        (0.4, 0.0),
    )
    flat = [x for three in masters for x in three]
    *fresh, fresh_small, new_pack = call(
        lambda *refs: update_kernel(rates, len(sums), *refs),
        [(x.shape, F32) for x in (*flat, small)] + [((dl, bw + 2 * fl), BF)],
        *sums,
        *flat,
        small,
    )
    copies = [new_pack]
    for bit in line_bits[::-1]:
        copies += [swap(x, bit, "dp") for x in copies]
    copies += [swap(x, 1, "dp") for x in copies]
    own_out, _ = lax.optimization_barrier((own_out, shares[0]))
    pieces = {0: own_out}
    for bit in chip_bits:
        mine = mine + swap(mine, bit)
        for r in list(pieces):
            pieces[r ^ bit] = swap(pieces[r], bit)
    late = {r: lax.optimization_barrier((x, copies[2]))[0] if r else x for r, x in pieces.items()}
    for r, x in late.items():
        pieces[r], pieces[r ^ 1] = x, swap(x, 1)
    mine, _ = lax.optimization_barrier((mine, copies[2]))
    input_grad, layer_out = call(
        assemble_kernel,
        [((seq, D), F32), ((seq, D), BF)],
        info,
        mine,
        swap(mine, 1),
        *(pieces[r] for r in names),
        smem=1,
    )
    copies[-2], input_grad = lax.optimization_barrier((copies[-2], input_grad))
    projector_copy, combiner_copy, expander_copy, reducer_copy = call(
        finish_kernel,
        [((3, cl, D), BF), ((cl, D), BF), ((D, fl), BF), ((fl, D), BF)],
        order,
        *copies,
    )
    for i in (3, 4, 5, 9, 10, 11):
        fresh[i] = fresh[i].T
    return (
        layer_out,
        input_grad,
        *fresh,
        *fresh_small,
        jnp.swapaxes(projector_copy, 1, 2),
        combiner_copy,
        expander_copy,
        reducer_copy,
    )


def solution(mesh):
    rows = P("dp", None)
    by_weight = [P(None, "dp", "mp"), P("mp", "dp"), P("dp", "mp"), P("mp", "dp"), P(None, "dp")]
    threes = [spec for spec in by_weight for _ in range(3)]
    return jax.shard_map(
        body,
        mesh=mesh,
        in_specs=(rows, rows, P("dp"), *threes),
        out_specs=(
            rows,
            rows,
            *threes,
            P(None, None, "mp"),
            P("mp", None),
            P(None, "mp"),
            P("mp", None),
        ),
        check_vma=False,
    )
```

```python
import math

import jax
import jax.numpy as jnp
from jax import lax
from jax.experimental import pallas as pl
from jax.experimental.pallas import tpu as pltpu
from jax.sharding import PartitionSpec as P

D = 256
FF = 2048
HD = 32
SEQ = 1024
WROW = 32
STEP = 5
LANES = 128
LOG2E = 1.4426950408889634
INTERPRET = False
BF = jnp.bfloat16
F32 = jnp.float32


def dot(a, b):
    return jnp.dot(a, b, preferred_element_type=F32)


def dot_nt(a, b):
    return lax.dot_general(a, b, (((1,), (1,)), ((), ())), preferred_element_type=F32)


def flip(x):
    return x.T


def lane_of(shape):
    return lax.broadcasted_iota(jnp.int32, shape, 1)


def row_of(shape):
    return lax.broadcasted_iota(jnp.int32, shape, 0)


def place_rows(x, start, total):
    parts = []
    if start:
        parts.append(jnp.zeros((start, x.shape[1]), x.dtype))
    parts.append(x)
    if total - start - x.shape[0]:
        parts.append(jnp.zeros((total - start - x.shape[0], x.shape[1]), x.dtype))
    return jnp.concatenate(parts, axis=0) if len(parts) > 1 else x


def call(kernel, outs, *args, scratch=(), smem=0, flops=0):
    vm = pl.BlockSpec(memory_space=pltpu.VMEM)
    sm = pl.BlockSpec(memory_space=pltpu.SMEM)
    return pl.pallas_call(
        kernel,
        out_shape=[jax.ShapeDtypeStruct(s, d) for s, d in outs],
        in_specs=[sm] * smem + [vm] * (len(args) - smem),
        out_specs=[vm] * len(outs),
        scratch_shapes=[pltpu.VMEM(s, d) for s, d in scratch],
        cost_estimate=pl.CostEstimate(flops=flops, transcendentals=0, bytes_accessed=0)
        if flops
        else None,
        compiler_params=pltpu.CompilerParams(vmem_limit_bytes=24 * 2**20),
        interpret=INTERPRET,
    )(*args)


def pack_kernel(*refs):
    given, pack, held, arrived = refs[:5], refs[5], refs[6:11], refs[11]
    fetches = [
        pltpu.make_async_copy(source, target, arrived.at[i])
        for i, (source, target) in enumerate(zip(given, held, strict=True))
    ]
    for fetch in fetches:
        fetch.start()
    projector, combiner_t, expander, reducer_t, affines = held
    dl, fl = expander.shape
    cl = combiner_t.shape[1]
    for fetch in fetches:
        fetch.wait()
    gains = jnp.concatenate([affines[...], jnp.zeros((LANES - 4, dl), F32)], axis=0).T
    high = gains.astype(BF).astype(F32)
    rest = pltpu.roll(gains - high, 4, 1)
    tail = jnp.where(lane_of(high.shape) < 4, high, rest).astype(BF)
    low = [projector[i].astype(BF) for i in range(3)] + [combiner_t[...].astype(BF)]
    pack[:, : 4 * cl] = jnp.concatenate(low, axis=1)
    pack[:, 4 * cl : 4 * cl + fl] = expander[...].astype(BF)
    pack[:, 4 * cl + fl : 4 * cl + 2 * fl] = reducer_t[...].astype(BF)
    pack[:, 4 * cl + 2 * fl :] = tail


def prepare_kernel(shares, info, tokens, tokens_out, query_in, tokens_t, query_t, order, whole):
    seq, width = tokens.shape
    half = width // 2
    rows = seq // WROW
    shape = (max(rows, WROW), half)
    channel = lane_of(shape)
    exponent = (2 * (channel // 2)).astype(F32) / half
    angles = (row_of(shape) + 1).astype(F32) * jnp.exp(-math.log(10000.0) * exponent)
    table = jnp.where(channel % 2 == 0, jnp.sin(angles), jnp.cos(angles))
    for i in range(rows):
        lower = i * WROW
        spot = jnp.concatenate(
            [jnp.broadcast_to(table[i : i + 1], (WROW, half)), table[:WROW]], axis=1
        )
        part = tokens[lower : lower + WROW, :].astype(F32) + spot
        whole[lower : lower + WROW, :] = part.astype(BF)
    share = width // shares
    bits = shares.bit_length() - 1
    place = lane_of((width, width))
    slot = place // share
    source = jnp.zeros_like(slot)
    for k in range(bits):
        source = source + (((slot >> k) & 1) << (bits - 1 - k))
    source = (source ^ info[2]) * share + place % share
    order[...] = jnp.where(row_of((width, width)) == source, 1.0, 0.0).astype(BF)
    for source_ref, out, out_t in ((whole, query_in, query_t), (tokens, tokens_out, tokens_t)):
        moved = dot(source_ref[...], order[...]).astype(BF)
        out[...] = moved
        out_t[...] = flip(moved)


def stack(upper, lower):
    return jnp.concatenate([upper[...], lower[...]], axis=0)


def attend_kernel(blocks, chunk, info, tokens, query_in, *refs):
    ins, outs, scores = refs[: 2 * blocks], refs[2 * blocks : -1], refs[-1]
    seq = tokens.shape[0]
    length, offset = info[0], info[1]
    fold = HD**-0.5 * LOG2E
    whole = [stack(*ins[2 * b : 2 * b + 2]) for b in range(blocks)]
    bw = whole[0].shape[1]
    cl = bw // 4
    mid = 2 * cl
    from_query = dot(query_in[...], jnp.concatenate([x[:, :mid] for x in whole], axis=1))
    from_token = dot(tokens[...], jnp.concatenate([x[:, mid:] for x in whole], axis=1))
    dead = jnp.where(row_of((seq, 1)) < length, 0.0, 1.0)
    work = []
    for b in range(blocks):
        block = whole[b]
        z, z_t, q_t, context_t, inverse, raised = outs[6 * b : 6 * b + 6]
        rows = q_t.shape[1]
        left = from_query[:, b * mid : (b + 1) * mid]
        z[:, :mid] = jnp.where(lane_of((1, mid)) == 0, dead, left).astype(BF)
        z[:, mid:] = from_token[:, b * mid : (b + 1) * mid].astype(BF)
        own = query_in[pl.ds(pl.multiple_of(offset, 8), rows), :]
        q_all = flip(dot(own, block).astype(BF))
        q_t[...] = q_all[:cl]
        z_t[...] = flip(z[...])
        for h in range(cl // HD):
            lower = h * HD
            side = place_rows(q_all[lower : lower + HD], cl + lower, bw)
            side = jnp.where(row_of(side.shape) == 0, -1e30, side.astype(F32)).astype(BF)
            work.append((b, h, side))
    def score(i):
        b, h, side = work[i]
        z = outs[6 * b]
        peak = jnp.full((1, rows), -jnp.inf, F32)
        for c in range(0, seq, chunk):
            part = dot(z[c : c + chunk, :], side)
            scores[i, c : c + chunk, :] = part
            peak = jnp.maximum(peak, jnp.max(part, axis=0, keepdims=True))
        return peak

    def mix(i):
        b, h, side = work[i]
        z, z_t, q_t, context_t, inverse, raised = outs[6 * b : 6 * b + 6]
        lower = h * HD
        mixed = dot(z_t[2 * cl + lower : 2 * cl + lower + HD, :], raised[h])
        context_t[lower : lower + HD, :] = mixed * inverse[h : h + 1, :]

    peak = score(0)
    for i, (b, h, side) in enumerate(work):
        inverse, raised = outs[6 * b + 4 : 6 * b + 6]
        after = score(i + 1) if i + 1 < len(work) else None
        total = jnp.zeros((1, rows), F32)
        for c in range(0, seq, chunk):
            part = jnp.exp2((scores[i, c : c + chunk, :] - peak) * fold)
            total = total + jnp.sum(part, axis=0, keepdims=True)
            raised[h, c : c + chunk, :] = part.astype(BF)
        inverse[h : h + 1, :] = 1.0 / total
        peak = after
        if i:
            mix(i - 1)
    mix(len(work) - 1)


def norm(x):
    average = jnp.mean(x, axis=-1, keepdims=True)
    centred = x - average
    scale = lax.rsqrt(jnp.mean(centred * centred, axis=-1, keepdims=True) + 1e-05)
    return centred * scale, scale


def norm_back(grad, unit, scale, gains):
    inner = grad * gains
    mean_one = jnp.mean(inner, axis=-1, keepdims=True)
    mean_two = jnp.mean(inner * unit, axis=-1, keepdims=True)
    back = scale * (inner - mean_one - unit * mean_two)
    gain_grad = jnp.sum(grad * unit, axis=0, keepdims=True)
    bias_grad = jnp.sum(grad, axis=0, keepdims=True)
    return back, gain_grad, bias_grad


def feed_kernel(blocks, info, tokens, cotangent, *refs):
    order, contexts, pairs = refs[0], refs[1 : blocks + 1], refs[blocks + 1 : 5 * blocks + 1]
    attention_pairs, feed_pairs = pairs[: 2 * blocks], pairs[2 * blocks :]
    layer_out, grad_one, *grads = refs[5 * blocks + 1 : 7 * blocks + 3]
    slopes, hidden_all = refs[7 * blocks + 3 :]
    attention_blocks = [stack(*attention_pairs[2 * b : 2 * b + 2]) for b in range(blocks)]
    halves = [feed_pairs[2 * b : 2 * b + 2] for b in range(blocks)]
    rows, width = layer_out.shape
    length, offset = info[0], pl.multiple_of(info[1], 8)
    bw = attention_blocks[0].shape[1]
    cl = bw // 4
    fl = (feed_pairs[0].shape[1] - LANES) // 2
    half = width // 2
    first_blocks = [stack(up.at[:, :fl], low.at[:, :fl]) for up, low in halves]
    second_blocks = [stack(up.at[:, fl : 2 * fl], low.at[:, fl : 2 * fl]) for up, low in halves]
    own = tokens[pl.ds(offset, rows), :].astype(F32)
    context = flip(jnp.concatenate([ref[...].astype(BF) for ref in contexts], axis=0))
    combiner = jnp.concatenate([attention_blocks[b][:, 3 * cl :] for b in range(blocks)], axis=1)
    attention = dot_nt(context, combiner)
    tail = [x[:, 2 * fl :].astype(F32) for x in halves[0]]
    pieces = jnp.concatenate(tail, axis=0).T
    gain_one, bias_one, gain_two, bias_two = (
        pieces[i : i + 1] + pieces[i + 4 : i + 5] for i in range(4)
    )
    unit_one, scale_one = norm(own + attention)
    first = unit_one * gain_one + bias_one
    first_low = first.astype(BF)
    feed = jnp.zeros((rows, width), F32)
    after = dot(first_low, first_blocks[0])
    for b in range(blocks):
        pre = after
        if b + 1 < blocks:
            after = dot(first_low, first_blocks[b + 1])
        square = pre * pre
        half_pre = 0.5 * pre
        bend = jnp.tanh(pre * (0.7978845608 + 0.035677408 * square))
        hidden = (half_pre + half_pre * bend).astype(BF)
        steep = 0.7978845608 + 0.107032224 * square
        slopes[b] = (0.5 + 0.5 * bend) + half_pre * (1.0 - bend * bend) * steep
        hidden_all[b] = hidden
        feed = feed + dot_nt(hidden, second_blocks[b])
    unit_two, scale_two = norm(first + feed)
    layer_out[...] = dot_nt((unit_two * gain_two + bias_two).astype(BF), order[...]).astype(BF)
    live = (row_of((rows, width)) + offset) < length
    seed = jnp.where(live, dot(cotangent[pl.ds(offset, rows), :], order[...]), 0.0)
    grad_two, d_gain_two, d_bias_two = norm_back(seed, unit_two, scale_two, gain_two)
    grad_two_low = grad_two.astype(BF)
    grad_two_t = flip(grad_two_low)
    first_t = flip(first_low)
    grad_first = grad_two
    after = dot(grad_two_low, second_blocks[0])
    for b in range(blocks):
        grad_hidden = after
        if b + 1 < blocks:
            after = dot(grad_two_low, second_blocks[b + 1])
        grad_pre = (grad_hidden * slopes[b]).astype(BF)
        for side in range(2):
            part = slice(side * half, (side + 1) * half)
            out = grads[2 * b + side]
            out[:, :fl] = dot(first_t[part], grad_pre).astype(BF)
            out[:, fl : 2 * fl] = dot(grad_two_t[part], hidden_all[b]).astype(BF)
        grad_first = grad_first + dot_nt(grad_pre, first_blocks[b])
    back, d_gain_one, d_bias_one = norm_back(grad_first, unit_one, scale_one, gain_one)
    grad_one[...] = back
    stacked = jnp.concatenate(
        [d_gain_one, d_bias_one, d_gain_two, d_bias_two, jnp.zeros((LANES - 4, width), F32)], axis=0
    )
    columns = stacked.T.astype(BF)
    for b in range(blocks):
        grads[2 * b][:, 2 * fl :] = columns[:half]
        grads[2 * b + 1][:, 2 * fl :] = columns[half:]


def attend_back_kernel(blocks, chunk, first, last, info, query_in, tokens_t, query_t, grad_one, *refs):
    made = blocks + 4 + last
    order, ins = refs[0], refs[1 : 8 * blocks + 1]
    rest = refs[8 * blocks + 1 :]
    earlier = None if first else rest[0]
    seq, width = query_in.shape
    score_grads, total, moved = rest[-3:]
    outs = rest[len(rest) - made : -3]
    rows = grad_one.shape[0]
    offset = pl.multiple_of(info[1], 8)
    scaling = HD**-0.5
    grad_low = grad_one[...].astype(BF)
    bw = ins[2].shape[1]
    cl = bw // 4
    mid = 2 * cl
    heads = range(cl // HD)
    sources = jnp.concatenate([flip(query_in[pl.ds(offset, rows), :]), flip(grad_low)], axis=1)
    own_total = flip(grad_one[...]) if earlier is None else jnp.zeros((width, rows), F32)
    ready = []
    for b in range(blocks):
        upper, lower_half, z, _, _, context_ref, inverse, _ = ins[8 * b : 8 * b + 8]
        block = stack(upper, lower_half)
        grad_context_t = dot(grad_low, block).T[3 * cl :]
        scaled = [
            (grad_context_t[h * HD : (h + 1) * HD] * inverse[h : h + 1, :]).astype(BF)
            for h in heads
        ]
        deltas = [
            jnp.sum(
                scaled[h].astype(F32) * context_ref[h * HD : (h + 1) * HD, :], axis=0, keepdims=True
            )
            for h in heads
        ]
        ready.append((block, scaled, deltas))

    def slope(b):
        z, raised = ins[8 * b + 2], ins[8 * b + 7]
        _, scaled, deltas = ready[b]
        for h in heads:
            side = place_rows(scaled[h], mid + h * HD, bw)
            for c in range(0, seq, chunk):
                weights = raised[h, c : c + chunk, :].astype(F32)
                slopes = weights * (dot(z[c : c + chunk, :], side) - deltas[h])
                score_grads[b, h, c : c + chunk, :] = slopes.astype(BF)

    def close(b):
        z_t, q_t, context_ref, raised = (ins[8 * b + i] for i in (3, 4, 5, 7))
        block, scaled, _ = ready[b]
        keys = [dot_nt(q_t[h * HD : (h + 1) * HD, :], score_grads[b, h]) * scaling for h in heads]
        values = [dot_nt(scaled[h], raised[h]) for h in heads]
        query_grads = [
            dot(z_t[cl + h * HD : cl + (h + 1) * HD, :], score_grads[b, h]) * scaling for h in heads
        ]
        edge = jnp.zeros((cl, seq), BF)
        keys = jnp.concatenate([edge, *(x.astype(BF) for x in keys)], axis=0)
        values = jnp.concatenate([*(x.astype(BF) for x in values), edge], axis=0)
        of_query = dot_nt(query_t[...], keys)
        of_token = dot_nt(tokens_t[...], values)
        part = dot(block, jnp.concatenate([keys, values], axis=0))
        if b:
            part = part + total[...]
        elif earlier is not None:
            part = part + earlier[...]
        total[...] = part
        query_grad = place_rows(jnp.concatenate(query_grads, axis=0).astype(BF), 0, bw)
        context = place_rows(context_ref[...].astype(BF), 3 * cl, bw)
        weight_grad = dot_nt(sources, jnp.concatenate([query_grad, context], axis=1))
        outs[b][:, :mid] = (weight_grad[:, :mid] + of_query).astype(BF)
        outs[b][:, mid:] = (weight_grad[:, mid:] + of_token).astype(BF)
        return dot(block, query_grad)

    slope(0)
    for b in range(1, blocks):
        slope(b)
        own_total = own_total + close(b - 1)
    own_total = own_total + close(blocks - 1)
    own_lanes = pl.ds(pl.multiple_of(info[1], LANES), rows)
    total[:, own_lanes] = total[:, own_lanes] + own_total
    if not last:
        outs[-1][...] = total[...]
        return
    moved[...] = flip(dot(order[...], total[...].astype(BF)).astype(BF))
    half = seq // 2
    for out, core in zip(outs[-2:], (info[3], 1 - info[3]), strict=True):
        out[...] = moved[pl.ds(pl.multiple_of(core * half, 16), half), :]


def merge_kernel(shares, *refs):
    ins, outs = refs[:-shares], refs[-shares:]
    bw = ins[0].shape[1]
    rows = outs[0].shape[0]
    low, high = ([x[...].astype(F32) for x in group] for group in (ins[:2], ins[2:]))
    low, high = low[0] + low[1], sum(high[1:], high[0])
    for i, out in enumerate(outs):
        part = slice(i * rows, (i + 1) * rows)
        out[:, :bw] = low[part].astype(BF)
        out[:, bw:] = high[part].astype(BF)


def adamw(weight, moment_one, moment_two, grad, step_rate, decay_rate):
    mean_next = 0.5 * moment_one + 0.5 * grad
    square_next = 0.5 * moment_two + 0.5 * grad * grad
    correct = 1.0 - 0.5**STEP
    direction = mean_next / correct / (jnp.sqrt(square_next / correct) + 1e-08)
    weight_next = weight - step_rate * (direction + decay_rate * weight)
    return (weight_next, mean_next, square_next)


def update_kernel(rates, count, *refs):
    grad = sum((x[...].astype(F32) for x in refs[1:count]), refs[0][...].astype(F32))
    refs = refs[count:]
    ins, outs, pack = refs[:13], refs[13:26], refs[26]
    cl = ins[0].shape[2]
    fl = ins[6].shape[1]
    fresh = []
    for i in range(3):
        fresh.append(
            adamw(*(ins[k][i] for k in range(3)), grad[:, i * cl : (i + 1) * cl], *rates[0])
        )
        for k in range(3):
            outs[k][i] = fresh[-1][k]
    start = 3 * cl
    for j, size in ((1, cl), (2, fl), (3, fl)):
        fresh.append(
            adamw(*(ins[3 * j + k][...] for k in range(3)), grad[:, start : start + size], *rates[j])
        )
        for k in range(3):
            outs[3 * j + k][...] = fresh[-1][k]
        start += size
    small = grad[:, start:].T[:4]
    for k, value in enumerate(adamw(*(ins[12][k] for k in range(3)), small, *rates[4])):
        outs[12][k] = value
    whole = jnp.concatenate([new[0].astype(BF) for new in fresh], axis=1)
    pack[...] = whole


def assemble_kernel(info, mine, other, *refs):
    *pieces, input_grad, layer_out = refs
    half = mine.shape[0]
    for part, core in ((mine, info[3]), (other, 1 - info[3])):
        input_grad[pl.ds(pl.multiple_of(core * half, 8), half), :] = part[...].astype(F32)
    rows = pieces[0].shape[0]
    for r, piece in enumerate(pieces):
        layer_out[pl.ds(pl.multiple_of((info[4] ^ r) * rows, 16), rows), :] = piece[...]


def finish_kernel(order, *refs):
    *pieces, projector_t, combiner, expander, reducer = refs
    copies = jnp.concatenate([piece[...] for piece in pieces], axis=0)
    copies = dot(order[...], copies).astype(BF)
    cl = combiner.shape[0]
    fl = reducer.shape[0]
    for i in range(3):
        projector_t[i] = flip(copies[:, i * cl : (i + 1) * cl])
    combiner[...] = flip(copies[:, 3 * cl : 4 * cl])
    expander[...] = copies[:, 4 * cl : 4 * cl + fl]
    reducer[...] = flip(copies[:, 4 * cl + fl : 4 * cl + 2 * fl])


def body(
    tokens,
    cotangent,
    lengths,
    projector,
    projector_mean,
    projector_square,
    combiner,
    combiner_mean,
    combiner_square,
    expander,
    expander_mean,
    expander_square,
    reducer,
    reducer_mean,
    reducer_square,
    affines,
    affines_mean,
    affines_square,
):
    mp = lax.axis_size("mp")
    dp = lax.axis_size("dp")
    me = lax.axis_index("mp")
    seq = tokens.shape[0]
    if lengths.shape[0] != 1 or mp & (mp - 1):
        raise ValueError("unsupported mesh")
    rows = seq // mp
    dl = expander.shape[0]
    cl = projector.shape[2]
    fl = expander.shape[1]
    bw = 4 * cl
    heads = cl // HD
    chunk = 256
    spot = lax.axis_index("dp")
    me, spot = me.astype(jnp.int32), spot.astype(jnp.int32)
    info = jnp.stack([lengths[0], me * rows, spot, me & 1, me])

    def swap(x, bit, axis="mp"):
        return lax.ppermute(x, axis, [(i, i ^ bit) for i in range(lax.axis_size(axis))])

    pack_width = bw + 2 * fl + LANES
    shares = [projector, combiner.T, expander, reducer.T, affines]
    [pack] = pl.pallas_call(
        pack_kernel,
        out_shape=[jax.ShapeDtypeStruct((dl, pack_width), BF)],
        in_specs=[pl.BlockSpec(memory_space=pltpu.HBM)] * len(shares),
        out_specs=[pl.BlockSpec(memory_space=pltpu.VMEM)],
        scratch_shapes=[
            *(pltpu.VMEM(x.shape, x.dtype) for x in shares),
            pltpu.SemaphoreType.DMA((len(shares),)),
        ],
        interpret=INTERPRET,
    )(*(pltpu.with_memory_space_constraint(x, pltpu.HBM) for x in shares))
    names = list(range(mp))
    near, far = names[:2], names[2:]
    chip_bits = [1 << i for i in range(1, mp.bit_length() - 1)]
    down = chip_bits[::-1]
    line_bits = [1 << i for i in range(1, dp.bit_length() - 1)]
    tokens_in, query_in, tokens_t, query_t, order = call(
        lambda *refs: prepare_kernel(dp, *refs),
        [((seq, D), BF)] * 2 + [((D, seq), BF)] * 2 + [((D, D), BF)],
        info,
        tokens,
        scratch=[((seq, D), BF)],
        smem=1,
    )
    small = jnp.stack([affines, affines_mean, affines_square])
    line = [pack]
    for bit in line_bits[::-1]:
        line += [swap(x, bit, "dp") for x in line]
    line[-1], order, small = lax.optimization_barrier((line[-1], order, small))
    pack = jnp.concatenate(line, axis=0)

    def cross(part):
        halves = {0: part}
        for bit in chip_bits:
            for r in list(halves):
                halves[r ^ bit] = swap(halves[r], bit)
        return halves

    def pair(blocks, group):
        for r in group:
            blocks[r ^ 1] = [swap(x, 1) for x in blocks[r]]

    attention_half, feed_half = pack[:, :bw], pack[:, bw:]
    upper = cross(attention_half)
    attention_blocks = {r: [x, swap(x, 1, "dp")] for r, x in upper.items()}
    feed_upper = cross(feed_half)
    feed_other, attention_blocks[0][1], attention_blocks[2][0] = lax.optimization_barrier(
        (swap(feed_half, 1, "dp"), attention_blocks[0][1], attention_blocks[2][0])
    )
    feed_lower = cross(feed_other)
    feed_blocks = {r: [feed_upper[r], feed_lower[r]] for r in feed_upper}
    pair(attention_blocks, names[:1])
    pair(feed_blocks, names[:1])

    def attend(group):
        made = call(
            lambda *refs: attend_kernel(len(group), chunk, *refs),
            [
                ((seq, bw), BF),
                ((bw, seq), BF),
                ((cl, rows), BF),
                ((cl, rows), F32),
                ((heads, rows), F32),
                ((heads, seq, rows), BF),
            ]
            * len(group),
            info,
            tokens_in,
            query_in,
            *(x for r in group for x in attention_blocks[r]),
            scratch=[((len(group) * heads, seq, rows), F32)],
            smem=1,
            flops=4 * len(group) * (heads + 1) * seq * rows * D,
        )
        return {r: list(made[6 * i : 6 * i + 6]) for i, r in enumerate(group)}

    kept = attend(near)
    for r in far[::2]:
        attention_blocks[r][1], kept[0][3] = lax.optimization_barrier(
            (attention_blocks[r][1], kept[0][3])
        )
    pair(attention_blocks, far[::2])
    for r in far[::2]:
        feed_blocks[r], attention_blocks[r ^ 1] = lax.optimization_barrier(
            (feed_blocks[r], attention_blocks[r ^ 1])
        )
    pair(feed_blocks, far[::2])
    kept.update(attend(far))
    own_out, grad_one, *feed_grads = call(
        lambda *refs: feed_kernel(mp, *refs),
        [((rows, D), BF), ((rows, D), F32)]
        + [((D // 2, 2 * fl + LANES), BF)] * (2 * mp),
        info,
        tokens_in,
        cotangent,
        order,
        *(kept[r][3] for r in names),
        *(x for r in names for x in attention_blocks[r]),
        *(x for r in names for x in feed_blocks[r]),
        scratch=[((mp, rows, fl), F32), ((mp, rows, fl), BF)],
        smem=1,
        flops=12 * mp * rows * D * fl,
    )

    def attend_back(group, earlier=(), last=False):
        return call(
            lambda *refs: attend_back_kernel(len(group), chunk, not earlier, last, *refs),
            [((D, bw), BF)] * len(group)
            + ([((seq // 2, D), BF)] * 2 if last else [((D, seq), F32)]),
            info,
            query_in,
            tokens_t,
            query_t,
            grad_one,
            order,
            *(x for r in group for x in (*attention_blocks[r], *kept[r])),
            *earlier,
            scratch=[((len(group), heads, seq, rows), BF), ((D, seq), F32), ((seq, D), BF)],
            smem=1,
            flops=8 * len(group) * (heads + 1) * seq * rows * D,
        )

    def reduce_blocks(left, order):
        left = dict(left)
        for bit in order:
            for r in sorted({r & ~bit for r in left if r & bit}):
                came = swap(left.pop(r ^ bit), bit)
                left[r] = left[r] + came if r in left else came
        return left

    down = chip_bits[::-1]
    own_side, other_side = (dict(zip(names, feed_grads[i::2], strict=True)) for i in range(2))
    far_side = reduce_blocks({r: other_side[r] for r in far}, [1])
    far_side, grad_one = lax.optimization_barrier((far_side, grad_one))
    near_side = reduce_blocks({r: other_side[r] for r in near}, [1])
    own_side = reduce_blocks(own_side, [1])
    other_side = reduce_blocks({**far_side, **near_side}, down)[0]
    *far_grads, side_grad, near_part = attend_back([*far, near[1]])
    far_grads = reduce_blocks(zip(far, far_grads, strict=True), [1])
    far_grads, other_side, own_side, near_part = lax.optimization_barrier(
        (far_grads, other_side, own_side, near_part)
    )
    far_grads = reduce_blocks(far_grads, down)[0]
    own_side = reduce_blocks(own_side, down[:-1])
    came = [swap(other_side, 1, "dp"), *(swap(own_side[r], r) for r in down[-1:])]
    [own_grad, mine, theirs] = attend_back(near[:1], (near_part,), last=True)
    near_grads = own_grad + swap(side_grad, 1) + far_grads
    half = D // 2
    shares = call(
        lambda *refs: merge_kernel(dp // 2, *refs),
        [((dl, pack_width), BF)] * (dp // 2),
        near_grads[:half],
        swap(near_grads[half:], 1, "dp"),
        own_side[0],
        *came,
    )
    first, *others = shares
    theirs, first = lax.optimization_barrier((theirs, first))
    shares = [first, *others]
    mine = mine + swap(theirs, 1)
    sums = shares[:1]
    for bit in line_bits:
        half = len(shares) // 2
        arrived = [swap(x, bit, "dp") for x in shares[half:]]
        sums.append(arrived[0])
        shares = [shares[0], *(x + y for x, y in zip(shares[1:half], arrived[1:], strict=True))]
    arrived = sums[-1]
    masters = (
        (projector, projector_mean, projector_square),
        (combiner.T, combiner_mean.T, combiner_square.T),
        (expander, expander_mean, expander_square),
        (reducer.T, reducer_mean.T, reducer_square.T),
    )
    rates = (
        (D ** (-0.5), 0.0001),
        (max(1, D * 8 // SEQ) ** (-0.5), 0.0001),
        (D ** (-0.5), 0.0001),
        (FF ** (-0.5), 0.0001),
        (0.4, 0.0),
    )
    flat = [x for three in masters for x in three]
    *fresh, fresh_small, new_pack = call(
        lambda *refs: update_kernel(rates, len(sums), *refs),
        [(x.shape, F32) for x in (*flat, small)] + [((dl, bw + 2 * fl), BF)],
        *sums,
        *flat,
        small,
    )
    copies = [new_pack]
    for bit in line_bits[::-1]:
        copies += [swap(x, bit, "dp") for x in copies]
    copies += [swap(x, 1, "dp") for x in copies]
    copies[1], copies[len(copies) // 2] = lax.optimization_barrier((copies[1], copies[len(copies) // 2]))
    own_out, _ = lax.optimization_barrier((own_out, shares[0]))
    pieces = {0: own_out}
    for bit in chip_bits:
        mine = mine + swap(mine, bit)
        for r in list(pieces):
            pieces[r ^ bit] = swap(pieces[r], bit)
    late = {r: lax.optimization_barrier((x, copies[2]))[0] if r else x for r, x in pieces.items()}
    for r, x in late.items():
        pieces[r], pieces[r ^ 1] = x, swap(x, 1)
    mine, _ = lax.optimization_barrier((mine, copies[2]))
    input_grad, layer_out = call(
        assemble_kernel,
        [((seq, D), F32), ((seq, D), BF)],
        info,
        mine,
        swap(mine, 1),
        *(pieces[r] for r in names),
        smem=1,
    )
    copies[-2], input_grad = lax.optimization_barrier((copies[-2], input_grad))
    projector_copy, combiner_copy, expander_copy, reducer_copy = call(
        finish_kernel,
        [((3, cl, D), BF), ((cl, D), BF), ((D, fl), BF), ((fl, D), BF)],
        order,
        *copies,
    )
    for i in (3, 4, 5, 9, 10, 11):
        fresh[i] = fresh[i].T
    return (
        layer_out,
        input_grad,
        *fresh,
        *fresh_small,
        jnp.swapaxes(projector_copy, 1, 2),
        combiner_copy,
        expander_copy,
        reducer_copy,
    )


def solution(mesh):
    rows = P("dp", None)
    by_weight = [P(None, "dp", "mp"), P("mp", "dp"), P("dp", "mp"), P("mp", "dp"), P(None, "dp")]
    threes = [spec for spec in by_weight for _ in range(3)]
    return jax.shard_map(
        body,
        mesh=mesh,
        in_specs=(rows, rows, P("dp"), *threes),
        out_specs=(
            rows,
            rows,
            *threes,
            P(None, None, "mp"),
            P("mp", None),
            P(None, "mp"),
            P("mp", None),
        ),
        check_vma=False,
    )
```

```python
import math

import jax
import jax.numpy as jnp
from jax import lax
from jax.experimental import pallas as pl
from jax.experimental.pallas import tpu as pltpu
from jax.sharding import PartitionSpec as P

D = 256
FF = 2048
HD = 32
SEQ = 1024
WROW = 32
STEP = 5
LANES = 128
LOG2E = 1.4426950408889634
INTERPRET = False
BF = jnp.bfloat16
F32 = jnp.float32


def dot(a, b):
    return jnp.dot(a, b, preferred_element_type=F32)


def dot_nt(a, b):
    return lax.dot_general(a, b, (((1,), (1,)), ((), ())), preferred_element_type=F32)


def flip(x):
    return x.T


def lane_of(shape):
    return lax.broadcasted_iota(jnp.int32, shape, 1)


def row_of(shape):
    return lax.broadcasted_iota(jnp.int32, shape, 0)


def place_rows(x, start, total):
    parts = []
    if start:
        parts.append(jnp.zeros((start, x.shape[1]), x.dtype))
    parts.append(x)
    if total - start - x.shape[0]:
        parts.append(jnp.zeros((total - start - x.shape[0], x.shape[1]), x.dtype))
    return jnp.concatenate(parts, axis=0) if len(parts) > 1 else x


def call(kernel, outs, *args, scratch=(), smem=0, flops=0):
    vm = pl.BlockSpec(memory_space=pltpu.VMEM)
    sm = pl.BlockSpec(memory_space=pltpu.SMEM)
    return pl.pallas_call(
        kernel,
        out_shape=[jax.ShapeDtypeStruct(s, d) for s, d in outs],
        in_specs=[sm] * smem + [vm] * (len(args) - smem),
        out_specs=[vm] * len(outs),
        scratch_shapes=[pltpu.VMEM(s, d) for s, d in scratch],
        cost_estimate=pl.CostEstimate(flops=flops, transcendentals=0, bytes_accessed=0)
        if flops
        else None,
        compiler_params=pltpu.CompilerParams(vmem_limit_bytes=24 * 2**20),
        interpret=INTERPRET,
    )(*args)


def pack_kernel(*refs):
    given, pack, held, arrived = refs[:5], refs[5], refs[6:11], refs[11]
    fetches = [
        pltpu.make_async_copy(source, target, arrived.at[i])
        for i, (source, target) in enumerate(zip(given, held, strict=True))
    ]
    for fetch in fetches:
        fetch.start()
    projector, combiner_t, expander, reducer_t, affines = held
    dl, fl = expander.shape
    cl = combiner_t.shape[1]
    for fetch in fetches:
        fetch.wait()
    gains = jnp.concatenate([affines[...], jnp.zeros((LANES - 4, dl), F32)], axis=0).T
    high = gains.astype(BF).astype(F32)
    rest = pltpu.roll(gains - high, 4, 1)
    tail = jnp.where(lane_of(high.shape) < 4, high, rest).astype(BF)
    low = [projector[i].astype(BF) for i in range(3)] + [combiner_t[...].astype(BF)]
    pack[:, : 4 * cl] = jnp.concatenate(low, axis=1)
    pack[:, 4 * cl : 4 * cl + fl] = expander[...].astype(BF)
    pack[:, 4 * cl + fl : 4 * cl + 2 * fl] = reducer_t[...].astype(BF)
    pack[:, 4 * cl + 2 * fl :] = tail


def prepare_kernel(shares, info, tokens, tokens_out, query_in, tokens_t, query_t, order, whole):
    seq, width = tokens.shape
    half = width // 2
    rows = seq // WROW
    shape = (max(rows, WROW), half)
    channel = lane_of(shape)
    exponent = (2 * (channel // 2)).astype(F32) / half
    angles = (row_of(shape) + 1).astype(F32) * jnp.exp(-math.log(10000.0) * exponent)
    table = jnp.where(channel % 2 == 0, jnp.sin(angles), jnp.cos(angles))
    for i in range(rows):
        lower = i * WROW
        spot = jnp.concatenate(
            [jnp.broadcast_to(table[i : i + 1], (WROW, half)), table[:WROW]], axis=1
        )
        part = tokens[lower : lower + WROW, :].astype(F32) + spot
        whole[lower : lower + WROW, :] = part.astype(BF)
    share = width // shares
    bits = shares.bit_length() - 1
    place = lane_of((width, width))
    slot = place // share
    source = jnp.zeros_like(slot)
    for k in range(bits):
        source = source + (((slot >> k) & 1) << (bits - 1 - k))
    source = (source ^ info[2]) * share + place % share
    order[...] = jnp.where(row_of((width, width)) == source, 1.0, 0.0).astype(BF)
    for source_ref, out, out_t in ((whole, query_in, query_t), (tokens, tokens_out, tokens_t)):
        moved = dot(source_ref[...], order[...]).astype(BF)
        out[...] = moved
        out_t[...] = flip(moved)


def stack(upper, lower):
    return jnp.concatenate([upper[...], lower[...]], axis=0)


def attend_kernel(blocks, chunk, info, tokens, query_in, *refs):
    ins, outs, scores = refs[: 2 * blocks], refs[2 * blocks : -1], refs[-1]
    seq = tokens.shape[0]
    length, offset = info[0], info[1]
    fold = HD**-0.5 * LOG2E
    whole = [stack(*ins[2 * b : 2 * b + 2]) for b in range(blocks)]
    bw = whole[0].shape[1]
    cl = bw // 4
    mid = 2 * cl
    from_query = dot(query_in[...], jnp.concatenate([x[:, :mid] for x in whole], axis=1))
    from_token = dot(tokens[...], jnp.concatenate([x[:, mid:] for x in whole], axis=1))
    dead = jnp.where(row_of((seq, 1)) < length, 0.0, 1.0)
    work = []
    for b in range(blocks):
        block = whole[b]
        z, z_t, q_t, context_t, inverse, raised = outs[6 * b : 6 * b + 6]
        rows = q_t.shape[1]
        left = from_query[:, b * mid : (b + 1) * mid]
        z[:, :mid] = jnp.where(lane_of((1, mid)) == 0, dead, left).astype(BF)
        z[:, mid:] = from_token[:, b * mid : (b + 1) * mid].astype(BF)
        own = query_in[pl.ds(pl.multiple_of(offset, 8), rows), :]
        q_all = flip(dot(own, block).astype(BF))
        q_t[...] = q_all[:cl]
        z_t[...] = flip(z[...])
        for h in range(cl // HD):
            lower = h * HD
            side = place_rows(q_all[lower : lower + HD], cl + lower, bw)
            side = jnp.where(row_of(side.shape) == 0, -1e30, side.astype(F32)).astype(BF)
            work.append((b, h, side))
    def score(i):
        b, h, side = work[i]
        z = outs[6 * b]
        peak = jnp.full((1, rows), -jnp.inf, F32)
        for c in range(0, seq, chunk):
            part = dot(z[c : c + chunk, :], side)
            scores[i, c : c + chunk, :] = part
            peak = jnp.maximum(peak, jnp.max(part, axis=0, keepdims=True))
        return peak

    def mix(i):
        b, h, side = work[i]
        z, z_t, q_t, context_t, inverse, raised = outs[6 * b : 6 * b + 6]
        lower = h * HD
        mixed = dot(z_t[2 * cl + lower : 2 * cl + lower + HD, :], raised[h])
        context_t[lower : lower + HD, :] = mixed * inverse[h : h + 1, :]

    peak = score(0)
    for i, (b, h, side) in enumerate(work):
        inverse, raised = outs[6 * b + 4 : 6 * b + 6]
        after = score(i + 1) if i + 1 < len(work) else None
        total = jnp.zeros((1, rows), F32)
        for c in range(0, seq, chunk):
            part = jnp.exp2((scores[i, c : c + chunk, :] - peak) * fold)
            total = total + jnp.sum(part, axis=0, keepdims=True)
            raised[h, c : c + chunk, :] = part.astype(BF)
        inverse[h : h + 1, :] = 1.0 / total
        peak = after
        if i:
            mix(i - 1)
    mix(len(work) - 1)


def norm(x):
    average = jnp.mean(x, axis=-1, keepdims=True)
    centred = x - average
    scale = lax.rsqrt(jnp.mean(centred * centred, axis=-1, keepdims=True) + 1e-05)
    return centred * scale, scale


def norm_back(grad, unit, scale, gains):
    inner = grad * gains
    mean_one = jnp.mean(inner, axis=-1, keepdims=True)
    mean_two = jnp.mean(inner * unit, axis=-1, keepdims=True)
    back = scale * (inner - mean_one - unit * mean_two)
    gain_grad = jnp.sum(grad * unit, axis=0, keepdims=True)
    bias_grad = jnp.sum(grad, axis=0, keepdims=True)
    return back, gain_grad, bias_grad


def feed_kernel(blocks, info, tokens, cotangent, *refs):
    order, contexts, pairs = refs[0], refs[1 : blocks + 1], refs[blocks + 1 : 5 * blocks + 1]
    attention_pairs, feed_pairs = pairs[: 2 * blocks], pairs[2 * blocks :]
    layer_out, grad_one, *grads = refs[5 * blocks + 1 : 7 * blocks + 3]
    slopes, hidden_all = refs[7 * blocks + 3 :]
    attention_blocks = [stack(*attention_pairs[2 * b : 2 * b + 2]) for b in range(blocks)]
    halves = [feed_pairs[2 * b : 2 * b + 2] for b in range(blocks)]
    rows, width = layer_out.shape
    length, offset = info[0], pl.multiple_of(info[1], 8)
    bw = attention_blocks[0].shape[1]
    cl = bw // 4
    fl = (feed_pairs[0].shape[1] - LANES) // 2
    half = width // 2
    first_blocks = [stack(up.at[:, :fl], low.at[:, :fl]) for up, low in halves]
    second_blocks = [stack(up.at[:, fl : 2 * fl], low.at[:, fl : 2 * fl]) for up, low in halves]
    own = tokens[pl.ds(offset, rows), :].astype(F32)
    context = flip(jnp.concatenate([ref[...].astype(BF) for ref in contexts], axis=0))
    combiner = jnp.concatenate([attention_blocks[b][:, 3 * cl :] for b in range(blocks)], axis=1)
    attention = dot_nt(context, combiner)
    tail = [x[:, 2 * fl :].astype(F32) for x in halves[0]]
    pieces = jnp.concatenate(tail, axis=0).T
    gain_one, bias_one, gain_two, bias_two = (
        pieces[i : i + 1] + pieces[i + 4 : i + 5] for i in range(4)
    )
    unit_one, scale_one = norm(own + attention)
    first = unit_one * gain_one + bias_one
    first_low = first.astype(BF)
    feed = jnp.zeros((rows, width), F32)
    after = dot(first_low, first_blocks[0])
    for b in range(blocks):
        pre = after
        if b + 1 < blocks:
            after = dot(first_low, first_blocks[b + 1])
        square = pre * pre
        half_pre = 0.5 * pre
        bend = jnp.tanh(pre * (0.7978845608 + 0.035677408 * square))
        hidden = (half_pre + half_pre * bend).astype(BF)
        steep = 0.7978845608 + 0.107032224 * square
        slopes[b] = (0.5 + 0.5 * bend) + half_pre * (1.0 - bend * bend) * steep
        hidden_all[b] = hidden
        feed = feed + dot_nt(hidden, second_blocks[b])
    unit_two, scale_two = norm(first + feed)
    layer_out[...] = dot_nt((unit_two * gain_two + bias_two).astype(BF), order[...]).astype(BF)
    live = (row_of((rows, width)) + offset) < length
    seed = jnp.where(live, dot(cotangent[pl.ds(offset, rows), :], order[...]), 0.0)
    grad_two, d_gain_two, d_bias_two = norm_back(seed, unit_two, scale_two, gain_two)
    grad_two_low = grad_two.astype(BF)
    grad_two_t = flip(grad_two_low)
    first_t = flip(first_low)
    grad_first = grad_two
    after = dot(grad_two_low, second_blocks[0])
    for b in range(blocks):
        grad_hidden = after
        if b + 1 < blocks:
            after = dot(grad_two_low, second_blocks[b + 1])
        grad_pre = (grad_hidden * slopes[b]).astype(BF)
        for side in range(2):
            part = slice(side * half, (side + 1) * half)
            out = grads[2 * b + side]
            out[:, :fl] = dot(first_t[part], grad_pre).astype(BF)
            out[:, fl : 2 * fl] = dot(grad_two_t[part], hidden_all[b]).astype(BF)
        grad_first = grad_first + dot_nt(grad_pre, first_blocks[b])
    back, d_gain_one, d_bias_one = norm_back(grad_first, unit_one, scale_one, gain_one)
    grad_one[...] = back
    stacked = jnp.concatenate(
        [d_gain_one, d_bias_one, d_gain_two, d_bias_two, jnp.zeros((LANES - 4, width), F32)], axis=0
    )
    columns = stacked.T.astype(BF)
    for b in range(blocks):
        grads[2 * b][:, 2 * fl :] = columns[:half]
        grads[2 * b + 1][:, 2 * fl :] = columns[half:]


def attend_back_kernel(blocks, chunk, first, last, info, query_in, tokens_t, query_t, grad_one, *refs):
    made = blocks + 4 + last
    order, ins = refs[0], refs[1 : 8 * blocks + 1]
    rest = refs[8 * blocks + 1 :]
    earlier = None if first else rest[0]
    seq, width = query_in.shape
    score_grads, total, moved = rest[-3:]
    outs = rest[len(rest) - made : -3]
    rows = grad_one.shape[0]
    offset = pl.multiple_of(info[1], 8)
    scaling = HD**-0.5
    grad_low = grad_one[...].astype(BF)
    bw = ins[2].shape[1]
    cl = bw // 4
    mid = 2 * cl
    heads = range(cl // HD)
    sources = jnp.concatenate([flip(query_in[pl.ds(offset, rows), :]), flip(grad_low)], axis=1)
    own_total = flip(grad_one[...]) if earlier is None else jnp.zeros((width, rows), F32)
    ready = []
    for b in range(blocks):
        upper, lower_half, z, _, _, context_ref, inverse, _ = ins[8 * b : 8 * b + 8]
        block = stack(upper, lower_half)
        grad_context_t = dot(grad_low, block).T[3 * cl :]
        scaled = [
            (grad_context_t[h * HD : (h + 1) * HD] * inverse[h : h + 1, :]).astype(BF)
            for h in heads
        ]
        deltas = [
            jnp.sum(
                scaled[h].astype(F32) * context_ref[h * HD : (h + 1) * HD, :], axis=0, keepdims=True
            )
            for h in heads
        ]
        ready.append((block, scaled, deltas))

    def slope(b):
        z, raised = ins[8 * b + 2], ins[8 * b + 7]
        _, scaled, deltas = ready[b]
        for h in heads:
            side = place_rows(scaled[h], mid + h * HD, bw)
            for c in range(0, seq, chunk):
                weights = raised[h, c : c + chunk, :].astype(F32)
                slopes = weights * (dot(z[c : c + chunk, :], side) - deltas[h])
                score_grads[b, h, c : c + chunk, :] = slopes.astype(BF)

    def close(b):
        z_t, q_t, context_ref, raised = (ins[8 * b + i] for i in (3, 4, 5, 7))
        block, scaled, _ = ready[b]
        keys = [dot_nt(q_t[h * HD : (h + 1) * HD, :], score_grads[b, h]) * scaling for h in heads]
        values = [dot_nt(scaled[h], raised[h]) for h in heads]
        query_grads = [
            dot(z_t[cl + h * HD : cl + (h + 1) * HD, :], score_grads[b, h]) * scaling for h in heads
        ]
        edge = jnp.zeros((cl, seq), BF)
        keys = jnp.concatenate([edge, *(x.astype(BF) for x in keys)], axis=0)
        values = jnp.concatenate([*(x.astype(BF) for x in values), edge], axis=0)
        of_query = dot_nt(query_t[...], keys)
        of_token = dot_nt(tokens_t[...], values)
        part = dot(block, jnp.concatenate([keys, values], axis=0))
        if b:
            part = part + total[...]
        elif earlier is not None:
            part = part + earlier[...]
        total[...] = part
        query_grad = place_rows(jnp.concatenate(query_grads, axis=0).astype(BF), 0, bw)
        context = place_rows(context_ref[...].astype(BF), 3 * cl, bw)
        weight_grad = dot_nt(sources, jnp.concatenate([query_grad, context], axis=1))
        outs[b][:, :mid] = (weight_grad[:, :mid] + of_query).astype(BF)
        outs[b][:, mid:] = (weight_grad[:, mid:] + of_token).astype(BF)
        return dot(block, query_grad)

    slope(0)
    for b in range(1, blocks):
        slope(b)
        own_total = own_total + close(b - 1)
    own_total = own_total + close(blocks - 1)
    own_lanes = pl.ds(pl.multiple_of(info[1], LANES), rows)
    total[:, own_lanes] = total[:, own_lanes] + own_total
    if not last:
        outs[-1][...] = total[...]
        return
    moved[...] = flip(dot(order[...], total[...].astype(BF)).astype(BF))
    half = seq // 2
    for out, core in zip(outs[-2:], (info[3], 1 - info[3]), strict=True):
        out[...] = moved[pl.ds(pl.multiple_of(core * half, 16), half), :]


def merge_kernel(shares, *refs):
    ins, outs = refs[:-shares], refs[-shares:]
    bw = ins[0].shape[1]
    rows = outs[0].shape[0]
    low, high = ([x[...].astype(F32) for x in group] for group in (ins[:2], ins[2:]))
    low, high = low[0] + low[1], sum(high[1:], high[0])
    for i, out in enumerate(outs):
        part = slice(i * rows, (i + 1) * rows)
        out[:, :bw] = low[part].astype(BF)
        out[:, bw:] = high[part].astype(BF)


def adamw(weight, moment_one, moment_two, grad, step_rate, decay_rate):
    mean_next = 0.5 * moment_one + 0.5 * grad
    square_next = 0.5 * moment_two + 0.5 * grad * grad
    correct = 1.0 - 0.5**STEP
    direction = mean_next / correct / (jnp.sqrt(square_next / correct) + 1e-08)
    weight_next = weight - step_rate * (direction + decay_rate * weight)
    return (weight_next, mean_next, square_next)


def update_kernel(rates, count, *refs):
    grad = sum((x[...].astype(F32) for x in refs[1:count]), refs[0][...].astype(F32))
    refs = refs[count:]
    ins, outs, pack = refs[:13], refs[13:26], refs[26]
    cl = ins[0].shape[2]
    fl = ins[6].shape[1]
    fresh = []
    for i in range(3):
        fresh.append(
            adamw(*(ins[k][i] for k in range(3)), grad[:, i * cl : (i + 1) * cl], *rates[0])
        )
        for k in range(3):
            outs[k][i] = fresh[-1][k]
    start = 3 * cl
    for j, size in ((1, cl), (2, fl), (3, fl)):
        fresh.append(
            adamw(*(ins[3 * j + k][...] for k in range(3)), grad[:, start : start + size], *rates[j])
        )
        for k in range(3):
            outs[3 * j + k][...] = fresh[-1][k]
        start += size
    small = grad[:, start:].T[:4]
    for k, value in enumerate(adamw(*(ins[12][k] for k in range(3)), small, *rates[4])):
        outs[12][k] = value
    whole = jnp.concatenate([new[0].astype(BF) for new in fresh], axis=1)
    pack[...] = whole


def assemble_kernel(info, mine, other, *refs):
    *pieces, input_grad, layer_out = refs
    half = mine.shape[0]
    for part, core in ((mine, info[3]), (other, 1 - info[3])):
        input_grad[pl.ds(pl.multiple_of(core * half, 8), half), :] = part[...].astype(F32)
    rows = pieces[0].shape[0]
    for r, piece in enumerate(pieces):
        layer_out[pl.ds(pl.multiple_of((info[4] ^ r) * rows, 16), rows), :] = piece[...]


def finish_kernel(order, *refs):
    *pieces, projector_t, combiner, expander, reducer = refs
    copies = jnp.concatenate([piece[...] for piece in pieces], axis=0)
    copies = dot(order[...], copies).astype(BF)
    cl = combiner.shape[0]
    fl = reducer.shape[0]
    for i in range(3):
        projector_t[i] = flip(copies[:, i * cl : (i + 1) * cl])
    combiner[...] = flip(copies[:, 3 * cl : 4 * cl])
    expander[...] = copies[:, 4 * cl : 4 * cl + fl]
    reducer[...] = flip(copies[:, 4 * cl + fl : 4 * cl + 2 * fl])


def body(
    tokens,
    cotangent,
    lengths,
    projector,
    projector_mean,
    projector_square,
    combiner,
    combiner_mean,
    combiner_square,
    expander,
    expander_mean,
    expander_square,
    reducer,
    reducer_mean,
    reducer_square,
    affines,
    affines_mean,
    affines_square,
):
    mp = lax.axis_size("mp")
    dp = lax.axis_size("dp")
    me = lax.axis_index("mp")
    seq = tokens.shape[0]
    if lengths.shape[0] != 1 or mp & (mp - 1):
        raise ValueError("unsupported mesh")
    rows = seq // mp
    dl = expander.shape[0]
    cl = projector.shape[2]
    fl = expander.shape[1]
    bw = 4 * cl
    heads = cl // HD
    chunk = 256
    spot = lax.axis_index("dp")
    me, spot = me.astype(jnp.int32), spot.astype(jnp.int32)
    info = jnp.stack([lengths[0], me * rows, spot, me & 1, me])

    def swap(x, bit, axis="mp"):
        return lax.ppermute(x, axis, [(i, i ^ bit) for i in range(lax.axis_size(axis))])

    pack_width = bw + 2 * fl + LANES
    shares = [projector, combiner.T, expander, reducer.T, affines]
    [pack] = pl.pallas_call(
        pack_kernel,
        out_shape=[jax.ShapeDtypeStruct((dl, pack_width), BF)],
        in_specs=[pl.BlockSpec(memory_space=pltpu.HBM)] * len(shares),
        out_specs=[pl.BlockSpec(memory_space=pltpu.VMEM)],
        scratch_shapes=[
            *(pltpu.VMEM(x.shape, x.dtype) for x in shares),
            pltpu.SemaphoreType.DMA((len(shares),)),
        ],
        interpret=INTERPRET,
    )(*(pltpu.with_memory_space_constraint(x, pltpu.HBM) for x in shares))
    names = list(range(mp))
    near, far = names[:2], names[2:]
    chip_bits = [1 << i for i in range(1, mp.bit_length() - 1)]
    down = chip_bits[::-1]
    line_bits = [1 << i for i in range(1, dp.bit_length() - 1)]
    tokens_in, query_in, tokens_t, query_t, order = call(
        lambda *refs: prepare_kernel(dp, *refs),
        [((seq, D), BF)] * 2 + [((D, seq), BF)] * 2 + [((D, D), BF)],
        info,
        tokens,
        scratch=[((seq, D), BF)],
        smem=1,
    )
    small = jnp.stack([affines, affines_mean, affines_square])
    line = [pack]
    for bit in line_bits[::-1]:
        line += [swap(x, bit, "dp") for x in line]
    line[-1], order, small = lax.optimization_barrier((line[-1], order, small))
    pack = jnp.concatenate(line, axis=0)

    def cross(part):
        halves = {0: part}
        for bit in chip_bits:
            for r in list(halves):
                halves[r ^ bit] = swap(halves[r], bit)
        return halves

    def pair(blocks, group):
        for r in group:
            blocks[r ^ 1] = [swap(x, 1) for x in blocks[r]]

    attention_half, feed_half = pack[:, :bw], pack[:, bw:]
    upper = cross(attention_half)
    attention_blocks = {r: [x, swap(x, 1, "dp")] for r, x in upper.items()}
    feed_upper = cross(feed_half)
    feed_other, attention_blocks[0][1], attention_blocks[2][0] = lax.optimization_barrier(
        (swap(feed_half, 1, "dp"), attention_blocks[0][1], attention_blocks[2][0])
    )
    feed_lower = cross(feed_other)
    feed_blocks = {r: [feed_upper[r], feed_lower[r]] for r in feed_upper}
    pair(attention_blocks, names[:1])
    pair(feed_blocks, names[:1])

    def attend(group):
        made = call(
            lambda *refs: attend_kernel(len(group), chunk, *refs),
            [
                ((seq, bw), BF),
                ((bw, seq), BF),
                ((cl, rows), BF),
                ((cl, rows), F32),
                ((heads, rows), F32),
                ((heads, seq, rows), BF),
            ]
            * len(group),
            info,
            tokens_in,
            query_in,
            *(x for r in group for x in attention_blocks[r]),
            scratch=[((len(group) * heads, seq, rows), F32)],
            smem=1,
            flops=4 * len(group) * (heads + 1) * seq * rows * D,
        )
        return {r: list(made[6 * i : 6 * i + 6]) for i, r in enumerate(group)}

    kept = attend(near)
    for r in far[::2]:
        attention_blocks[r][1], kept[0][3] = lax.optimization_barrier(
            (attention_blocks[r][1], kept[0][3])
        )
    pair(attention_blocks, far[::2])
    for r in far[::2]:
        feed_blocks[r], attention_blocks[r ^ 1] = lax.optimization_barrier(
            (feed_blocks[r], attention_blocks[r ^ 1])
        )
    pair(feed_blocks, far[::2])
    kept.update(attend(far))
    own_out, grad_one, *feed_grads = call(
        lambda *refs: feed_kernel(mp, *refs),
        [((rows, D), BF), ((rows, D), F32)]
        + [((D // 2, 2 * fl + LANES), BF)] * (2 * mp),
        info,
        tokens_in,
        cotangent,
        order,
        *(kept[r][3] for r in names),
        *(x for r in names for x in attention_blocks[r]),
        *(x for r in names for x in feed_blocks[r]),
        scratch=[((mp, rows, fl), F32), ((mp, rows, fl), BF)],
        smem=1,
        flops=12 * mp * rows * D * fl,
    )

    def attend_back(group, earlier=(), last=False):
        return call(
            lambda *refs: attend_back_kernel(len(group), chunk, not earlier, last, *refs),
            [((D, bw), BF)] * len(group)
            + ([((seq // 2, D), BF)] * 2 if last else [((D, seq), F32)]),
            info,
            query_in,
            tokens_t,
            query_t,
            grad_one,
            order,
            *(x for r in group for x in (*attention_blocks[r], *kept[r])),
            *earlier,
            scratch=[((len(group), heads, seq, rows), BF), ((D, seq), F32), ((seq, D), BF)],
            smem=1,
            flops=8 * len(group) * (heads + 1) * seq * rows * D,
        )

    def reduce_blocks(left, order):
        left = dict(left)
        for bit in order:
            for r in sorted({r & ~bit for r in left if r & bit}):
                came = swap(left.pop(r ^ bit), bit)
                left[r] = left[r] + came if r in left else came
        return left

    down = chip_bits[::-1]
    own_side, other_side = (dict(zip(names, feed_grads[i::2], strict=True)) for i in range(2))
    far_side = reduce_blocks({r: other_side[r] for r in far}, [1])
    far_side, grad_one = lax.optimization_barrier((far_side, grad_one))
    near_side = reduce_blocks({r: other_side[r] for r in near}, [1])
    own_side = reduce_blocks(own_side, [1])
    other_side = reduce_blocks({**far_side, **near_side}, down)[0]
    *far_grads, side_grad, near_part = attend_back([*far, near[1]])
    far_grads = reduce_blocks(zip(far, far_grads, strict=True), [1])
    other_side, own_side, near_part = lax.optimization_barrier((other_side, own_side, near_part))
    far_grads = reduce_blocks(far_grads, down)[0]
    own_side = reduce_blocks(own_side, down[:-1])
    came = [swap(other_side, 1, "dp"), *(swap(own_side[r], r) for r in down[-1:])]
    [own_grad, mine, theirs] = attend_back(near[:1], (near_part,), last=True)
    near_grads = own_grad + swap(side_grad, 1) + far_grads
    half = D // 2
    shares = call(
        lambda *refs: merge_kernel(dp // 2, *refs),
        [((dl, pack_width), BF)] * (dp // 2),
        near_grads[:half],
        swap(near_grads[half:], 1, "dp"),
        own_side[0],
        *came,
    )
    first, *others = shares
    theirs, first = lax.optimization_barrier((theirs, first))
    shares = [first, *others]
    mine = mine + swap(theirs, 1)
    sums = shares[:1]
    for bit in line_bits:
        half = len(shares) // 2
        arrived = [swap(x, bit, "dp") for x in shares[half:]]
        sums.append(arrived[0])
        shares = [shares[0], *(x + y for x, y in zip(shares[1:half], arrived[1:], strict=True))]
    arrived = sums[-1]
    masters = (
        (projector, projector_mean, projector_square),
        (combiner.T, combiner_mean.T, combiner_square.T),
        (expander, expander_mean, expander_square),
        (reducer.T, reducer_mean.T, reducer_square.T),
    )
    rates = (
        (D ** (-0.5), 0.0001),
        (max(1, D * 8 // SEQ) ** (-0.5), 0.0001),
        (D ** (-0.5), 0.0001),
        (FF ** (-0.5), 0.0001),
        (0.4, 0.0),
    )
    flat = [x for three in masters for x in three]
    *fresh, fresh_small, new_pack = call(
        lambda *refs: update_kernel(rates, len(sums), *refs),
        [(x.shape, F32) for x in (*flat, small)] + [((dl, bw + 2 * fl), BF)],
        *sums,
        *flat,
        small,
    )
    copies = [new_pack]
    for bit in line_bits[::-1]:
        copies += [swap(x, bit, "dp") for x in copies]
    copies += [swap(x, 1, "dp") for x in copies]
    copies[1], copies[len(copies) // 2] = lax.optimization_barrier((copies[1], copies[len(copies) // 2]))
    own_out, _ = lax.optimization_barrier((own_out, shares[0]))
    pieces = {0: own_out}
    for bit in chip_bits:
        mine = mine + swap(mine, bit)
        for r in list(pieces):
            pieces[r ^ bit] = swap(pieces[r], bit)
    late = {r: lax.optimization_barrier((x, copies[2]))[0] if r else x for r, x in pieces.items()}
    for r, x in late.items():
        pieces[r], pieces[r ^ 1] = x, swap(x, 1)
    mine, _ = lax.optimization_barrier((mine, copies[2]))
    input_grad, layer_out = call(
        assemble_kernel,
        [((seq, D), F32), ((seq, D), BF)],
        info,
        mine,
        swap(mine, 1),
        *(pieces[r] for r in names),
        smem=1,
    )
    copies[-2], input_grad = lax.optimization_barrier((copies[-2], input_grad))
    projector_copy, combiner_copy, expander_copy, reducer_copy = call(
        finish_kernel,
        [((3, cl, D), BF), ((cl, D), BF), ((D, fl), BF), ((fl, D), BF)],
        order,
        *copies,
    )
    for i in (3, 4, 5, 9, 10, 11):
        fresh[i] = fresh[i].T
    return (
        layer_out,
        input_grad,
        *fresh,
        *fresh_small,
        jnp.swapaxes(projector_copy, 1, 2),
        combiner_copy,
        expander_copy,
        reducer_copy,
    )


def solution(mesh):
    rows = P("dp", None)
    by_weight = [P(None, "dp", "mp"), P("mp", "dp"), P("dp", "mp"), P("mp", "dp"), P(None, "dp")]
    threes = [spec for spec in by_weight for _ in range(3)]
    return jax.shard_map(
        body,
        mesh=mesh,
        in_specs=(rows, rows, P("dp"), *threes),
        out_specs=(
            rows,
            rows,
            *threes,
            P(None, None, "mp"),
            P("mp", None),
            P(None, "mp"),
            P("mp", None),
        ),
        check_vma=False,
    )
```
